32 devices in a mesh: dp: 8 (over y, x, core), tensor: 4 (over z).
Axes of the slice: x: 2, y: 2, z: 4, core: 2. Of those that a mesh axis runs over, the one named last changes fastest.
Arguments:
- block_input: bfloat16 [4096, 768], P('dp'), may hold values from -6 to 6
- attn_gain: bfloat16 [768], P('dp'), may hold values from 0.25 to 1.75
- query_weight: bfloat16 [768, 768], P('dp', 'tensor'), may hold values from -0.21875 to 0.21875
- key_weight: bfloat16 [768, 768], P('dp', 'tensor'), may hold values from -0.21875 to 0.21875
- value_weight: bfloat16 [768, 768], P('dp', 'tensor'), may hold values from -0.21875 to 0.21875
- output_weight: bfloat16 [768, 768], P('dp', 'tensor'), may hold values from -0.875 to 0.875
- bias_table: float32 [12, 32], P('tensor'), may hold values from -6 to 306
- ffn_gain: bfloat16 [768], P('dp'), may hold values from 0.25 to 1.75
- router_weight: bfloat16 [768, 8], P('dp'), may hold values from -0.4375 to 0.4375
- expert_in: bfloat16 [8, 768, 3072], P('dp', None, 'tensor'), may hold values from -0.21875 to 0.21875
- expert_out: bfloat16 [8, 3072, 768], P('dp', 'tensor'), may hold values from -0.21875 to 0.21875
- expert_ids: int32 [4096, 2], P('dp'), may hold values from 0 to 7, all different within a row; in each aligned block of 512 rows (0 to 511, 512 to 1023, ...) at most 152 rows name the same one
- out_cotangent: bfloat16 [4096, 768], P('dp'), may hold values from -6 to 6
Outputs:
- block_output: bfloat16 [4096, 768], P('dp', 'tensor')
- input_grad: float32 [4096, 768], P('dp', 'tensor')
- attn_gain_grad: float32 [768], P('dp')
- query_grad: float32 [768, 768], P('dp', 'tensor')
- key_grad: float32 [768, 768], P('dp', 'tensor')
- value_grad: float32 [768, 768], P('dp', 'tensor')
- output_grad: float32 [768, 768], P('dp', 'tensor')
- bias_grad: float32 [12, 32], P('tensor')
- ffn_gain_grad: float32 [768], P('dp')
- router_grad: float32 [768, 8], P('dp')
- expert_in_grad: float32 [8, 768, 3072], P('dp', None, 'tensor')
- expert_out_grad: float32 [8, 3072, 768], P('dp', 'tensor')
The draws below stay inside these ranges and needn't reach their ends.
Inputs may be any that keep to these rules, and one draw needn't show every extreme that they name: `expert_ids`: the two experts of a token differ; among the tokens of one dp index no expert is named more than 152 times.
All inputs are finite; a program needn't handle non-finite values.
Results may differ from the reference program's by a relative error of at most 0.018.
Values may be sent and summed in bfloat16 or wider, within the bound.
A program may use at most 320 MiB of HBM per device.

```python
import math
import jax
import jax.numpy as jnp
import numpy as np
from jax import lax

D = 768
HEADS = 12
HEAD_DIM = 64
FF = 3072
NB = 32
SEQ_LEN = 512
HD_ALL = 768
EXPERTS = 8
TOK_DEV = 512
TOKENS = 4096
CAP = 152
N_DP = 8


def draw_bias_table(key, part):
    baseline_key = jax.random.fold_in(key, 0)
    baseline = 1.5 * jax.random.truncated_normal(baseline_key, -4.0, 4.0, (HEADS, NB), jnp.float32)
    return baseline


def with_spikes(array, key, source, target, parts, factor):
    def block_of(position):
        return (jnp.arange(array.shape[position]) // (array.shape[position] // parts)).reshape((-1,) + (1,) * (array.ndim - 1 - position))

    one_side = jax.random.permutation(key, parts)[block_of(target)]
    second = (block_of(target) + parts // 2) % parts
    return jnp.where((block_of(source) == one_side) | (block_of(source) == second), factor * array, array)


def block_scale(stream_key, extent, cuts, least, high):
    loudness, own = 1.0, jax.random.fold_in(stream_key, 6)
    for dim, blocks in cuts:
        heights = jnp.exp(jax.random.uniform(jax.random.fold_in(own, dim), (blocks,), jnp.float32, least / len(cuts), high / len(cuts)))
        loudness = loudness * jnp.repeat(heights, extent[dim] // blocks).reshape([-1 if axis == dim else 1 for axis in range(len(extent))])
    return loudness


def shared_out(rng, own, number, rows, number_of, top, reach, lean):
    sequence = jax.random.permutation(rng, number_of)
    heavy_load, ordinary = load_shares(number_of, rows * top, reach, lean, True), load_shares(number_of, rows * top, reach, lean, False)
    places = jnp.arange(number_of)

    def named(lengths, offset_by):
        used = int((lengths > 0).sum())
        fixed = max(1, used // 4)
        passed = fixed + (places - fixed + offset_by * (used - fixed)) % max(1, number_of - fixed)
        return jnp.zeros((number_of,), jnp.int32).at[sequence[jnp.where(places < fixed, places, passed)]].set(jnp.asarray(lengths, jnp.int32))

    lengths = jnp.where(number % 4 == 0, named(heavy_load, number // 4), named(ordinary, number - number // 4 - 1))
    mixed = jax.random.permutation(jax.random.fold_in(own, 3), number_of)
    donor, taker = mixed[0:number_of // 2 * 2:2], mixed[1:number_of // 2 * 2:2]
    slack = jnp.minimum(lengths[donor] - 1, reach - lengths[taker]) // 2
    slack = jnp.where((donor == sequence[0]) | (taker == sequence[0]) | (lengths[taker] == 0), 0, jnp.maximum(slack, 0))
    passed = jax.random.randint(jax.random.fold_in(own, 4), (number_of // 2,), 0, 1 << 20) % (slack + 1)
    lengths = lengths.at[donor].add(-passed).at[taker].add(passed)
    items = jnp.searchsorted(jnp.cumsum(lengths), jnp.arange(rows * top), side="right").astype(jnp.int32)
    table = items.reshape(top, rows).T
    table = table[jax.random.permutation(jax.random.fold_in(own, 1), rows)]
    offset_by = jax.random.randint(jax.random.fold_in(own, 2), (rows, 1), 0, top)
    return jnp.take_along_axis(table, (jnp.arange(top)[None, :] + offset_by) % top, axis=1)


def load_shares(count, total, most, skew, full):
    loads = [(1 << 20) // math.isqrt(grade ** skew) + 1 for grade in range(1, count + 1)]
    largest = most if full else min(most, max(-(-total // count), total * loads[0] // sum(loads)))
    least = 1 if total - largest >= count - 1 else 0
    counts, spare = [largest] + [least] * (count - 1), total - largest - least * (count - 1)
    while spare > 0:
        candidates = [i for i in range(1, count) if counts[i] < largest] or [i for i in range(1, count) if counts[i] < most]
        pool, budget = sum([loads[i] for i in candidates]), spare
        for i in candidates:
            extra = min(most - counts[i], max(1, budget * loads[i] // pool), spare)
            counts[i] = counts[i] + extra
            spare = spare - extra
    return np.array(counts)


def noise(rng, dims, deviation, most, pieces=(), held_as=jnp.bfloat16):
    factor_of = block_scale(rng, dims, pieces, -0.22, 0.18) if pieces else 1.0
    values = jax.random.normal(rng, dims, jnp.float32) * deviation * factor_of
    return jnp.minimum(jnp.maximum(values, -most), most).astype(held_as)


def noise_with(key, extent, deviation, bound, cuts, heavy, held_as=jnp.bfloat16):
    array = deviation * jax.random.normal(key, extent, jnp.float32)
    if cuts:
        array = array * block_scale(key, extent, cuts, -0.22, 0.18)
    return jnp.clip(with_spikes(array, jax.random.fold_in(key, 3), *heavy), -bound, bound).astype(held_as)


def setup_inputs(seed: int = 0) -> dict:
    arg_keys = jax.random.split(jax.random.key(seed), 14)
    block_input = noise_with(arg_keys[0], (TOKENS, D), 1.0, 6.0, ((0, 8),), (0, 1, 8, 2.0))
    attn_gain = jnp.clip(1.0 + 0.15 * jax.random.normal(arg_keys[1], (D,), jnp.float32), 0.25, 1.75).astype(jnp.bfloat16)
    query_weight = noise(arg_keys[2], (D, HD_ALL), D ** -0.5, 0.21875, ((0, 8), (1, 4)))
    key_weight = noise(arg_keys[3], (D, HD_ALL), D ** -0.5, 0.21875, ((0, 8), (1, 4)))
    value_weight = noise(arg_keys[4], (D, HD_ALL), D ** -0.5, 0.21875, ((0, 8), (1, 4)))
    output_weight = noise(arg_keys[5], (D, HD_ALL), (HD_ALL // 16) ** -0.5, 0.875, ((0, 8), (1, 4)))
    bias_table = draw_bias_table(jax.random.fold_in(arg_keys[13], 71), 0)
    ffn_gain = jnp.clip(1.0 + 0.15 * jax.random.normal(arg_keys[7], (D,), jnp.float32), 0.25, 1.75).astype(jnp.bfloat16)
    router_weight = noise(arg_keys[8], (D, EXPERTS), (D // 4) ** -0.5, 0.4375, ((0, 8),))
    expert_in = noise(arg_keys[9], (EXPERTS, D, FF), D ** -0.5, 0.21875, ((0, 8), (2, 4)))
    expert_out = noise(arg_keys[10], (EXPERTS, FF, D), (FF // 4) ** -0.5, 0.21875, ((0, 8), (1, 4)))
    expert_ids_keys = jax.random.split(jax.random.fold_in(arg_keys[11], 1), TOKENS // TOK_DEV)
    expert_ids_turns = jax.random.permutation(jax.random.fold_in(arg_keys[11], 3), TOKENS // TOK_DEV)
    expert_ids = jax.vmap(lambda own, number: shared_out(jax.random.fold_in(arg_keys[11], 2), own, number, TOK_DEV, EXPERTS, 2, CAP, 2))(expert_ids_keys, expert_ids_turns).reshape((TOKENS, 2))
    out_cotangent = noise_with(arg_keys[12], (TOKENS, D), 1.0, 6.0, ((0, 8),), (0, 1, 8, 2.0))
    return dict(block_input=block_input, attn_gain=attn_gain, query_weight=query_weight, key_weight=key_weight, value_weight=value_weight, output_weight=output_weight, bias_table=bias_table, ffn_gain=ffn_gain, router_weight=router_weight, expert_in=expert_in, expert_out=expert_out, expert_ids=expert_ids, out_cotangent=out_cotangent)


EPSILON = 1e-06
MASKED = -1e+30

def bucket_matrix(length, bucket_count):
    exact_count = bucket_count // 2
    steps_ids = jnp.arange(length, dtype=jnp.int32)
    distant = jnp.full((length,), exact_count, jnp.int32)
    for level_index in range(1, bucket_count - exact_count):
        border = int(math.ceil(exact_count * 8.0 ** (level_index / (bucket_count - exact_count))))
        distant = distant + (steps_ids >= border).astype(jnp.int32)
    bucket_vec = jnp.where(steps_ids < exact_count, steps_ids, distant).astype(jnp.int32)
    row_ids = lax.broadcasted_iota(jnp.int32, (length, length), 0)
    col_ids = lax.broadcasted_iota(jnp.int32, (length, length), 1)
    distance = jnp.maximum(row_ids - col_ids, 0).astype(jnp.int32)
    return (bucket_vec, distance, row_ids >= col_ids)

def rms_scale(matrix):
    return lax.rsqrt(lax.optimization_barrier(jnp.mean(matrix * matrix, axis=-1, keepdims=True)) + EPSILON)

def norm_back(dnormed, row_values, row_scale, gain_row):
    inner_mean = lax.optimization_barrier(jnp.mean(gain_row * dnormed * row_values, axis=-1, keepdims=True))
    return row_scale * (gain_row * dnormed - row_values * row_scale * row_scale * inner_mean)

def bucket_sums(grads, bucket_vec, bucket_count):
    head_count = grads.shape[0]
    length = grads.shape[1]
    flipped = grads[:, :, ::-1]
    padded = jnp.pad(flipped, ((0, 0), (0, 0), (0, length)))
    skewed = padded.reshape(head_count, 2 * length * length)[:, :length * (2 * length - 1)]
    skewed = skewed.reshape(head_count, length, 2 * length - 1)
    diagonal = lax.optimization_barrier(jnp.sum(skewed, axis=1))[:, length - 1:]
    labels = jnp.arange(bucket_count, dtype=jnp.int32)
    onehot = (bucket_vec[:, None] == labels[None, :]).astype(jnp.float32)
    return jnp.dot(diagonal, onehot, precision=lax.Precision.HIGHEST, preferred_element_type=jnp.float32)

def attention_scores(queries, key_rows, bias_heads, causal):
    factor = queries.shape[-1] ** (-0.5)
    products = jnp.einsum('qhd,khd->hqk', queries.astype(jnp.float32), key_rows.astype(jnp.float32))
    return jnp.where(causal[None], products * factor + bias_heads, MASKED)

def attend_forward(queries, key_rows, value_rows, bias_heads, causal):
    scores = attention_scores(queries, key_rows, bias_heads, causal)
    row_max = lax.optimization_barrier(jnp.max(scores, axis=-1, keepdims=True))
    row_total = lax.optimization_barrier(jnp.sum(jnp.exp(scores - row_max), axis=-1, keepdims=True))
    log_total = row_max + jnp.log(row_total)
    weights_low = jnp.exp(scores - log_total).astype(jnp.bfloat16)
    context = jnp.einsum('hqk,khd->qhd', weights_low.astype(jnp.float32), value_rows.astype(jnp.float32))
    return (context.astype(jnp.bfloat16), log_total)

def attend_backward(queries, key_rows, value_rows, bias_heads, causal, log_total, dcontext, bucket_vec, bucket_count):
    factor = queries.shape[-1] ** (-0.5)
    scores = attention_scores(queries, key_rows, bias_heads, causal)
    weights = jnp.exp(scores - log_total)
    weights_low = weights.astype(jnp.bfloat16)
    dweights = jnp.einsum('qhd,khd->hqk', dcontext.astype(jnp.float32), value_rows.astype(jnp.float32))
    dvalues = jnp.einsum('hqk,qhd->khd', weights_low.astype(jnp.float32), dcontext.astype(jnp.float32))
    agreement = lax.optimization_barrier(jnp.sum(weights * dweights, axis=-1, keepdims=True))
    dscores = weights * (dweights - agreement)
    dbias = bucket_sums(dscores, bucket_vec, bucket_count)
    dscores_low = dscores.astype(jnp.bfloat16).astype(jnp.float32)
    dqueries = factor * jnp.einsum('hqk,khd->qhd', dscores_low, key_rows.astype(jnp.float32))
    dkeys = factor * jnp.einsum('hqk,qhd->khd', dscores_low, queries.astype(jnp.float32))
    return (dqueries.astype(jnp.bfloat16), dkeys.astype(jnp.bfloat16), dvalues.astype(jnp.bfloat16), dbias)

def expert_forward(rows_in, weight_in, weight_out):
    pre_act = jnp.dot(rows_in, weight_in, preferred_element_type=jnp.float32)
    active = jax.nn.gelu(pre_act).astype(jnp.bfloat16)
    return (pre_act, active, jnp.dot(active, weight_out, preferred_element_type=jnp.float32))

def expert_backward(rows_in, pre_act, active, drows_in, weight_in, weight_out):
    dactive = jnp.dot(drows_in, weight_out.T, preferred_element_type=jnp.float32)
    unused_value, pullback = jax.vjp(jax.nn.gelu, pre_act)
    dpre_low = pullback(dactive)[0].astype(jnp.bfloat16)
    grad_out = jnp.dot(active.T, drows_in, preferred_element_type=jnp.float32)
    grad_in = jnp.dot(rows_in.T, dpre_low, preferred_element_type=jnp.float32)
    owner_back = jnp.dot(dpre_low, weight_in.T, preferred_element_type=jnp.float32)
    return (grad_in, grad_out, owner_back)

def reference(block_input, attn_gain, query_weight, key_weight, value_weight, output_weight, bias_table, ffn_gain, router_weight, expert_in, expert_out, expert_ids, out_cotangent):
    inputs_f = block_input.astype(jnp.float32)
    scale_one = rms_scale(inputs_f)
    gain_one = attn_gain.astype(jnp.float32)
    normed_one = (inputs_f * scale_one * gain_one).astype(jnp.bfloat16)
    queries = jnp.dot(normed_one, query_weight, preferred_element_type=jnp.float32).astype(jnp.bfloat16)
    key_rows = jnp.dot(normed_one, key_weight, preferred_element_type=jnp.float32).astype(jnp.bfloat16)
    value_rows = jnp.dot(normed_one, value_weight, preferred_element_type=jnp.float32).astype(jnp.bfloat16)
    bucket_vec, distance, causal = bucket_matrix(SEQ_LEN, NB)
    bias_heads = jnp.take(jnp.take(bias_table, bucket_vec, axis=1), distance, axis=1)
    seq_count = TOKENS // SEQ_LEN

    def split_heads(matrix):
        return matrix.reshape(seq_count, SEQ_LEN, HEADS, HEAD_DIM)

    def forward_one(triple):
        return attend_forward(triple[0], triple[1], triple[2], bias_heads, causal)
    context, log_total = lax.map(forward_one, (split_heads(queries), split_heads(key_rows), split_heads(value_rows)))
    context_flat = context.reshape(TOKENS, HD_ALL)
    attn_out = jnp.dot(context_flat, output_weight.T, preferred_element_type=jnp.float32)
    residual = inputs_f + attn_out
    scale_two = rms_scale(residual)
    gain_two = ffn_gain.astype(jnp.float32)
    normed_two = (residual * scale_two * gain_two).astype(jnp.bfloat16)
    logits = jnp.dot(normed_two, router_weight, preferred_element_type=jnp.float32)
    labels = jnp.arange(EXPERTS, dtype=jnp.int32)
    picked = (expert_ids[:, :, None] == labels[None, None, :]).astype(jnp.float32)
    chosen = lax.optimization_barrier(jnp.sum(picked * logits[:, None, :], axis=2))
    first_gate = jax.nn.sigmoid(chosen[:, 0] - chosen[:, 1])
    gate_pair = jnp.stack([first_gate, 1.0 - first_gate], axis=1)
    block_ids = expert_ids.reshape(N_DP, TOK_DEV * 2)
    ids_onehot = (block_ids[:, :, None] == labels[None, None, :]).astype(jnp.int32)
    earlier = jnp.cumsum(ids_onehot, axis=1) - ids_onehot
    slot_index = lax.optimization_barrier(jnp.sum(earlier * ids_onehot, axis=2))
    sources = lax.broadcasted_iota(jnp.int32, (N_DP, TOK_DEV * 2), 0)
    places = (sources * CAP + slot_index).reshape(-1).astype(jnp.int32)
    flat_ids = expert_ids.reshape(-1).astype(jnp.int32)

    def place_rows(token_rows):
        return jnp.zeros((EXPERTS, N_DP * CAP, D), jnp.bfloat16).at[flat_ids, places].set(token_rows)
    expert_rows = place_rows(jnp.repeat(normed_two, 2, axis=0))
    cot_f = out_cotangent.astype(jnp.float32)
    cot_rows = (gate_pair[:, :, None] * cot_f[:, None, :]).astype(jnp.bfloat16).reshape(TOKENS * 2, D)
    expert_drows = place_rows(cot_rows)

    def one_expert(member_set):
        rows_in, drows_in, weight_in, weight_out = member_set
        pre_act, active, owner_out = expert_forward(rows_in, weight_in, weight_out)
        grad_in, grad_out, owner_back = expert_backward(rows_in, pre_act, active, drows_in, weight_in, weight_out)
        return (owner_out.astype(jnp.bfloat16), owner_back.astype(jnp.bfloat16), grad_in, grad_out)
    results, row_grads, expert_in_grad, expert_out_grad = lax.map(one_expert, (expert_rows, expert_drows, expert_in, expert_out))
    result_rows = results[flat_ids, places].reshape(TOKENS, 2, D).astype(jnp.float32)
    mixture = lax.optimization_barrier(jnp.sum(gate_pair[:, :, None] * result_rows, axis=1))
    block_output = (residual + mixture).astype(jnp.bfloat16)
    gate_grads = lax.optimization_barrier(jnp.sum(cot_f[:, None, :] * result_rows, axis=2))
    dlogit = (gate_grads[:, 0] - gate_grads[:, 1]) * first_gate * (1.0 - first_gate)
    signed = jnp.stack([dlogit, -dlogit], axis=1)
    dlogits = lax.optimization_barrier(jnp.sum(picked * signed[:, :, None], axis=1)).astype(jnp.bfloat16)
    router_grad = jnp.dot(normed_two.T, dlogits, preferred_element_type=jnp.float32)
    back_rows = row_grads[flat_ids, places].reshape(TOKENS, 2, D).astype(jnp.float32)
    dnormed_two = lax.optimization_barrier(jnp.sum(back_rows, axis=1)) + jnp.dot(dlogits, router_weight.T, preferred_element_type=jnp.float32)
    ffn_gain_grad = lax.optimization_barrier(jnp.sum(dnormed_two * residual * scale_two, axis=0))
    dresidual = cot_f + norm_back(dnormed_two, residual, scale_two, gain_two)
    dres_low = dresidual.astype(jnp.bfloat16)
    output_grad = jnp.dot(dres_low.T, context_flat, preferred_element_type=jnp.float32)
    dcontext = jnp.dot(dres_low, output_weight, preferred_element_type=jnp.float32).astype(jnp.bfloat16)

    def backward_one(member_set):
        return attend_backward(member_set[0], member_set[1], member_set[2], bias_heads, causal, member_set[3], member_set[4], bucket_vec, NB)
    dqueries, dkeys, dvalues, dbias = lax.map(backward_one, (split_heads(queries), split_heads(key_rows), split_heads(value_rows), log_total, split_heads(dcontext)))
    bias_grad = lax.optimization_barrier(jnp.sum(dbias, axis=0))
    dq_flat = dqueries.reshape(TOKENS, HD_ALL)
    dk_flat = dkeys.reshape(TOKENS, HD_ALL)
    dv_flat = dvalues.reshape(TOKENS, HD_ALL)
    query_grad = jnp.dot(normed_one.T, dq_flat, preferred_element_type=jnp.float32)
    key_grad = jnp.dot(normed_one.T, dk_flat, preferred_element_type=jnp.float32)
    value_grad = jnp.dot(normed_one.T, dv_flat, preferred_element_type=jnp.float32)
    dnormed_one = jnp.dot(dq_flat, query_weight.T, preferred_element_type=jnp.float32)
    dnormed_one = dnormed_one + jnp.dot(dk_flat, key_weight.T, preferred_element_type=jnp.float32)
    dnormed_one = dnormed_one + jnp.dot(dv_flat, value_weight.T, preferred_element_type=jnp.float32)
    attn_gain_grad = lax.optimization_barrier(jnp.sum(dnormed_one * inputs_f * scale_one, axis=0))
    input_grad = dresidual + norm_back(dnormed_one, inputs_f, scale_one, gain_one)
    return (block_output, input_grad, attn_gain_grad, query_grad, key_grad, value_grad, output_grad, bias_grad, ffn_gain_grad, router_grad, expert_in_grad, expert_out_grad)
```

```python
import functools
import math

import jax
import jax.numpy as jnp
from jax import lax
from jax.experimental import pallas as pl
from jax.experimental.pallas import tpu as pltpu
from jax.sharding import PartitionSpec as P

HEAD_DIM = 64
NB = 32
SEQ_LEN = 512
LANES = 128


EPSILON = 1e-06
MASKED = -1e30


def bucket_vector_at(steps_ids, bucket_count):
    exact_count = bucket_count // 2
    distant = jnp.full(steps_ids.shape, exact_count, jnp.int32)
    for level_index in range(1, bucket_count - exact_count):
        border = int(math.ceil(exact_count * 8.0 ** (level_index / (bucket_count - exact_count))))
        distant = distant + (steps_ids >= border).astype(jnp.int32)
    return jnp.where(steps_ids < exact_count, steps_ids, distant)


def norm_back(dnormed, row_values, row_scale, gain_row):
    inner_mean = jnp.mean(gain_row * dnormed * row_values, axis=-1, keepdims=True)
    return row_scale * (gain_row * dnormed - row_values * row_scale * row_scale * inner_mean)


def rms_scale(matrix):
    return lax.rsqrt(jnp.mean(matrix * matrix, axis=-1, keepdims=True) + EPSILON)


def dot(left, right, dims=((1,), (0,))):
    return lax.dot_general(left, right, (dims, ((), ())), preferred_element_type=jnp.float32)


def forward_kernel(qkv_ref, wrapped_ref, context_ref, probs_ref):
    length = qkv_ref.shape[0]
    heads = probs_ref.shape[0]
    width = heads * HEAD_DIM
    factor = HEAD_DIM ** (-0.5)
    rows = lax.broadcasted_iota(jnp.int32, (length, length), 0)
    cols = lax.broadcasted_iota(jnp.int32, (length, length), 1)
    causal = rows >= cols
    for h in range(heads):
        lo, hi = h * HEAD_DIM, (h + 1) * HEAD_DIM
        queries = qkv_ref[:, lo:hi]
        keys = qkv_ref[:, width + lo : width + hi]
        values = qkv_ref[:, 2 * width + lo : 2 * width + hi]
        bias = jnp.broadcast_to(wrapped_ref[h : h + 1, :], (length, length))
        bias = pltpu.roll(bias, 0, 1, stride=1, stride_axis=0)
        scores = jnp.where(causal, dot(queries, keys, ((1,), (1,))) * factor + bias, MASKED)
        row_max = jnp.max(scores, axis=-1, keepdims=True)
        row_total = jnp.sum(jnp.exp(scores - row_max), axis=-1, keepdims=True)
        probs = jnp.exp(scores - (row_max + jnp.log(row_total))).astype(jnp.bfloat16)
        probs_ref[h] = probs
        context_ref[:, lo:hi] = dot(probs, values).astype(jnp.bfloat16)


def backward_kernel(qkv_ref, probs_ref, dcontext_ref, dqkv_ref, diagonal_ref):
    length = qkv_ref.shape[0]
    heads = probs_ref.shape[0]
    width = heads * HEAD_DIM
    factor = HEAD_DIM ** (-0.5)
    rows = lax.broadcasted_iota(jnp.int32, (length, length), 0)
    cols = lax.broadcasted_iota(jnp.int32, (length, length), 1)
    flip = (rows + cols == length - 1).astype(jnp.float32).astype(jnp.bfloat16)
    for h in range(heads):
        lo, hi = h * HEAD_DIM, (h + 1) * HEAD_DIM
        queries = qkv_ref[:, lo:hi]
        keys = qkv_ref[:, width + lo : width + hi]
        values = qkv_ref[:, 2 * width + lo : 2 * width + hi]
        dcontext = dcontext_ref[:, lo:hi]
        probs = probs_ref[h]
        weights = probs.astype(jnp.float32)
        dweights = dot(dcontext, values, ((1,), (1,)))
        agreement = jnp.sum(weights * dweights, axis=-1, keepdims=True)
        dscores = (weights * (dweights - agreement)).astype(jnp.bfloat16)
        dqkv_ref[:, lo:hi] = (factor * dot(dscores, keys)).astype(jnp.bfloat16)
        dqkv_ref[:, width + lo : width + hi] = (
            factor * dot(dscores, queries, ((0,), (0,)))
        ).astype(jnp.bfloat16)
        dqkv_ref[:, 2 * width + lo : 2 * width + hi] = dot(
            probs, dcontext, ((0,), (0,))
        ).astype(jnp.bfloat16)
        skewed = pltpu.roll(dot(flip, dscores), 0, 1, stride=1, stride_axis=0)
        diagonal_ref[h : h + 1, :] = jnp.sum(skewed, axis=0, keepdims=True)


def attend_forward(qkv, wrapped, seq_count, heads):
    width = heads * HEAD_DIM
    return pl.pallas_call(
        forward_kernel,
        grid=(seq_count,),
        out_shape=(
            jax.ShapeDtypeStruct((seq_count * SEQ_LEN, width), jnp.bfloat16),
            jax.ShapeDtypeStruct((seq_count, heads, SEQ_LEN, SEQ_LEN), jnp.bfloat16),
        ),
        in_specs=[
            pl.BlockSpec((SEQ_LEN, 3 * width), lambda s: (s, 0)),
            pl.BlockSpec((heads, SEQ_LEN), lambda s: (0, 0)),
        ],
        out_specs=(
            pl.BlockSpec((SEQ_LEN, width), lambda s: (s, 0)),
            pl.BlockSpec((None, heads, SEQ_LEN, SEQ_LEN), lambda s: (s, 0, 0, 0)),
        ),
        name="attend_forward",
    )(qkv, wrapped)


def attend_backward(qkv, probs, dcontext, seq_count, heads):
    width = heads * HEAD_DIM
    return pl.pallas_call(
        backward_kernel,
        grid=(seq_count,),
        out_shape=(
            jax.ShapeDtypeStruct((seq_count * SEQ_LEN, 3 * width), jnp.bfloat16),
            jax.ShapeDtypeStruct((seq_count, heads, SEQ_LEN), jnp.float32),
        ),
        in_specs=[
            pl.BlockSpec((SEQ_LEN, 3 * width), lambda s: (s, 0)),
            pl.BlockSpec((None, heads, SEQ_LEN, SEQ_LEN), lambda s: (s, 0, 0, 0)),
            pl.BlockSpec((SEQ_LEN, width), lambda s: (s, 0)),
        ],
        out_specs=(
            pl.BlockSpec((SEQ_LEN, 3 * width), lambda s: (s, 0)),
            pl.BlockSpec((None, heads, SEQ_LEN), lambda s: (s, 0, 0)),
        ),
        name="attend_backward",
    )(qkv, probs, dcontext)


def exchange(parcel):
    return lax.all_to_all(parcel, "dp", split_axis=0, concat_axis=0, tiled=True)


def in_mesh(axis, index):
    return {axis: index}


def remote(src, dst, send_sem, recv_sem, axis, index):
    return pltpu.make_async_remote_copy(
        src_ref=src,
        dst_ref=dst,
        send_sem=send_sem,
        recv_sem=recv_sem,
        device_id={axis: index},
        device_id_type=pl.DeviceIdType.MESH,
    )


def rows_at(index, count):
    return pl.ds(pl.multiple_of(index * count, count), count)


def bucket_of(distance):
    return bucket_vector_at(distance, NB)


def front_kernel(
    group_size,
    tensor_size,
    x_ref,
    q_ref,
    k_ref,
    v_ref,
    o_ref,
    small_ref,
    bias_ref,
    ids_ref,
    cot_ref,
    wqkv_ref,
    wo_ref,
    gains_ref,
    qkv_ref,
    probs_ref,
    context_ref,
    attn_ref,
    normed_ref,
    both_ref,
    signed_ref,
    rows_ref,
    cots_ref,
    small_buf,
    code_ref,
    part_ref,
    near_ref,
    middle_ref,
    send_ref,
    cot_send_ref,
    w_send,
    w_recv,
    cot_sems,
    row_sems,
    line_send,
    line_recv,
):
    me = lax.axis_index("dp")
    level = lax.axis_index("tensor")
    token_count, model_width = x_ref.shape
    expert_count = group_size
    capacity = rows_ref.shape[0] // group_size
    block_rows = q_ref.shape[0]
    head_width = q_ref.shape[1]
    heads = probs_ref.shape[0]
    low = jnp.bfloat16
    near = level + 1 - 2 * lax.rem(level, 2)
    across = tensor_size - 1 - level
    is_end = jnp.logical_or(level == 0, level == tensor_size - 1)

    mine = rows_at(me, block_rows)
    wqkv_ref[mine, :] = jnp.concatenate([q_ref[...], k_ref[...], v_ref[...]], axis=1)
    wo_ref[mine, :] = o_ref[...]
    small_buf[me] = small_ref[...]

    barrier = pltpu.get_barrier_semaphore()

    def greet(step, carry):
        peer = lax.rem(me + step, group_size)
        pl.semaphore_signal(
            barrier, inc=1, device_id={"dp": peer}, device_id_type=pl.DeviceIdType.MESH
        )
        return carry

    lax.fori_loop(1, group_size, greet, 0)
    for other in (near, across):
        pl.semaphore_signal(
            barrier, inc=1, device_id={"tensor": other}, device_id_type=pl.DeviceIdType.MESH
        )
    pl.semaphore_wait(barrier, group_size + 1)

    def weight_copies(peer, source):
        block = rows_at(source, block_rows)
        return [
            remote(wqkv_ref.at[block], wqkv_ref.at[block], w_send.at[0, peer], w_recv.at[0, source], "dp", peer),
            remote(wo_ref.at[block], wo_ref.at[block], w_send.at[1, peer], w_recv.at[1, source], "dp", peer),
            remote(small_buf.at[source], small_buf.at[source], w_send.at[2, peer], w_recv.at[2, source], "dp", peer),
        ]

    def send_weights(step, carry):
        for copy in weight_copies(lax.rem(me + step, group_size), me):
            copy.start()
        return carry

    lax.fori_loop(1, group_size, send_weights, 0)

    ids_first = ids_ref[0:1, :]
    ids_second = ids_ref[1:2, :]
    labels = lax.broadcasted_iota(jnp.int32, (expert_count, token_count), 0)
    member = jnp.logical_or(labels == ids_first, labels == ids_second)
    tokens_r = lax.broadcasted_iota(jnp.int32, (token_count, token_count), 0)
    tokens_c = lax.broadcasted_iota(jnp.int32, (token_count, token_count), 1)
    upper = jnp.where(tokens_r < tokens_c, 1.0, 0.0).astype(low)
    counted = dot(jnp.where(member, 1.0, 0.0).astype(low), upper)
    code_ref[...] = jnp.where(member, counted, -1.0)
    slots = lax.broadcasted_iota(jnp.int32, (capacity, token_count), 0).astype(jnp.float32)
    id_total = jnp.broadcast_to(
        (ids_first + ids_second).astype(jnp.float32), (LANES, token_count)
    ).astype(low)

    def make_maps(expert, carry):
        block = rows_at(expert, capacity)
        hit = slots == code_ref[pl.ds(expert, 1), :]
        sign = jnp.where(ids_first == expert, 1.0, -1.0)
        both = jnp.where(hit, 1.0, 0.0).astype(low)
        both_ref[block, :] = both
        signed_ref[block, :] = jnp.where(hit, sign, 0.0).astype(low)
        cot_send_ref[block, :model_width] = dot(both, cot_ref[...]).astype(low)
        cot_send_ref[block, model_width:] = dot(both, id_total, ((1,), (1,))).astype(low)
        return carry

    lax.fori_loop(0, expert_count, make_maps, 0)

    inputs_f = x_ref[...].astype(jnp.float32)
    scaled = inputs_f * rms_scale(inputs_f)

    def take_weights(step, carry):
        source = lax.rem(me + step, group_size)
        for copy in weight_copies(source, source):
            copy.wait_recv()
        return carry

    lax.fori_loop(1, group_size, take_weights, 0)

    def cot_copy(peer, source):
        return remote(
            cot_send_ref.at[rows_at(peer, capacity)],
            cots_ref.at[rows_at(source, capacity)],
            cot_sems.at[0, peer],
            cot_sems.at[1, source],
            "dp",
            peer,
        )

    def send_cots(step, carry):
        cot_copy(lax.rem(me + step, group_size), me).start()
        return carry

    lax.fori_loop(1, group_size, send_cots, 0)

    gains = small_buf[0].astype(jnp.float32)
    for source in range(1, group_size):
        gains = gains + small_buf[source].astype(jnp.float32)
    gains_ref[...] = gains
    gain_one = gains[0:1, :]
    gain_two = gains[1:2, :]
    normed_one = (scaled * gain_one).astype(low)
    qkv_ref[...] = dot(normed_one, wqkv_ref[...]).astype(low)

    lane = lax.broadcasted_iota(jnp.int32, (heads, token_count), 1)
    wrap_bucket = bucket_of(jnp.where(lane == 0, 0, token_count - lane))
    wrapped = jnp.zeros((heads, token_count), jnp.float32)
    for b in range(NB):
        wrapped = jnp.where(wrap_bucket == b, bias_ref[:, b : b + 1], wrapped)

    chunk = LANES
    chunks = token_count // chunk
    factor = HEAD_DIM ** (-0.5)

    def line_copies(c):
        block = slice(c * chunk, (c + 1) * chunk)
        up = remote(part_ref.at[block], near_ref.at[block], line_send.at[0, c], line_recv.at[0, c], "tensor", near)
        over = remote(part_ref.at[block], middle_ref.at[block], line_send.at[1, c], line_recv.at[1, c], "tensor", across)
        down = remote(attn_ref.at[block], attn_ref.at[block], line_send.at[2, c], line_recv.at[2, c], "tensor", near)
        return up, over, down

    def line_first(c):
        block = slice(c * chunk, (c + 1) * chunk)
        up, over, down = line_copies(c)

        @pl.when(jnp.logical_not(is_end))
        def _():
            up.wait_recv()
            part_ref[block, :] = (
                part_ref[block, :].astype(jnp.float32) + near_ref[block, :].astype(jnp.float32)
            ).astype(low)
            over.start()

    def line_second(c):
        block = slice(c * chunk, (c + 1) * chunk)
        up, over, down = line_copies(c)

        @pl.when(jnp.logical_not(is_end))
        def _():
            over.wait_recv()
            attn_ref[block, :] = (
                part_ref[block, :].astype(jnp.float32) + middle_ref[block, :].astype(jnp.float32)
            ).astype(low)
            down.start()

    for c in range(chunks):
        lo, hi = c * chunk, (c + 1) * chunk
        causal = lax.broadcasted_iota(jnp.int32, (chunk, hi), 0) + lo >= (
            lax.broadcasted_iota(jnp.int32, (chunk, hi), 1)
        )
        pieces = []
        for h in range(heads):
            at = h * HEAD_DIM
            queries = qkv_ref[lo:hi, at : at + HEAD_DIM]
            keys = qkv_ref[0:hi, head_width + at : head_width + at + HEAD_DIM]
            values = qkv_ref[0:hi, 2 * head_width + at : 2 * head_width + at + HEAD_DIM]
            bias = jnp.broadcast_to(wrapped[h : h + 1, :], (chunk, token_count))
            bias = pltpu.roll(bias, lo, 1, stride=1, stride_axis=0)[:, :hi]
            scores = jnp.where(causal, dot(queries, keys, ((1,), (1,))) * factor + bias, MASKED)
            row_max = jnp.max(scores, axis=-1, keepdims=True)
            grown = jnp.exp(scores - row_max)
            total = jnp.sum(grown, axis=-1, keepdims=True)
            probs = (grown * (1.0 / total)).astype(low)
            probs_ref[h, lo:hi, 0:hi] = probs
            if hi < token_count:
                probs_ref[h, lo:hi, hi:token_count] = jnp.zeros((chunk, token_count - hi), low)
            pieces.append(dot(probs, values).astype(low))
        context = jnp.concatenate(pieces, axis=1)
        context_ref[lo:hi, :] = context
        part_ref[lo:hi, :] = dot(context, wo_ref[...], ((1,), (1,))).astype(low)

        @pl.when(is_end)
        def _():
            line_copies(c)[0].start()

        if c >= 1:
            line_first(c - 1)
        if c >= 2:
            line_second(c - 2)
    line_first(chunks - 1)
    line_second(chunks - 2)
    line_second(chunks - 1)

    for c in range(chunks):
        block = slice(c * chunk, (c + 1) * chunk)

        @pl.when(is_end)
        def _():
            line_copies(c)[2].wait_recv()

        residual = x_ref[block, :].astype(jnp.float32) + attn_ref[block, :].astype(jnp.float32)
        normed_ref[block, :] = (residual * rms_scale(residual) * gain_two).astype(low)

    def row_copy(peer, source):
        return remote(
            send_ref.at[rows_at(peer, capacity)],
            rows_ref.at[rows_at(source, capacity)],
            row_sems.at[0, peer],
            row_sems.at[1, source],
            "dp",
            peer,
        )

    def send_rows(step, carry):
        peer = lax.rem(me + step, group_size)
        block = rows_at(peer, capacity)
        send_ref[block, :] = dot(both_ref[block, :], normed_ref[...]).astype(low)
        row_copy(peer, me).start()
        return carry

    lax.fori_loop(1, group_size, send_rows, 0)
    own = rows_at(me, capacity)
    rows_ref[own, :] = dot(both_ref[own, :], normed_ref[...]).astype(low)
    cots_ref[own, :] = cot_send_ref[own, :]

    def take(step, carry):
        source = lax.rem(me + step, group_size)
        cot_copy(source, source).wait_recv()
        row_copy(source, source).wait_recv()
        return carry

    lax.fori_loop(1, group_size, take, 0)

    def drain(step, carry):
        peer = lax.rem(me + step, group_size)
        for copy in weight_copies(peer, me):
            copy.wait_send()
        cot_copy(peer, me).wait_send()
        row_copy(peer, me).wait_send()
        return carry

    lax.fori_loop(1, group_size, drain, 0)
    for c in range(chunks):
        up, over, down = line_copies(c)

        @pl.when(is_end)
        def _():
            up.wait_send()

        @pl.when(jnp.logical_not(is_end))
        def _():
            over.wait_send()
            down.wait_send()


def front(group_size, tensor_size, capacity, x, q, k, v, o, small, bias, ids, cot):
    tokens, width = x.shape
    block_rows, head_width = q.shape
    heads = bias.shape[0]
    slots = group_size * capacity
    low = jnp.bfloat16
    full = group_size * block_rows
    chunks = tokens // LANES

    def shape(dims, dtype=low):
        return jax.ShapeDtypeStruct(dims, dtype)

    vmem = pl.BlockSpec(memory_space=pltpu.VMEM)
    return pl.pallas_call(
        functools.partial(front_kernel, group_size, tensor_size),
        out_shape=(
            shape((full, 3 * head_width)),
            shape((full, head_width)),
            shape(small.shape, jnp.float32),
            shape((tokens, 3 * head_width)),
            shape((heads, tokens, tokens)),
            shape((tokens, head_width)),
            shape((tokens, width)),
            shape((tokens, width)),
            shape((slots, tokens)),
            shape((slots, tokens)),
            shape((slots, width)),
            shape((slots, width + LANES)),
        ),
        in_specs=[vmem] * 9,
        out_specs=(vmem,) * 12,
        scratch_shapes=[
            pltpu.VMEM((group_size,) + small.shape, low),
            pltpu.VMEM((group_size, tokens), jnp.float32),
            pltpu.VMEM((tokens, width), low),
            pltpu.VMEM((tokens, width), low),
            pltpu.VMEM((tokens, width), low),
            pltpu.VMEM((slots, width), low),
            pltpu.VMEM((slots, width + LANES), low),
            pltpu.SemaphoreType.DMA((3, group_size)),
            pltpu.SemaphoreType.DMA((3, group_size)),
            pltpu.SemaphoreType.DMA((2, group_size)),
            pltpu.SemaphoreType.DMA((2, group_size)),
            pltpu.SemaphoreType.DMA((3, chunks)),
            pltpu.SemaphoreType.DMA((3, chunks)),
        ],
        compiler_params=pltpu.CompilerParams(
            collective_id=0, has_side_effects=True, vmem_limit_bytes=60 * 1024 * 1024
        ),
        name="front",
    )(x, q, k, v, o, small, bias, ids, cot)


def on_device_general(
    block_input,
    attn_gain,
    query_weight,
    key_weight,
    value_weight,
    output_weight,
    bias_table,
    ffn_gain,
    router_weight,
    expert_in,
    expert_out,
    expert_ids,
    out_cotangent,
):
    tensor_size = lax.axis_size("tensor")
    group_size = lax.axis_size("dp")
    tensor_index = lax.axis_index("tensor")
    own_expert = lax.axis_index("dp")
    token_count, model_width = block_input.shape
    column_width = model_width // tensor_size
    column_start = tensor_index * column_width
    expert_count = group_size * expert_in.shape[0]
    capacity = tensor_size * max(1, 3 * token_count // (5 * expert_count))
    slot_rows = expert_count * capacity
    seq_count = token_count // SEQ_LEN
    head_local = bias_table.shape[0]
    head_width = head_local * HEAD_DIM
    block_rows = query_weight.shape[0]
    low = jnp.bfloat16

    def own_columns(matrix):
        return lax.dynamic_slice_in_dim(matrix, column_start, column_width, 1)

    packed = jnp.concatenate(
        [
            query_weight,
            key_weight,
            value_weight,
            output_weight,
            router_weight,
            attn_gain[:, None],
            ffn_gain[:, None],
        ],
        axis=1,
    )
    packed = lax.all_gather(packed, "dp", axis=0, tiled=True)

    labels = jnp.arange(expert_count, dtype=jnp.int32)
    flat_ids = expert_ids.reshape(-1)
    ids_onehot = (flat_ids[:, None] == labels[None, :]).astype(jnp.int32)
    pair_rows = lax.broadcasted_iota(jnp.int32, (2 * token_count, 2 * token_count), 0)
    pair_cols = lax.broadcasted_iota(jnp.int32, (2 * token_count, 2 * token_count), 1)
    before = (pair_cols < pair_rows).astype(low)
    earlier = dot(before, ids_onehot.astype(low)).astype(jnp.int32)
    slot_index = jnp.sum(earlier * ids_onehot, axis=1)
    places = (flat_ids * capacity + slot_index).reshape(token_count, 2)
    place_rows = jnp.arange(slot_rows, dtype=jnp.int32)
    at_first = places[:, 0][None, :] == place_rows[:, None]
    at_second = places[:, 1][None, :] == place_rows[:, None]
    map_first = at_first.astype(low)
    map_second = at_second.astype(low)
    map_both = (at_first | at_second).astype(low)

    ids_low = jnp.broadcast_to(expert_ids.astype(low)[:, :, None], (token_count, 2, LANES))
    cot_source = jnp.concatenate(
        [
            jnp.concatenate([out_cotangent, ids_low[:, 1]], axis=1),
            jnp.concatenate([out_cotangent, ids_low[:, 0]], axis=1),
        ],
        axis=0,
    )
    cot_parcel = dot(jnp.concatenate([map_first, map_second], axis=1), cot_source).astype(low)
    packed, cot_parcel = lax.optimization_barrier((packed, cot_parcel))
    cot_arrived = exchange(
        cot_parcel.reshape(expert_count, capacity, model_width + LANES)
    ).reshape(slot_rows, model_width + LANES)
    cot_rows = cot_arrived[:, :model_width].astype(jnp.float32)
    other_ids = cot_arrived[:, model_width].astype(jnp.int32)

    qkv_full = packed[:, : 3 * head_width]
    output_full = packed[:, 3 * head_width : 4 * head_width]
    at = 4 * head_width
    router_full = packed[:, at : at + expert_count]
    gain_one = packed[:, at + expert_count].astype(jnp.float32)
    gain_two = packed[:, at + expert_count + 1].astype(jnp.float32)
    inputs_f = block_input.astype(jnp.float32)
    scale_one = rms_scale(inputs_f)
    normed_one = (inputs_f * scale_one * gain_one).astype(low)
    qkv = dot(normed_one, qkv_full).astype(low)
    bucket_vec = bucket_vector_at(jnp.arange(SEQ_LEN, dtype=jnp.int32), NB)
    bucket_labels = jnp.arange(NB, dtype=jnp.int32)
    wrap = (SEQ_LEN - jnp.arange(SEQ_LEN, dtype=jnp.int32)) % SEQ_LEN
    wrapped_onehot = bucket_vector_at(wrap, NB)[None, :] == bucket_labels[:, None]
    wrapped = jnp.sum(
        jnp.where(wrapped_onehot[None], bias_table[:, :, None], 0.0), axis=1
    )
    context, probs = attend_forward(qkv, wrapped, seq_count, head_local)
    attn_part = dot(context, output_full, ((1,), (1,))).astype(low)
    attn_out = lax.psum(attn_part, "tensor").astype(jnp.float32)
    residual = inputs_f + attn_out
    scale_two = rms_scale(residual)
    normed_two = (residual * scale_two * gain_two).astype(low)

    logits = dot(normed_two, router_full)
    picked = (expert_ids[:, :, None] == labels[None, None, :]).astype(jnp.float32)
    chosen = jnp.sum(picked * logits[:, None, :], axis=2)
    first_gate = jax.nn.sigmoid(chosen[:, 0] - chosen[:, 1])
    second_gate = 1.0 - first_gate

    weight_in = expert_in[0]
    weight_out = expert_out[0]
    parcel = dot(map_both, normed_two).astype(low)
    expert_rows = exchange(parcel.reshape(expert_count, capacity, model_width)).reshape(
        slot_rows, model_width
    )
    pre_act = dot(expert_rows, weight_in)
    active, pullback = jax.vjp(jax.nn.gelu, pre_act)
    active = active.astype(low)
    owner_out = dot(active, weight_out)
    owner_logits = dot(expert_rows, router_full)
    own_logit = jnp.sum(
        jnp.where(labels[None, :] == own_expert, owner_logits, 0.0), axis=1
    )
    other_logit = jnp.sum(
        jnp.where(labels[None, :] == other_ids[:, None], owner_logits, 0.0), axis=1
    )
    row_gate = jax.nn.sigmoid(own_logit - other_logit)
    expert_drows = (row_gate[:, None] * cot_rows).astype(low)
    dpre = pullback(dot(expert_drows, weight_out, ((1,), (1,))))[0].astype(low)
    owner_back = dot(dpre, weight_in, ((1,), (1,))).astype(low)
    gate_part = jnp.sum(cot_rows * owner_out, axis=1, keepdims=True).astype(low)
    back_parcel = jnp.concatenate(
        [owner_back, jnp.broadcast_to(gate_part, (slot_rows, LANES))], axis=1
    )
    back_rows = exchange(
        back_parcel.reshape(group_size, capacity, model_width + LANES)
    ).reshape(slot_rows, model_width + LANES)
    out_rows = exchange(
        owner_out.astype(low).reshape(group_size, capacity, model_width)
    ).reshape(slot_rows, model_width)
    out_grad = dot(active, expert_drows, ((0,), (0,)))
    in_grad = dot(expert_rows, dpre, ((0,), (0,)))

    dnormed_part = dot(map_both, back_rows[:, :model_width], ((0,), (0,)))
    gate_diff_part = dot(map_first - map_second, back_rows[:, model_width:], ((0,), (0,)))
    gate_rows = -(-token_count // model_width)
    gate_line = jnp.pad(gate_diff_part[:, 0], (0, gate_rows * model_width - token_count))
    summed = lax.psum(
        jnp.concatenate(
            [dnormed_part, gate_line.reshape(gate_rows, model_width)], axis=0
        ).astype(low),
        "tensor",
    ).astype(jnp.float32)
    gate_diff = summed[token_count:].reshape(-1)[:token_count]
    mixture_part = first_gate[:, None] * dot(map_first, out_rows, ((0,), (0,)))
    mixture_part = mixture_part + second_gate[:, None] * dot(
        map_second, out_rows, ((0,), (0,))
    )
    mixture_parts = mixture_part.astype(low).reshape(token_count, tensor_size, column_width)
    mixture_parts = jnp.swapaxes(mixture_parts, 0, 1)

    dlogit = gate_diff * first_gate * second_gate
    signed = jnp.stack([dlogit, -dlogit], axis=1)
    dlogits = jnp.sum(picked * signed[:, :, None], axis=1).astype(low)
    router_term = dot(normed_two, dlogits, ((0,), (0,)))
    dnormed_two = summed[:token_count] + dot(dlogits, router_full, ((1,), (1,)))
    ffn_term = jnp.sum(dnormed_two * residual * scale_two, axis=0)
    cot_f = out_cotangent.astype(jnp.float32)
    dresidual = cot_f + norm_back(dnormed_two, residual, scale_two, gain_two)
    dres_low = dresidual.astype(low)
    mixture_parts, dres_low = lax.optimization_barrier((mixture_parts, dres_low))
    mixture_parts = lax.all_to_all(
        mixture_parts, "tensor", split_axis=0, concat_axis=0, tiled=True
    )

    output_term = dot(dres_low, context, ((0,), (0,)))
    dcontext = dot(dres_low, output_full).astype(low)
    dqkv, diagonal = attend_backward(qkv, probs, dcontext, seq_count, head_local)
    reverse_onehot = (bucket_vec[::-1][:, None] == bucket_labels[None, :]).astype(jnp.float32)
    bias_term = jnp.dot(
        jnp.sum(diagonal, axis=0),
        reverse_onehot,
        precision=lax.Precision.HIGHEST,
        preferred_element_type=jnp.float32,
    )
    dnormed_part = dot(dqkv, qkv_full, ((1,), (1,))).astype(low)
    dnormed_part, mixture_parts = lax.optimization_barrier((dnormed_part, mixture_parts))
    dnormed_one = lax.psum(dnormed_part, "tensor").astype(jnp.float32)
    qkv_term = dot(normed_one, dqkv, ((0,), (0,)))
    bias_count = bias_term.size
    bias_cols = -(-bias_count // block_rows)
    bias_block = jnp.pad(bias_term.reshape(-1), (0, bias_cols * block_rows - bias_count))
    bias_block = jnp.tile(bias_block.reshape(block_rows, bias_cols), (group_size, 1))
    terms = jnp.concatenate(
        [qkv_term, output_term, router_term, ffn_term[:, None], bias_block],
        axis=1,
    ).astype(low)
    term_width = terms.shape[1]
    arrived = exchange(terms.reshape(group_size, block_rows, term_width))
    arrived, dnormed_one = lax.optimization_barrier((arrived, dnormed_one))
    mixture = jnp.sum(mixture_parts.astype(jnp.float32), axis=0)
    block_output = (own_columns(residual) + mixture).astype(low)
    reduced = jnp.sum(arrived.astype(jnp.float32), axis=0)
    at = 4 * head_width
    grads = [reduced[:, k * head_width : (k + 1) * head_width] for k in range(4)]
    router_grad = reduced[:, at : at + expert_count]
    at = at + expert_count
    bias_grad = reduced[:, at + 1 :].reshape(-1)[:bias_count].reshape(bias_term.shape)
    attn_term = jnp.sum(dnormed_one * inputs_f * scale_one, axis=0)
    attn_gain_grad = jnp.sum(exchange(attn_term.reshape(group_size, block_rows)), axis=0)
    first_back = norm_back(dnormed_one, inputs_f, scale_one, gain_one)
    input_grad = own_columns(dresidual + first_back)
    return (
        block_output,
        input_grad,
        attn_gain_grad,
        grads[0],
        grads[1],
        grads[2],
        grads[3],
        bias_grad,
        reduced[:, at],
        router_grad,
        in_grad[None],
        out_grad[None],
    )


def on_device(
    block_input,
    attn_gain,
    query_weight,
    key_weight,
    value_weight,
    output_weight,
    bias_table,
    ffn_gain,
    router_weight,
    expert_in,
    expert_out,
    expert_ids,
    out_cotangent,
):
    tensor_size = lax.axis_size("tensor")
    group_size = lax.axis_size("dp")
    tensor_index = lax.axis_index("tensor")
    own_expert = lax.axis_index("dp")
    token_count, model_width = block_input.shape
    column_width = model_width // tensor_size
    column_start = tensor_index * column_width
    expert_count = group_size * expert_in.shape[0]
    capacity = tensor_size * max(1, 3 * token_count // (5 * expert_count))
    slot_rows = expert_count * capacity
    seq_count = token_count // SEQ_LEN
    head_local = bias_table.shape[0]
    head_width = head_local * HEAD_DIM
    block_rows = query_weight.shape[0]
    low = jnp.bfloat16

    def own_columns(matrix):
        return lax.dynamic_slice_in_dim(matrix, column_start, column_width, 1)

    capacity = -(-capacity // 16) * 16
    slot_rows = expert_count * capacity
    small = jnp.concatenate(
        [attn_gain[None, :], ffn_gain[None, :], jnp.zeros((6, block_rows), low), router_weight.T],
        axis=0,
    )
    small = lax.dynamic_update_slice(
        jnp.zeros((small.shape[0], model_width), low), small, (0, own_expert * block_rows)
    )
    (
        qkv_full,
        output_full,
        gains,
        qkv,
        probs,
        context,
        attn_out,
        normed_two,
        map_both,
        map_signed,
        expert_rows,
        cot_arrived,
    ) = front(
        group_size,
        tensor_size,
        capacity,
        block_input,
        query_weight,
        key_weight,
        value_weight,
        output_weight,
        small,
        bias_table,
        expert_ids.T,
        out_cotangent,
    )
    probs = probs[None]
    labels = jnp.arange(expert_count, dtype=jnp.int32)
    map_first = jnp.maximum(map_signed, 0)
    map_second = jnp.maximum(-map_signed, 0)
    cot_rows = cot_arrived[:, :model_width].astype(jnp.float32)
    other_ids = cot_arrived[:, model_width].astype(jnp.int32) - own_expert
    router_full = gains[8:].T.astype(low)
    gain_one = gains[0]
    gain_two = gains[1]
    inputs_f = block_input.astype(jnp.float32)
    scale_one = rms_scale(inputs_f)
    normed_one = (inputs_f * scale_one * gain_one).astype(low)
    bucket_vec = bucket_vector_at(jnp.arange(SEQ_LEN, dtype=jnp.int32), NB)
    bucket_labels = jnp.arange(NB, dtype=jnp.int32)
    residual = inputs_f + attn_out.astype(jnp.float32)
    scale_two = rms_scale(residual)

    logits = dot(normed_two, router_full)
    picked = (expert_ids[:, :, None] == labels[None, None, :]).astype(jnp.float32)
    chosen = jnp.sum(picked * logits[:, None, :], axis=2)
    first_gate = jax.nn.sigmoid(chosen[:, 0] - chosen[:, 1])
    second_gate = 1.0 - first_gate

    weight_in = expert_in[0]
    weight_out = expert_out[0]
    pre_act = dot(expert_rows, weight_in)
    active, pullback = jax.vjp(jax.nn.gelu, pre_act)
    active = active.astype(low)
    owner_out = dot(active, weight_out)
    owner_logits = dot(expert_rows, router_full)
    own_logit = jnp.sum(
        jnp.where(labels[None, :] == own_expert, owner_logits, 0.0), axis=1
    )
    other_logit = jnp.sum(
        jnp.where(labels[None, :] == other_ids[:, None], owner_logits, 0.0), axis=1
    )
    row_gate = jax.nn.sigmoid(own_logit - other_logit)
    expert_drows = (row_gate[:, None] * cot_rows).astype(low)
    dpre = pullback(dot(expert_drows, weight_out, ((1,), (1,))))[0].astype(low)
    owner_back = dot(dpre, weight_in, ((1,), (1,))).astype(low)
    gate_part = jnp.sum(cot_rows * owner_out, axis=1, keepdims=True).astype(low)
    back_parcel = jnp.concatenate(
        [owner_back, jnp.broadcast_to(gate_part, (slot_rows, LANES))], axis=1
    )
    back_rows = exchange(
        back_parcel.reshape(group_size, capacity, model_width + LANES)
    ).reshape(slot_rows, model_width + LANES)
    out_rows = exchange(
        owner_out.astype(low).reshape(group_size, capacity, model_width)
    ).reshape(slot_rows, model_width)
    out_grad = dot(active, expert_drows, ((0,), (0,)))
    in_grad = dot(expert_rows, dpre, ((0,), (0,)))

    dnormed_part = dot(map_both, back_rows[:, :model_width], ((0,), (0,)))
    gate_diff_part = dot(map_first - map_second, back_rows[:, model_width:], ((0,), (0,)))
    gate_rows = -(-token_count // model_width)
    gate_line = jnp.pad(gate_diff_part[:, 0], (0, gate_rows * model_width - token_count))
    summed = lax.psum(
        jnp.concatenate(
            [dnormed_part, gate_line.reshape(gate_rows, model_width)], axis=0
        ).astype(low),
        "tensor",
    ).astype(jnp.float32)
    gate_diff = summed[token_count:].reshape(-1)[:token_count]
    mixture_part = first_gate[:, None] * dot(map_first, out_rows, ((0,), (0,)))
    mixture_part = mixture_part + second_gate[:, None] * dot(
        map_second, out_rows, ((0,), (0,))
    )
    mixture_parts = mixture_part.astype(low).reshape(token_count, tensor_size, column_width)
    mixture_parts = jnp.swapaxes(mixture_parts, 0, 1)

    dlogit = gate_diff * first_gate * second_gate
    signed = jnp.stack([dlogit, -dlogit], axis=1)
    dlogits = jnp.sum(picked * signed[:, :, None], axis=1).astype(low)
    router_term = dot(normed_two, dlogits, ((0,), (0,)))
    dnormed_two = summed[:token_count] + dot(dlogits, router_full, ((1,), (1,)))
    ffn_term = jnp.sum(dnormed_two * residual * scale_two, axis=0)
    cot_f = out_cotangent.astype(jnp.float32)
    dresidual = cot_f + norm_back(dnormed_two, residual, scale_two, gain_two)
    dres_low = dresidual.astype(low)
    mixture_parts, dres_low = lax.optimization_barrier((mixture_parts, dres_low))
    mixture_parts = lax.all_to_all(
        mixture_parts, "tensor", split_axis=0, concat_axis=0, tiled=True
    )

    output_term = dot(dres_low, context, ((0,), (0,)))
    dcontext = dot(dres_low, output_full).astype(low)
    dqkv, diagonal = attend_backward(qkv, probs, dcontext, seq_count, head_local)
    reverse_onehot = (bucket_vec[::-1][:, None] == bucket_labels[None, :]).astype(jnp.float32)
    bias_term = jnp.dot(
        jnp.sum(diagonal, axis=0),
        reverse_onehot,
        precision=lax.Precision.HIGHEST,
        preferred_element_type=jnp.float32,
    )
    dnormed_part = dot(dqkv, qkv_full, ((1,), (1,))).astype(low)
    dnormed_part, mixture_parts = lax.optimization_barrier((dnormed_part, mixture_parts))
    dnormed_one = lax.psum(dnormed_part, "tensor").astype(jnp.float32)
    qkv_term = dot(normed_one, dqkv, ((0,), (0,)))
    bias_count = bias_term.size
    bias_cols = -(-bias_count // block_rows)
    bias_block = jnp.pad(bias_term.reshape(-1), (0, bias_cols * block_rows - bias_count))
    bias_block = jnp.tile(bias_block.reshape(block_rows, bias_cols), (group_size, 1))
    terms = jnp.concatenate(
        [qkv_term, output_term, router_term, ffn_term[:, None], bias_block],
        axis=1,
    ).astype(low)
    term_width = terms.shape[1]
    arrived = exchange(terms.reshape(group_size, block_rows, term_width))
    arrived, dnormed_one = lax.optimization_barrier((arrived, dnormed_one))
    mixture = jnp.sum(mixture_parts.astype(jnp.float32), axis=0)
    block_output = (own_columns(residual) + mixture).astype(low)
    reduced = jnp.sum(arrived.astype(jnp.float32), axis=0)
    at = 4 * head_width
    grads = [reduced[:, k * head_width : (k + 1) * head_width] for k in range(4)]
    router_grad = reduced[:, at : at + expert_count]
    at = at + expert_count
    bias_grad = reduced[:, at + 1 :].reshape(-1)[:bias_count].reshape(bias_term.shape)
    attn_term = jnp.sum(dnormed_one * inputs_f * scale_one, axis=0)
    attn_gain_grad = jnp.sum(exchange(attn_term.reshape(group_size, block_rows)), axis=0)
    first_back = norm_back(dnormed_one, inputs_f, scale_one, gain_one)
    input_grad = own_columns(dresidual + first_back)
    return (
        block_output,
        input_grad,
        attn_gain_grad,
        grads[0],
        grads[1],
        grads[2],
        grads[3],
        bias_grad,
        reduced[:, at],
        router_grad,
        in_grad[None],
        out_grad[None],
    )


def choose(mesh):
    def run(*arrays):
        block_rows = arrays[2].shape[0]
        fits = (
            block_rows % 16 == 0
            and arrays[9].shape[0] == 1
            and mesh.shape["tensor"] == 4
            and arrays[0].shape[0] == SEQ_LEN
        )
        return (on_device if fits else on_device_general)(*arrays)

    return run


def solution(mesh):
    placed = (
        P("dp", None),
        P("dp"),
        P("dp", "tensor"),
        P("dp", "tensor"),
        P("dp", "tensor"),
        P("dp", "tensor"),
        P("tensor", None),
        P("dp"),
        P("dp", None),
        P("dp", None, "tensor"),
        P("dp", "tensor", None),
        P("dp", None),
        P("dp", None),
    )
    return jax.shard_map(
        choose(mesh),
        mesh=mesh,
        in_specs=placed,
        out_specs=(
            P("dp", "tensor"),
            P("dp", "tensor"),
            P("dp"),
            P("dp", "tensor"),
            P("dp", "tensor"),
            P("dp", "tensor"),
            P("dp", "tensor"),
            P("tensor", None),
            P("dp"),
            P("dp", None),
            P("dp", None, "tensor"),
            P("dp", "tensor", None),
        ),
        check_vma=False,
    )
```

```python
import functools
import math

import jax
import jax.numpy as jnp
from jax import lax
from jax.experimental import pallas as pl
from jax.experimental.pallas import tpu as pltpu
from jax.sharding import PartitionSpec as P

HEAD_DIM = 64
NB = 32
SEQ_LEN = 512
LANES = 128
VMEM_BYTES = 63 * 1024 * 1024


EPSILON = 1e-06
MASKED = -1e30


def bucket_vector_at(steps_ids, bucket_count):
    exact_count = bucket_count // 2
    distant = jnp.full(steps_ids.shape, exact_count, jnp.int32)
    for level_index in range(1, bucket_count - exact_count):
        border = int(math.ceil(exact_count * 8.0 ** (level_index / (bucket_count - exact_count))))
        distant = distant + (steps_ids >= border).astype(jnp.int32)
    return jnp.where(steps_ids < exact_count, steps_ids, distant)


def norm_back(dnormed, row_values, row_scale, gain_row):
    inner_mean = jnp.mean(gain_row * dnormed * row_values, axis=-1, keepdims=True)
    return row_scale * (gain_row * dnormed - row_values * row_scale * row_scale * inner_mean)


def rms_scale(matrix):
    return lax.rsqrt(jnp.mean(matrix * matrix, axis=-1, keepdims=True) + EPSILON)


def dot(left, right, dims=((1,), (0,))):
    return lax.dot_general(left, right, (dims, ((), ())), preferred_element_type=jnp.float32)


def forward_kernel(qkv_ref, wrapped_ref, context_ref, probs_ref):
    length = qkv_ref.shape[0]
    heads = probs_ref.shape[0]
    width = heads * HEAD_DIM
    factor = HEAD_DIM ** (-0.5)
    rows = lax.broadcasted_iota(jnp.int32, (length, length), 0)
    cols = lax.broadcasted_iota(jnp.int32, (length, length), 1)
    causal = rows >= cols
    for h in range(heads):
        lo, hi = h * HEAD_DIM, (h + 1) * HEAD_DIM
        queries = qkv_ref[:, lo:hi]
        keys = qkv_ref[:, width + lo : width + hi]
        values = qkv_ref[:, 2 * width + lo : 2 * width + hi]
        bias = jnp.broadcast_to(wrapped_ref[h : h + 1, :], (length, length))
        bias = pltpu.roll(bias, 0, 1, stride=1, stride_axis=0)
        scores = jnp.where(causal, dot(queries, keys, ((1,), (1,))) * factor + bias, MASKED)
        row_max = jnp.max(scores, axis=-1, keepdims=True)
        row_total = jnp.sum(jnp.exp(scores - row_max), axis=-1, keepdims=True)
        probs = jnp.exp(scores - (row_max + jnp.log(row_total))).astype(jnp.bfloat16)
        probs_ref[h] = probs
        context_ref[:, lo:hi] = dot(probs, values).astype(jnp.bfloat16)


def backward_kernel(qkv_ref, probs_ref, dcontext_ref, dqkv_ref, diagonal_ref):
    length = qkv_ref.shape[0]
    heads = probs_ref.shape[0]
    width = heads * HEAD_DIM
    factor = HEAD_DIM ** (-0.5)
    rows = lax.broadcasted_iota(jnp.int32, (length, length), 0)
    cols = lax.broadcasted_iota(jnp.int32, (length, length), 1)
    flip = (rows + cols == length - 1).astype(jnp.float32).astype(jnp.bfloat16)
    for h in range(heads):
        lo, hi = h * HEAD_DIM, (h + 1) * HEAD_DIM
        queries = qkv_ref[:, lo:hi]
        keys = qkv_ref[:, width + lo : width + hi]
        values = qkv_ref[:, 2 * width + lo : 2 * width + hi]
        dcontext = dcontext_ref[:, lo:hi]
        probs = probs_ref[h]
        weights = probs.astype(jnp.float32)
        dweights = dot(dcontext, values, ((1,), (1,)))
        agreement = jnp.sum(weights * dweights, axis=-1, keepdims=True)
        dscores = (weights * (dweights - agreement)).astype(jnp.bfloat16)
        dqkv_ref[:, lo:hi] = (factor * dot(dscores, keys)).astype(jnp.bfloat16)
        dqkv_ref[:, width + lo : width + hi] = (
            factor * dot(dscores, queries, ((0,), (0,)))
        ).astype(jnp.bfloat16)
        dqkv_ref[:, 2 * width + lo : 2 * width + hi] = dot(
            probs, dcontext, ((0,), (0,))
        ).astype(jnp.bfloat16)
        skewed = pltpu.roll(dot(flip, dscores), 0, 1, stride=1, stride_axis=0)
        diagonal_ref[h : h + 1, :] = jnp.sum(skewed, axis=0, keepdims=True)


def attend_forward(qkv, wrapped, seq_count, heads):
    width = heads * HEAD_DIM
    return pl.pallas_call(
        forward_kernel,
        grid=(seq_count,),
        out_shape=(
            jax.ShapeDtypeStruct((seq_count * SEQ_LEN, width), jnp.bfloat16),
            jax.ShapeDtypeStruct((seq_count, heads, SEQ_LEN, SEQ_LEN), jnp.bfloat16),
        ),
        in_specs=[
            pl.BlockSpec((SEQ_LEN, 3 * width), lambda s: (s, 0)),
            pl.BlockSpec((heads, SEQ_LEN), lambda s: (0, 0)),
        ],
        out_specs=(
            pl.BlockSpec((SEQ_LEN, width), lambda s: (s, 0)),
            pl.BlockSpec((None, heads, SEQ_LEN, SEQ_LEN), lambda s: (s, 0, 0, 0)),
        ),
        name="attend_forward",
    )(qkv, wrapped)


def attend_backward(qkv, probs, dcontext, seq_count, heads):
    width = heads * HEAD_DIM
    return pl.pallas_call(
        backward_kernel,
        grid=(seq_count,),
        out_shape=(
            jax.ShapeDtypeStruct((seq_count * SEQ_LEN, 3 * width), jnp.bfloat16),
            jax.ShapeDtypeStruct((seq_count, heads, SEQ_LEN), jnp.float32),
        ),
        in_specs=[
            pl.BlockSpec((SEQ_LEN, 3 * width), lambda s: (s, 0)),
            pl.BlockSpec((None, heads, SEQ_LEN, SEQ_LEN), lambda s: (s, 0, 0, 0)),
            pl.BlockSpec((SEQ_LEN, width), lambda s: (s, 0)),
        ],
        out_specs=(
            pl.BlockSpec((SEQ_LEN, 3 * width), lambda s: (s, 0)),
            pl.BlockSpec((None, heads, SEQ_LEN), lambda s: (s, 0, 0)),
        ),
        name="attend_backward",
    )(qkv, probs, dcontext)


def exchange(parcel):
    return lax.all_to_all(parcel, "dp", split_axis=0, concat_axis=0, tiled=True)


def remote(src, dst, send_sem, recv_sem, axis, index):
    return pltpu.make_async_remote_copy(
        src_ref=src,
        dst_ref=dst,
        send_sem=send_sem,
        recv_sem=recv_sem,
        device_id={axis: index},
        device_id_type=pl.DeviceIdType.MESH,
    )


def rows_at(index, count):
    return pl.ds(pl.multiple_of(index * count, count), count)


def gelu_both(u):
    slope = math.sqrt(2.0 / math.pi)
    cubic = 0.044715
    square = u * u
    t = jnp.tanh(slope * u * (1.0 + cubic * square))
    half = 0.5 + 0.5 * t
    value = u * half
    grad = half + 0.5 * u * (1.0 - t * t) * (slope * (1.0 + 3.0 * cubic * square))
    return value, grad


def layer_kernel(
    group_size,
    tensor_size,
    x_ref,
    q_ref,
    k_ref,
    v_ref,
    o_ref,
    small_ref,
    bias_ref,
    ids_ref,
    cot_ref,
    win_hbm,
    wout_hbm,
    block_out,
    input_out,
    qkv_out,
    wo_out,
    sums_out,
    in_grad_hbm,
    out_grad_hbm,
    wqkv_ref,
    wo_ref,
    gains_ref,
    qkv_ref,
    probs_ref,
    context_ref,
    normed_one_ref,
    normed_ref,
    residual_ref,
    residual_t_ref,
    both_ref,
    signed_ref,
    gated_ref,
    rows_ref,
    cots_ref,
    win_ref,
    wout_ref,
    active_ref,
    drows_ref,
    dpre_ref,
    grad_ref,
    send_ref,
    cot_send_ref,
    back_send_ref,
    back_ref,
    out_send_ref,
    out_ref,
    gate_send_ref,
    gate_ref,
    small_buf,
    code_ref,
    gates_ref,
    part_ref,
    near_ref,
    middle_ref,
    total_ref,
    gate_line_ref,
    dres_ref,
    dres_low_ref,
    dkeys_ref,
    dvalues_ref,
    dqkv_ref,
    diagonal_ref,
    terms_send_ref,
    terms_ref,
    oterms_send_ref,
    oterms_ref,
    mix_send_ref,
    mix_ref,
    sums_send_ref,
    sums_ref,
    w_sems,
    a2a_sems,
    line_sems,
    z_sems,
    local_sems,
):
    me = lax.axis_index("dp")
    level = lax.axis_index("tensor")
    token_count, model_width = x_ref.shape
    experts = group_size
    capacity = rows_ref.shape[0] // group_size
    block_rows, head_width = q_ref.shape
    heads = bias_ref.shape[0]
    column_width = model_width // tensor_size
    low = jnp.bfloat16
    f32 = jnp.float32
    near = level + 1 - 2 * lax.rem(level, 2)
    across = tensor_size - 1 - level
    is_end = jnp.logical_or(level == 0, level == tensor_size - 1)
    is_middle = jnp.logical_not(is_end)
    chip = me // 2
    core = lax.rem(me, 2)
    chips = group_size // 2
    chunk = LANES
    chunks = token_count // chunk
    factor = HEAD_DIM ** (-0.5)

    def peer_of(j):
        other_chip = lax.rem(chip - j // 2 + chips, chips)
        return 2 * other_chip + lax.rem(core + j, 2)

    def each_peer(body):
        def step(j, carry):
            body(peer_of(j))
            return carry

        lax.fori_loop(1, group_size, step, 0)

    def load_in():
        return pltpu.make_async_copy(win_hbm, win_ref, local_sems.at[0])

    def load_out():
        return pltpu.make_async_copy(wout_hbm, wout_ref, local_sems.at[1])

    load_in().start()
    load_out().start()

    mine = rows_at(me, block_rows)
    wqkv_ref[mine, :] = jnp.concatenate([q_ref[...], k_ref[...], v_ref[...]], axis=1)
    wo_ref[mine, :] = o_ref[...]
    small_buf[me] = small_ref[...]

    barrier = pltpu.get_barrier_semaphore()
    each_peer(
        lambda peer: pl.semaphore_signal(
            barrier, inc=1, device_id={"dp": peer}, device_id_type=pl.DeviceIdType.MESH
        )
    )

    def greet(step, carry):
        other = lax.rem(level + step, tensor_size)
        pl.semaphore_signal(
            barrier, inc=1, device_id={"tensor": other}, device_id_type=pl.DeviceIdType.MESH
        )
        return carry

    lax.fori_loop(1, tensor_size, greet, 0)
    pl.semaphore_wait(barrier, group_size + tensor_size - 2)

    def weight_copies(peer, source):
        block = rows_at(source, block_rows)
        return [
            remote(wqkv_ref.at[block], wqkv_ref.at[block], w_sems.at[0, peer], w_sems.at[1, source], "dp", peer),
            remote(wo_ref.at[block], wo_ref.at[block], w_sems.at[2, peer], w_sems.at[3, source], "dp", peer),
            remote(small_buf.at[source], small_buf.at[source], w_sems.at[4, peer], w_sems.at[5, source], "dp", peer),
        ]

    def start_all(copies):
        for copy in copies:
            copy.start()

    def recv_all(copies):
        for copy in copies:
            copy.wait_recv()

    def sent_all(copies):
        for copy in copies:
            copy.wait_send()

    each_peer(lambda peer: start_all(weight_copies(peer, me)))

    def block_copy(kind, src, dst, peer, source, count):
        return remote(
            src.at[rows_at(peer, count)],
            dst.at[rows_at(source, count)],
            a2a_sems.at[2 * kind, peer],
            a2a_sems.at[2 * kind + 1, source],
            "dp",
            peer,
        )

    def cot_copy(peer, source):
        return block_copy(0, cot_send_ref, cots_ref, peer, source, capacity)

    def row_copy(peer, source):
        return block_copy(1, send_ref, rows_ref, peer, source, capacity)

    def back_copy(peer, source):
        return block_copy(2, back_send_ref, back_ref, peer, source, capacity)

    def out_copy(peer, source):
        return block_copy(3, out_send_ref, out_ref, peer, source, capacity)

    def term_copies(peer, source):
        return [
            block_copy(4, terms_send_ref, terms_ref, peer, source, block_rows),
            block_copy(5, oterms_send_ref, oterms_ref, peer, source, block_rows),
        ]

    def gate_copy(peer, source):
        return remote(
            gate_send_ref.at[peer], gate_ref.at[source], a2a_sems.at[12, peer], a2a_sems.at[13, source], "dp", peer
        )

    def sums_copy(peer, source):
        return remote(
            sums_send_ref, sums_ref.at[source], a2a_sems.at[14, peer], a2a_sems.at[15, source], "dp", peer
        )

    ids_first = ids_ref[0:1, :]
    ids_second = ids_ref[1:2, :]
    labels = lax.broadcasted_iota(jnp.int32, (experts, token_count), 0)
    member = jnp.logical_or(labels == ids_first, labels == ids_second)
    tokens_r = lax.broadcasted_iota(jnp.int32, (token_count, token_count), 0)
    tokens_c = lax.broadcasted_iota(jnp.int32, (token_count, token_count), 1)
    upper = jnp.where(tokens_r < tokens_c, 1.0, 0.0).astype(low)
    counted = dot(jnp.where(member, 1.0, 0.0).astype(low), upper)
    code_ref[...] = jnp.where(member, counted, -1.0)
    slots = lax.broadcasted_iota(jnp.int32, (capacity, token_count), 0).astype(f32)
    id_total = jnp.broadcast_to((ids_first + ids_second).astype(f32), (LANES, token_count)).astype(low)

    def make_maps(expert, carry):
        block = rows_at(expert, capacity)
        hit = slots == code_ref[pl.ds(expert, 1), :]
        sign = jnp.where(ids_first == expert, 1.0, -1.0)
        both = jnp.where(hit, 1.0, 0.0).astype(low)
        both_ref[block, :] = both
        signed_ref[block, :] = jnp.where(hit, sign, 0.0).astype(low)
        cot_send_ref[block, :model_width] = dot(both, cot_ref[...]).astype(low)
        cot_send_ref[block, model_width:] = dot(both, id_total, ((1,), (1,))).astype(low)
        return carry

    lax.fori_loop(0, experts, make_maps, 0)

    inputs_f = x_ref[...].astype(f32)
    scaled = inputs_f * rms_scale(inputs_f)

    lane = lax.broadcasted_iota(jnp.int32, (heads, token_count), 1)
    wrap_bucket = bucket_vector_at(jnp.where(lane == 0, 0, token_count - lane), NB)
    wrapped = jnp.zeros((heads, token_count), f32)
    for b in range(NB):
        wrapped = jnp.where(wrap_bucket == b, bias_ref[:, b : b + 1], wrapped)

    each_peer(lambda source: recv_all(weight_copies(source, source)))
    each_peer(lambda peer: cot_copy(peer, me).start())

    gains = small_buf[0].astype(f32)
    for source in range(1, group_size):
        gains = gains + small_buf[source].astype(f32)
    gains_ref[...] = gains
    gain_one = gains_ref[0:1, :]
    gain_two = gains_ref[1:2, :]
    normed_one_ref[...] = (scaled * gain_one).astype(low)
    qkv_ref[...] = dot(normed_one_ref[...], wqkv_ref[...]).astype(low)

    def at_chunk(c):
        return slice(c * chunk, (c + 1) * chunk)

    def line_up(r, c):
        if c is None:
            src, dst, c = gate_line_ref.at[0], gate_line_ref.at[1], chunks
        else:
            src, dst = part_ref.at[at_chunk(c)], near_ref.at[at_chunk(c)]
        return remote(src, dst, line_sems.at[r, 0, c], line_sems.at[r, 1, c], "tensor", near)

    def line_over(r, c):
        if c is None:
            src, dst, c = gate_line_ref.at[0], gate_line_ref.at[2], chunks
        else:
            src, dst = part_ref.at[at_chunk(c)], middle_ref.at[r % 2, at_chunk(c)]
        return remote(src, dst, line_sems.at[r, 2, c], line_sems.at[r, 3, c], "tensor", across)

    def line_down(r, c):
        if c is None:
            src = dst = gate_line_ref.at[3]
            c = chunks
        else:
            src = dst = total_ref.at[r, at_chunk(c)]
        return remote(src, dst, line_sems.at[r, 4, c], line_sems.at[r, 5, c], "tensor", near)

    def line_start(r, c):
        @pl.when(is_end)
        def _():
            line_up(r, c).start()

    def line_first(r, c):
        @pl.when(is_middle)
        def _():
            line_up(r, c).wait_recv()
            if c is None:
                gate_line_ref[0] = (gate_line_ref[0].astype(f32) + gate_line_ref[1].astype(f32)).astype(low)
            else:
                block = at_chunk(c)
                part_ref[block, :] = (part_ref[block, :].astype(f32) + near_ref[block, :].astype(f32)).astype(low)
            line_over(r, c).start()

    def line_second(r, c):
        @pl.when(is_middle)
        def _():
            line_over(r, c).wait_recv()
            if c is None:
                gate_line_ref[3] = (gate_line_ref[0].astype(f32) + gate_line_ref[2].astype(f32)).astype(low)
            else:
                block = at_chunk(c)
                total_ref[r, block, :] = (
                    part_ref[block, :].astype(f32) + middle_ref[r % 2, block, :].astype(f32)
                ).astype(low)
            line_down(r, c).start()

    def line_take(r, c):
        @pl.when(is_end)
        def _():
            line_down(r, c).wait_recv()

    def line_drain(r, c):
        @pl.when(is_end)
        def _():
            line_up(r, c).wait_send()

        @pl.when(is_middle)
        def _():
            line_over(r, c).wait_send()
            line_down(r, c).wait_send()

    for c in range(chunks):
        lo, hi = c * chunk, (c + 1) * chunk
        causal = lax.broadcasted_iota(jnp.int32, (chunk, hi), 0) + lo >= (
            lax.broadcasted_iota(jnp.int32, (chunk, hi), 1)
        )
        pieces = []
        for h in range(heads):
            at = h * HEAD_DIM
            queries = qkv_ref[lo:hi, at : at + HEAD_DIM]
            keys = qkv_ref[0:hi, head_width + at : head_width + at + HEAD_DIM]
            values = qkv_ref[0:hi, 2 * head_width + at : 2 * head_width + at + HEAD_DIM]
            bias = jnp.broadcast_to(wrapped[h : h + 1, :], (chunk, token_count))
            bias = pltpu.roll(bias, lo, 1, stride=1, stride_axis=0)[:, :hi]
            scores = jnp.where(causal, dot(queries, keys, ((1,), (1,))) * factor + bias, MASKED)
            row_max = jnp.max(scores, axis=-1, keepdims=True)
            grown = jnp.exp(scores - row_max)
            total = jnp.sum(grown, axis=-1, keepdims=True)
            probs = (grown * (1.0 / total)).astype(low)
            probs_ref[h, lo:hi, 0:hi] = probs
            pieces.append(dot(probs, values).astype(low))
        context = jnp.concatenate(pieces, axis=1)
        context_ref[lo:hi, :] = context
        part_ref[lo:hi, :] = dot(context, wo_ref[...], ((1,), (1,))).astype(low)
        line_start(0, c)
        if c >= 1:
            line_first(0, c - 1)
        if c >= 2:
            line_second(0, c - 2)
    line_first(0, chunks - 1)
    line_second(0, chunks - 2)
    line_second(0, chunks - 1)

    for c in range(chunks):
        block = at_chunk(c)
        line_take(0, c)
        residual = x_ref[block, :].astype(f32) + total_ref[0, block, :].astype(f32)
        residual_ref[block, :] = residual
        normed_ref[block, :] = (residual * rms_scale(residual) * gain_two).astype(low)

    def send_rows(peer):
        block = rows_at(peer, capacity)
        send_ref[block, :] = dot(both_ref[block, :], normed_ref[...]).astype(low)
        row_copy(peer, me).start()

    each_peer(send_rows)
    own = rows_at(me, capacity)
    rows_ref[own, :] = dot(both_ref[own, :], normed_ref[...]).astype(low)
    cots_ref[own, :] = cot_send_ref[own, :]

    gains_low = gains_ref[...].astype(low)
    logits = dot(gains_low, normed_ref[...], ((1,), (1,)))
    label_rows = lax.broadcasted_iota(jnp.int32, logits.shape, 0) - 8
    chosen_first = jnp.sum(jnp.where(label_rows == ids_first, logits, 0.0), axis=0, keepdims=True)
    chosen_second = jnp.sum(jnp.where(label_rows == ids_second, logits, 0.0), axis=0, keepdims=True)
    gate_first = jax.nn.sigmoid(chosen_first - chosen_second)
    gate_second = 1.0 - gate_first
    gates_ref[0:1, :] = gate_first
    gates_ref[1:2, :] = gate_second

    def make_gated(expert, carry):
        block = rows_at(expert, capacity)
        sign = signed_ref[block, :].astype(f32)
        gated_ref[block, :] = jnp.where(sign > 0, gate_first, jnp.where(sign < 0, gate_second, 0.0)).astype(low)
        return carry

    lax.fori_loop(0, experts, make_gated, 0)
    for z in range(tensor_size):

        @pl.when(level == z)
        def _():
            residual_t_ref[...] = jnp.transpose(residual_ref[:, z * column_width : (z + 1) * column_width])

    load_in().wait()
    load_out().wait()

    pair = 2 * capacity
    ones = jnp.ones((16, model_width), low)

    def expert_step(step, carry):
        other = lax.rem(chip + step, chips)
        block = rows_at(other, pair)
        for c in range(2):
            source = 2 * other + c

            @pl.when(source != me)
            def _():
                cot_copy(source, source).wait_recv()
                row_copy(source, source).wait_recv()

        rows = rows_ref[block, :]
        value, slope = gelu_both(dot(rows, win_ref[...]))
        active = value.astype(low)
        active_ref[block, :] = active
        owner_logits = dot(rows, gains_low, ((1,), (1,)))
        columns = lax.broadcasted_iota(jnp.int32, owner_logits.shape, 1) - 8
        other_ids = cots_ref[block, model_width : model_width + 1].astype(f32).astype(jnp.int32) - me
        own_logit = jnp.sum(jnp.where(columns == me, owner_logits, 0.0), axis=1, keepdims=True)
        other_logit = jnp.sum(jnp.where(columns == other_ids, owner_logits, 0.0), axis=1, keepdims=True)
        row_gate = jax.nn.sigmoid(own_logit - other_logit)
        cot = cots_ref[block, :model_width].astype(f32)
        drows = (row_gate * cot).astype(low)
        drows_ref[block, :] = drows
        dpre = (dot(drows, wout_ref[...], ((1,), (1,))) * slope).astype(low)
        dpre_ref[block, :] = dpre
        back_send_ref[block, :] = dot(dpre, win_ref[...], ((1,), (1,))).astype(low)
        for c in range(2):
            source = 2 * other + c

            @pl.when(source != me)
            def _():
                back_copy(source, me).start()

        owner_out = dot(active, wout_ref[...])
        out_send_ref[block, :] = owner_out.astype(low)
        agree = (cot * owner_out).astype(low)
        for c in range(2):
            source = 2 * other + c
            gate_send_ref[source] = dot(ones, agree[c * capacity : (c + 1) * capacity, :], ((1,), (1,))).astype(low)

            @pl.when(source != me)
            def _():
                gate_copy(source, me).start()

        return carry

    lax.fori_loop(0, chips, expert_step, 0)
    back_ref[own, :] = back_send_ref[own, :]
    out_ref[own, :] = out_send_ref[own, :]
    gate_ref[me] = gate_send_ref[me]

    def grad_out(which, part):
        target = (out_grad_hbm, in_grad_hbm)[which]
        block = slice(part * 256, (part + 1) * 256)
        return pltpu.make_async_copy(grad_ref.at[which, block], target.at[block], local_sems.at[2 + which * 8 + part])

    parts = win_ref.shape[0] // 256
    for part in range(parts):
        block = slice(part * 256, (part + 1) * 256)
        grad_ref[0, block, :] = dot(active_ref[:, block], drows_ref[...], ((0,), (0,)))
        grad_out(0, part).start()
        grad_ref[1, block, :] = dot(rows_ref[:, block], dpre_ref[...], ((0,), (0,)))
        grad_out(1, part).start()

    each_peer(lambda source: gate_copy(source, source).wait_recv())
    each_peer(lambda source: back_copy(source, source).wait_recv())
    each_peer(lambda peer: out_copy(peer, me).start())
    gate_line = dot(gate_ref[0], signed_ref[0:capacity, :])
    for e in range(1, experts):
        gate_line = gate_line + dot(gate_ref[e], signed_ref[e * capacity : (e + 1) * capacity, :])
    gate_line_ref[0] = gate_line.astype(low)
    line_start(1, None)
    order = list(range(chunks))[::-1]
    queue = [None] + order
    for place, c in enumerate(queue):
        if c is not None:
            block = at_chunk(c)
            line_drain(0, c)
            part_ref[block, :] = dot(both_ref[:, block], back_ref[...], ((0,), (0,))).astype(low)
            line_start(1, c)
        if place >= 1:
            line_first(1, queue[place - 1])
        if place >= 2:
            line_second(1, queue[place - 2])
    line_first(1, queue[-1])
    line_second(1, queue[-2])
    line_second(1, queue[-1])

    line_take(1, None)
    gate_diff = gate_line_ref[3, 0:1, :].astype(f32)
    dlogit = gate_diff * gates_ref[0:1, :] * gates_ref[1:2, :]
    dlogits = jnp.where(
        label_rows == ids_first, dlogit, jnp.where(label_rows == ids_second, -dlogit, 0.0)
    ).astype(low)
    sums_send_ref[...] = dot(dlogits, normed_ref[...])

    def backward_chunk(c, ffn_term):
        lo, hi = c * chunk, (c + 1) * chunk
        block = at_chunk(c)
        line_take(1, c)
        dnormed = total_ref[1, block, :].astype(f32) + dot(dlogits[:, block], gains_low, ((0,), (0,)))
        residual = residual_ref[block, :]
        scale_two = rms_scale(residual)
        ffn_term = ffn_term + jnp.sum(dnormed * residual * scale_two, axis=0, keepdims=True)
        dres = cot_ref[block, :].astype(f32) + norm_back(dnormed, residual, scale_two, gain_two)
        dres_ref[block, :] = dres
        dres_low = dres.astype(low)
        dres_low_ref[block, :] = dres_low
        dcontext = dot(dres_low, wo_ref[...]).astype(low)
        flip = (
            lax.broadcasted_iota(jnp.int32, (chunk, chunk), 0)
            + lax.broadcasted_iota(jnp.int32, (chunk, chunk), 1)
            == chunk - 1
        )
        flip = jnp.where(flip, 1.0, 0.0).astype(low)
        first, second, third = [], [], []
        for h in range(heads):
            at = h * HEAD_DIM
            queries = qkv_ref[lo:hi, at : at + HEAD_DIM]
            keys = qkv_ref[0:hi, head_width + at : head_width + at + HEAD_DIM]
            values = qkv_ref[0:hi, 2 * head_width + at : 2 * head_width + at + HEAD_DIM]
            dctx = dcontext[:, at : at + HEAD_DIM]
            probs = probs_ref[h, lo:hi, 0:hi]
            weights = probs.astype(f32)
            dweights = dot(dctx, values, ((1,), (1,)))
            agreement = jnp.sum(weights * dweights, axis=-1, keepdims=True)
            dscores = (weights * (dweights - agreement)).astype(low)
            first.append((factor * dot(dscores, keys)).astype(low))
            dkeys = dot(dscores, queries, ((0,), (0,)))
            dvalues = dot(probs, dctx, ((0,), (0,)))
            if c < chunks - 1:
                dkeys = dkeys + dkeys_ref[h, 0:hi, :]
                dvalues = dvalues + dvalues_ref[h, 0:hi, :]
            if lo:
                dkeys_ref[h, 0:lo, :] = dkeys[0:lo]
                dvalues_ref[h, 0:lo, :] = dvalues[0:lo]
            second.append((factor * dkeys[lo:hi]).astype(low))
            third.append(dvalues[lo:hi].astype(low))
            flipped = dot(flip, dscores)
            if hi < token_count:
                flipped = jnp.concatenate([flipped, jnp.zeros((chunk, token_count - hi), f32)], axis=1)
            skewed = pltpu.roll(flipped, token_count - (hi - 1), 1, stride=1, stride_axis=0)
            line = jnp.sum(skewed, axis=0, keepdims=True)
            if c < chunks - 1:
                line = line + diagonal_ref[h : h + 1, :]
            diagonal_ref[h : h + 1, :] = line
        dqkv = jnp.concatenate(first + second + third, axis=1)
        dqkv_ref[block, :] = dqkv
        line_drain(1, c)
        part_ref[block, :] = dot(dqkv, wqkv_ref[...], ((1,), (1,))).astype(low)
        line_start(2, c)
        return ffn_term

    ffn_term = jnp.zeros((1, model_width), f32)
    for place, c in enumerate(order):
        ffn_term = backward_chunk(c, ffn_term)
        if place >= 1:
            line_first(2, order[place - 1])
        if place >= 2:
            line_second(2, order[place - 2])

    for part in range(model_width // 256):
        block = slice(part * 256, (part + 1) * 256)
        terms_send_ref[block, :] = dot(normed_one_ref[:, block], dqkv_ref[...], ((0,), (0,))).astype(low)
        oterms_send_ref[block, :] = dot(dres_low_ref[:, block], context_ref[...], ((0,), (0,))).astype(low)
        if part == 0:
            line_first(2, order[-1])
            line_second(2, order[-2])
        if part == 1:
            line_second(2, order[-1])
    each_peer(lambda peer: start_all(term_copies(peer, me)))
    terms_ref[mine, :] = terms_send_ref[mine, :]
    oterms_ref[mine, :] = oterms_send_ref[mine, :]

    each_peer(lambda source: out_copy(source, source).wait_recv())
    for part in range(model_width // 256):
        block = slice(part * 256, (part + 1) * 256)
        mix_send_ref[block, :] = dot(out_ref[:, block], gated_ref[...], ((0,), (0,))).astype(low)

    def mix_copy(target, source):
        return remote(
            mix_send_ref.at[rows_at(target, column_width)],
            mix_ref.at[source],
            z_sems.at[0, target],
            z_sems.at[1, source],
            "tensor",
            target,
        )

    def each_level(body):
        def step(j, carry):
            body(lax.rem(level + j, tensor_size))
            return carry

        lax.fori_loop(1, tensor_size, step, 0)

    each_level(lambda target: mix_copy(target, level).start())
    mix_ref[level] = mix_send_ref[rows_at(level, column_width), :]

    attn_term = jnp.zeros((1, model_width), f32)
    for c in order:
        block = at_chunk(c)
        line_take(2, c)
        dnormed = total_ref[2, block, :].astype(f32)
        values = x_ref[block, :].astype(f32)
        scale_one = rms_scale(values)
        attn_term = attn_term + jnp.sum(dnormed * values * scale_one, axis=0, keepdims=True)
        dres_ref[block, :] = dres_ref[block, :] + norm_back(dnormed, values, scale_one, gain_one)

    sums_send_ref[0:1, :] = ffn_term
    sums_send_ref[1:2, :] = attn_term
    diagonal = diagonal_ref[0:heads, :]
    lanes = lax.broadcasted_iota(jnp.int32, (heads, model_width), 1)
    bias_rows = jnp.zeros((heads, model_width), f32)
    for b in range(NB):
        bucket_total = jnp.sum(jnp.where(wrap_bucket == b, diagonal, 0.0), axis=1, keepdims=True)
        bias_rows = jnp.where(lanes == b, bucket_total, bias_rows)
    sums_send_ref[2 : 2 + heads, :] = bias_rows
    each_peer(lambda peer: sums_copy(peer, me).start())
    sums_ref[me] = sums_send_ref[...]

    for z in range(tensor_size):

        @pl.when(level == z)
        def _():
            input_out[...] = jnp.transpose(dres_ref[:, z * column_width : (z + 1) * column_width])

    each_peer(lambda source: recv_all(term_copies(source, source)))
    reduced = terms_ref[0:block_rows, :].astype(f32)
    oreduced = oterms_ref[0:block_rows, :].astype(f32)
    for source in range(1, group_size):
        block = slice(source * block_rows, (source + 1) * block_rows)
        reduced = reduced + terms_ref[block, :].astype(f32)
        oreduced = oreduced + oterms_ref[block, :].astype(f32)
    for k in range(3):
        qkv_out[k] = reduced[:, k * head_width : (k + 1) * head_width]
    wo_out[...] = oreduced

    each_level(lambda source: mix_copy(source, source).wait_recv())
    mixture = mix_ref[0].astype(f32)
    for z in range(1, tensor_size):
        mixture = mixture + mix_ref[z].astype(f32)
    block_out[...] = (residual_t_ref[...] + mixture).astype(low)

    each_peer(lambda source: sums_copy(source, source).wait_recv())
    sums = sums_ref[0]
    for source in range(1, group_size):
        sums = sums + sums_ref[source]
    sums_out[...] = sums

    def drain(peer):
        sent_all(weight_copies(peer, me))
        cot_copy(peer, me).wait_send()
        row_copy(peer, me).wait_send()
        back_copy(peer, me).wait_send()
        gate_copy(peer, me).wait_send()
        out_copy(peer, me).wait_send()
        sent_all(term_copies(peer, me))
        sums_copy(peer, me).wait_send()

    each_peer(drain)
    each_level(lambda target: mix_copy(target, level).wait_send())
    line_drain(1, None)
    for c in order:
        line_drain(2, c)
    for part in range(parts):
        grad_out(0, part).wait()
        grad_out(1, part).wait()


def run_layer(group_size, tensor_size, capacity, x, q, k, v, o, small, bias, ids, cot, w_in, w_out):
    tokens, width = x.shape
    block_rows, head_width = q.shape
    heads = bias.shape[0]
    hidden = w_in.shape[1]
    slots = group_size * capacity
    low = jnp.bfloat16
    f32 = jnp.float32
    full = group_size * block_rows
    chunks = tokens // LANES
    column_width = width // tensor_size

    def shape(dims, dtype=low):
        return jax.ShapeDtypeStruct(dims, dtype)

    def room(*dims, dtype=low):
        return pltpu.VMEM(dims, dtype)

    vmem = pl.BlockSpec(memory_space=pltpu.VMEM)
    hbm = pl.BlockSpec(memory_space=pl.ANY)
    dma = pltpu.SemaphoreType.DMA
    return pl.pallas_call(
        functools.partial(layer_kernel, group_size, tensor_size),
        out_shape=(
            shape((column_width, tokens)),
            shape((column_width, tokens), f32),
            shape((3, block_rows, head_width), f32),
            shape((block_rows, head_width), f32),
            shape(small.shape, f32),
            shape((width, hidden), f32),
            shape((hidden, width), f32),
        ),
        in_specs=[vmem] * 9 + [hbm] * 2,
        out_specs=(vmem,) * 5 + (hbm,) * 2,
        scratch_shapes=[
            room(full, 3 * head_width),
            room(full, head_width),
            room(*small.shape, dtype=f32),
            room(tokens, 3 * head_width),
            room(heads, tokens, tokens),
            room(tokens, head_width),
            room(tokens, width),
            room(tokens, width),
            room(tokens, width, dtype=f32),
            room(column_width, tokens, dtype=f32),
            room(slots, tokens),
            room(slots, tokens),
            room(slots, tokens),
            room(slots, width),
            room(slots, width + LANES),
            room(width, hidden),
            room(hidden, width),
            room(slots, hidden),
            room(slots, width),
            room(slots, hidden),
            room(2, width, width, dtype=f32),
            room(slots, width),
            room(slots, width + LANES),
            room(slots, width),
            room(slots, width),
            room(slots, width),
            room(slots, width),
            room(group_size, 16, capacity),
            room(group_size, 16, capacity),
            room(group_size, *small.shape),
            room(group_size, tokens, dtype=f32),
            room(8, tokens, dtype=f32),
            room(tokens, width),
            room(tokens, width),
            room(2, tokens, width),
            room(3, tokens, width),
            room(4, 16, tokens),
            room(tokens, width, dtype=f32),
            room(tokens, width),
            room(heads, tokens, HEAD_DIM, dtype=f32),
            room(heads, tokens, HEAD_DIM, dtype=f32),
            room(tokens, 3 * head_width),
            room(8, tokens, dtype=f32),
            room(full, 3 * head_width),
            room(full, 3 * head_width),
            room(full, head_width),
            room(full, head_width),
            room(width, tokens),
            room(tensor_size, column_width, tokens),
            room(*small.shape, dtype=f32),
            room(group_size, *small.shape, dtype=f32),
            dma((6, group_size)),
            dma((16, group_size)),
            dma((3, 6, chunks + 1)),
            dma((2, tensor_size)),
            dma((18,)),
        ],
        compiler_params=pltpu.CompilerParams(
            collective_id=0, has_side_effects=True, vmem_limit_bytes=VMEM_BYTES
        ),
        name="layer",
    )(x, q, k, v, o, small, bias, ids, cot, w_in, w_out)


def on_device_general(
    block_input,
    attn_gain,
    query_weight,
    key_weight,
    value_weight,
    output_weight,
    bias_table,
    ffn_gain,
    router_weight,
    expert_in,
    expert_out,
    expert_ids,
    out_cotangent,
):
    tensor_size = lax.axis_size("tensor")
    group_size = lax.axis_size("dp")
    tensor_index = lax.axis_index("tensor")
    own_expert = lax.axis_index("dp")
    token_count, model_width = block_input.shape
    column_width = model_width // tensor_size
    column_start = tensor_index * column_width
    expert_count = group_size * expert_in.shape[0]
    capacity = tensor_size * max(1, 3 * token_count // (5 * expert_count))
    slot_rows = expert_count * capacity
    seq_count = token_count // SEQ_LEN
    head_local = bias_table.shape[0]
    head_width = head_local * HEAD_DIM
    block_rows = query_weight.shape[0]
    low = jnp.bfloat16

    def own_columns(matrix):
        return lax.dynamic_slice_in_dim(matrix, column_start, column_width, 1)

    packed = jnp.concatenate(
        [
            query_weight,
            key_weight,
            value_weight,
            output_weight,
            router_weight,
            attn_gain[:, None],
            ffn_gain[:, None],
        ],
        axis=1,
    )
    packed = lax.all_gather(packed, "dp", axis=0, tiled=True)

    labels = jnp.arange(expert_count, dtype=jnp.int32)
    flat_ids = expert_ids.reshape(-1)
    ids_onehot = (flat_ids[:, None] == labels[None, :]).astype(jnp.int32)
    pair_rows = lax.broadcasted_iota(jnp.int32, (2 * token_count, 2 * token_count), 0)
    pair_cols = lax.broadcasted_iota(jnp.int32, (2 * token_count, 2 * token_count), 1)
    before = (pair_cols < pair_rows).astype(low)
    earlier = dot(before, ids_onehot.astype(low)).astype(jnp.int32)
    slot_index = jnp.sum(earlier * ids_onehot, axis=1)
    places = (flat_ids * capacity + slot_index).reshape(token_count, 2)
    place_rows = jnp.arange(slot_rows, dtype=jnp.int32)
    at_first = places[:, 0][None, :] == place_rows[:, None]
    at_second = places[:, 1][None, :] == place_rows[:, None]
    map_first = at_first.astype(low)
    map_second = at_second.astype(low)
    map_both = (at_first | at_second).astype(low)

    ids_low = jnp.broadcast_to(expert_ids.astype(low)[:, :, None], (token_count, 2, LANES))
    cot_source = jnp.concatenate(
        [
            jnp.concatenate([out_cotangent, ids_low[:, 1]], axis=1),
            jnp.concatenate([out_cotangent, ids_low[:, 0]], axis=1),
        ],
        axis=0,
    )
    cot_parcel = dot(jnp.concatenate([map_first, map_second], axis=1), cot_source).astype(low)
    packed, cot_parcel = lax.optimization_barrier((packed, cot_parcel))
    cot_arrived = exchange(
        cot_parcel.reshape(expert_count, capacity, model_width + LANES)
    ).reshape(slot_rows, model_width + LANES)
    cot_rows = cot_arrived[:, :model_width].astype(jnp.float32)
    other_ids = cot_arrived[:, model_width].astype(jnp.int32)

    qkv_full = packed[:, : 3 * head_width]
    output_full = packed[:, 3 * head_width : 4 * head_width]
    at = 4 * head_width
    router_full = packed[:, at : at + expert_count]
    gain_one = packed[:, at + expert_count].astype(jnp.float32)
    gain_two = packed[:, at + expert_count + 1].astype(jnp.float32)
    inputs_f = block_input.astype(jnp.float32)
    scale_one = rms_scale(inputs_f)
    normed_one = (inputs_f * scale_one * gain_one).astype(low)
    qkv = dot(normed_one, qkv_full).astype(low)
    bucket_vec = bucket_vector_at(jnp.arange(SEQ_LEN, dtype=jnp.int32), NB)
    bucket_labels = jnp.arange(NB, dtype=jnp.int32)
    wrap = (SEQ_LEN - jnp.arange(SEQ_LEN, dtype=jnp.int32)) % SEQ_LEN
    wrapped_onehot = bucket_vector_at(wrap, NB)[None, :] == bucket_labels[:, None]
    wrapped = jnp.sum(
        jnp.where(wrapped_onehot[None], bias_table[:, :, None], 0.0), axis=1
    )
    context, probs = attend_forward(qkv, wrapped, seq_count, head_local)
    attn_part = dot(context, output_full, ((1,), (1,))).astype(low)
    attn_out = lax.psum(attn_part, "tensor").astype(jnp.float32)
    residual = inputs_f + attn_out
    scale_two = rms_scale(residual)
    normed_two = (residual * scale_two * gain_two).astype(low)

    logits = dot(normed_two, router_full)
    picked = (expert_ids[:, :, None] == labels[None, None, :]).astype(jnp.float32)
    chosen = jnp.sum(picked * logits[:, None, :], axis=2)
    first_gate = jax.nn.sigmoid(chosen[:, 0] - chosen[:, 1])
    second_gate = 1.0 - first_gate

    weight_in = expert_in[0]
    weight_out = expert_out[0]
    parcel = dot(map_both, normed_two).astype(low)
    expert_rows = exchange(parcel.reshape(expert_count, capacity, model_width)).reshape(
        slot_rows, model_width
    )
    pre_act = dot(expert_rows, weight_in)
    active, pullback = jax.vjp(jax.nn.gelu, pre_act)
    active = active.astype(low)
    owner_out = dot(active, weight_out)
    owner_logits = dot(expert_rows, router_full)
    own_logit = jnp.sum(
        jnp.where(labels[None, :] == own_expert, owner_logits, 0.0), axis=1
    )
    other_logit = jnp.sum(
        jnp.where(labels[None, :] == other_ids[:, None], owner_logits, 0.0), axis=1
    )
    row_gate = jax.nn.sigmoid(own_logit - other_logit)
    expert_drows = (row_gate[:, None] * cot_rows).astype(low)
    dpre = pullback(dot(expert_drows, weight_out, ((1,), (1,))))[0].astype(low)
    owner_back = dot(dpre, weight_in, ((1,), (1,))).astype(low)
    gate_part = jnp.sum(cot_rows * owner_out, axis=1, keepdims=True).astype(low)
    back_parcel = jnp.concatenate(
        [owner_back, jnp.broadcast_to(gate_part, (slot_rows, LANES))], axis=1
    )
    back_rows = exchange(
        back_parcel.reshape(group_size, capacity, model_width + LANES)
    ).reshape(slot_rows, model_width + LANES)
    out_rows = exchange(
        owner_out.astype(low).reshape(group_size, capacity, model_width)
    ).reshape(slot_rows, model_width)
    out_grad = dot(active, expert_drows, ((0,), (0,)))
    in_grad = dot(expert_rows, dpre, ((0,), (0,)))

    dnormed_part = dot(map_both, back_rows[:, :model_width], ((0,), (0,)))
    gate_diff_part = dot(map_first - map_second, back_rows[:, model_width:], ((0,), (0,)))
    gate_rows = -(-token_count // model_width)
    gate_line = jnp.pad(gate_diff_part[:, 0], (0, gate_rows * model_width - token_count))
    summed = lax.psum(
        jnp.concatenate(
            [dnormed_part, gate_line.reshape(gate_rows, model_width)], axis=0
        ).astype(low),
        "tensor",
    ).astype(jnp.float32)
    gate_diff = summed[token_count:].reshape(-1)[:token_count]
    mixture_part = first_gate[:, None] * dot(map_first, out_rows, ((0,), (0,)))
    mixture_part = mixture_part + second_gate[:, None] * dot(
        map_second, out_rows, ((0,), (0,))
    )
    mixture_parts = mixture_part.astype(low).reshape(token_count, tensor_size, column_width)
    mixture_parts = jnp.swapaxes(mixture_parts, 0, 1)

    dlogit = gate_diff * first_gate * second_gate
    signed = jnp.stack([dlogit, -dlogit], axis=1)
    dlogits = jnp.sum(picked * signed[:, :, None], axis=1).astype(low)
    router_term = dot(normed_two, dlogits, ((0,), (0,)))
    dnormed_two = summed[:token_count] + dot(dlogits, router_full, ((1,), (1,)))
    ffn_term = jnp.sum(dnormed_two * residual * scale_two, axis=0)
    cot_f = out_cotangent.astype(jnp.float32)
    dresidual = cot_f + norm_back(dnormed_two, residual, scale_two, gain_two)
    dres_low = dresidual.astype(low)
    mixture_parts, dres_low = lax.optimization_barrier((mixture_parts, dres_low))
    mixture_parts = lax.all_to_all(
        mixture_parts, "tensor", split_axis=0, concat_axis=0, tiled=True
    )

    output_term = dot(dres_low, context, ((0,), (0,)))
    dcontext = dot(dres_low, output_full).astype(low)
    dqkv, diagonal = attend_backward(qkv, probs, dcontext, seq_count, head_local)
    reverse_onehot = (bucket_vec[::-1][:, None] == bucket_labels[None, :]).astype(jnp.float32)
    bias_term = jnp.dot(
        jnp.sum(diagonal, axis=0),
        reverse_onehot,
        precision=lax.Precision.HIGHEST,
        preferred_element_type=jnp.float32,
    )
    dnormed_part = dot(dqkv, qkv_full, ((1,), (1,))).astype(low)
    dnormed_part, mixture_parts = lax.optimization_barrier((dnormed_part, mixture_parts))
    dnormed_one = lax.psum(dnormed_part, "tensor").astype(jnp.float32)
    qkv_term = dot(normed_one, dqkv, ((0,), (0,)))
    bias_count = bias_term.size
    bias_cols = -(-bias_count // block_rows)
    bias_block = jnp.pad(bias_term.reshape(-1), (0, bias_cols * block_rows - bias_count))
    bias_block = jnp.tile(bias_block.reshape(block_rows, bias_cols), (group_size, 1))
    terms = jnp.concatenate(
        [qkv_term, output_term, router_term, ffn_term[:, None], bias_block],
        axis=1,
    ).astype(low)
    term_width = terms.shape[1]
    arrived = exchange(terms.reshape(group_size, block_rows, term_width))
    arrived, dnormed_one = lax.optimization_barrier((arrived, dnormed_one))
    mixture = jnp.sum(mixture_parts.astype(jnp.float32), axis=0)
    block_output = (own_columns(residual) + mixture).astype(low)
    reduced = jnp.sum(arrived.astype(jnp.float32), axis=0)
    at = 4 * head_width
    grads = [reduced[:, k * head_width : (k + 1) * head_width] for k in range(4)]
    router_grad = reduced[:, at : at + expert_count]
    at = at + expert_count
    bias_grad = reduced[:, at + 1 :].reshape(-1)[:bias_count].reshape(bias_term.shape)
    attn_term = jnp.sum(dnormed_one * inputs_f * scale_one, axis=0)
    attn_gain_grad = jnp.sum(exchange(attn_term.reshape(group_size, block_rows)), axis=0)
    first_back = norm_back(dnormed_one, inputs_f, scale_one, gain_one)
    input_grad = own_columns(dresidual + first_back)
    return (
        block_output,
        input_grad,
        attn_gain_grad,
        grads[0],
        grads[1],
        grads[2],
        grads[3],
        bias_grad,
        reduced[:, at],
        router_grad,
        in_grad[None],
        out_grad[None],
    )


def on_device(
    block_input,
    attn_gain,
    query_weight,
    key_weight,
    value_weight,
    output_weight,
    bias_table,
    ffn_gain,
    router_weight,
    expert_in,
    expert_out,
    expert_ids,
    out_cotangent,
):
    tensor_size = lax.axis_size("tensor")
    group_size = lax.axis_size("dp")
    own = lax.axis_index("dp")
    token_count, model_width = block_input.shape
    block_rows = query_weight.shape[0]
    head_local = bias_table.shape[0]
    low = jnp.bfloat16
    capacity = tensor_size * max(1, 3 * token_count // (5 * group_size))
    capacity = -(-capacity // 16) * 16
    small = jnp.concatenate(
        [attn_gain[None, :], ffn_gain[None, :], jnp.zeros((6, block_rows), low), router_weight.T],
        axis=0,
    )
    small = lax.dynamic_update_slice(
        jnp.zeros((small.shape[0], model_width), low), small, (0, own * block_rows)
    )
    block_output, input_grad, qkv_grad, output_grad, sums, in_grad, out_grad = run_layer(
        group_size,
        tensor_size,
        capacity,
        block_input,
        query_weight,
        key_weight,
        value_weight,
        output_weight,
        small,
        bias_table,
        expert_ids.T,
        out_cotangent,
        expert_in[0],
        expert_out[0],
    )
    own_sums = lax.dynamic_slice_in_dim(sums, own * block_rows, block_rows, 1)
    return (
        block_output.T,
        input_grad.T,
        own_sums[1],
        qkv_grad[0],
        qkv_grad[1],
        qkv_grad[2],
        output_grad,
        sums[2 : 2 + head_local, :NB],
        own_sums[0],
        own_sums[8:].T,
        in_grad[None],
        out_grad[None],
    )


def choose(mesh):
    def run(*arrays):
        tokens, width = arrays[0].shape
        block_rows = arrays[2].shape[0]
        hidden = arrays[9].shape[2]
        group_size = mesh.shape["dp"]
        fits = (
            block_rows % 16 == 0
            and arrays[9].shape[0] == 1
            and mesh.shape["tensor"] == 4
            and group_size == 8
            and arrays[6].shape[0] <= 6
            and tokens == SEQ_LEN
            and hidden == width
            and width % 256 == 0
            and width % 64 == 0
        )
        return (on_device if fits else on_device_general)(*arrays)

    return run


def solution(mesh):
    placed = (
        P("dp", None),
        P("dp"),
        P("dp", "tensor"),
        P("dp", "tensor"),
        P("dp", "tensor"),
        P("dp", "tensor"),
        P("tensor", None),
        P("dp"),
        P("dp", None),
        P("dp", None, "tensor"),
        P("dp", "tensor", None),
        P("dp", None),
        P("dp", None),
    )
    return jax.shard_map(
        choose(mesh),
        mesh=mesh,
        in_specs=placed,
        out_specs=(
            P("dp", "tensor"),
            P("dp", "tensor"),
            P("dp"),
            P("dp", "tensor"),
            P("dp", "tensor"),
            P("dp", "tensor"),
            P("dp", "tensor"),
            P("tensor", None),
            P("dp"),
            P("dp", None),
            P("dp", None, "tensor"),
            P("dp", "tensor", None),
        ),
        check_vma=False,
    )
```

```python
import functools
import math

import jax
import jax.numpy as jnp
from jax import lax
from jax.experimental import pallas as pl
from jax.experimental.pallas import tpu as pltpu
from jax.sharding import PartitionSpec as P

HEAD_DIM = 64
NB = 32
SEQ_LEN = 512
LANES = 128
VMEM_BYTES = 63 * 1024 * 1024


EPSILON = 1e-06
MASKED = -1e30


def bucket_vector_at(steps_ids, bucket_count):
    exact_count = bucket_count // 2
    distant = jnp.full(steps_ids.shape, exact_count, jnp.int32)
    for level_index in range(1, bucket_count - exact_count):
        border = int(math.ceil(exact_count * 8.0 ** (level_index / (bucket_count - exact_count))))
        distant = distant + (steps_ids >= border).astype(jnp.int32)
    return jnp.where(steps_ids < exact_count, steps_ids, distant)


def norm_back(dnormed, row_values, row_scale, gain_row):
    inner_mean = jnp.mean(gain_row * dnormed * row_values, axis=-1, keepdims=True)
    return row_scale * (gain_row * dnormed - row_values * row_scale * row_scale * inner_mean)


def rms_scale(matrix):
    return lax.rsqrt(jnp.mean(matrix * matrix, axis=-1, keepdims=True) + EPSILON)


def dot(left, right, dims=((1,), (0,))):
    return lax.dot_general(left, right, (dims, ((), ())), preferred_element_type=jnp.float32)


def forward_kernel(qkv_ref, wrapped_ref, context_ref, probs_ref):
    length = qkv_ref.shape[0]
    heads = probs_ref.shape[0]
    width = heads * HEAD_DIM
    factor = HEAD_DIM ** (-0.5)
    rows = lax.broadcasted_iota(jnp.int32, (length, length), 0)
    cols = lax.broadcasted_iota(jnp.int32, (length, length), 1)
    causal = rows >= cols
    for h in range(heads):
        lo, hi = h * HEAD_DIM, (h + 1) * HEAD_DIM
        queries = qkv_ref[:, lo:hi]
        keys = qkv_ref[:, width + lo : width + hi]
        values = qkv_ref[:, 2 * width + lo : 2 * width + hi]
        bias = jnp.broadcast_to(wrapped_ref[h : h + 1, :], (length, length))
        bias = pltpu.roll(bias, 0, 1, stride=1, stride_axis=0)
        scores = jnp.where(causal, dot(queries, keys, ((1,), (1,))) * factor + bias, MASKED)
        row_max = jnp.max(scores, axis=-1, keepdims=True)
        row_total = jnp.sum(jnp.exp(scores - row_max), axis=-1, keepdims=True)
        probs = jnp.exp(scores - (row_max + jnp.log(row_total))).astype(jnp.bfloat16)
        probs_ref[h] = probs
        context_ref[:, lo:hi] = dot(probs, values).astype(jnp.bfloat16)


def backward_kernel(qkv_ref, probs_ref, dcontext_ref, dqkv_ref, diagonal_ref):
    length = qkv_ref.shape[0]
    heads = probs_ref.shape[0]
    width = heads * HEAD_DIM
    factor = HEAD_DIM ** (-0.5)
    rows = lax.broadcasted_iota(jnp.int32, (length, length), 0)
    cols = lax.broadcasted_iota(jnp.int32, (length, length), 1)
    flip = (rows + cols == length - 1).astype(jnp.float32).astype(jnp.bfloat16)
    for h in range(heads):
        lo, hi = h * HEAD_DIM, (h + 1) * HEAD_DIM
        queries = qkv_ref[:, lo:hi]
        keys = qkv_ref[:, width + lo : width + hi]
        values = qkv_ref[:, 2 * width + lo : 2 * width + hi]
        dcontext = dcontext_ref[:, lo:hi]
        probs = probs_ref[h]
        weights = probs.astype(jnp.float32)
        dweights = dot(dcontext, values, ((1,), (1,)))
        agreement = jnp.sum(weights * dweights, axis=-1, keepdims=True)
        dscores = (weights * (dweights - agreement)).astype(jnp.bfloat16)
        dqkv_ref[:, lo:hi] = (factor * dot(dscores, keys)).astype(jnp.bfloat16)
        dqkv_ref[:, width + lo : width + hi] = (
            factor * dot(dscores, queries, ((0,), (0,)))
        ).astype(jnp.bfloat16)
        dqkv_ref[:, 2 * width + lo : 2 * width + hi] = dot(
            probs, dcontext, ((0,), (0,))
        ).astype(jnp.bfloat16)
        skewed = pltpu.roll(dot(flip, dscores), 0, 1, stride=1, stride_axis=0)
        diagonal_ref[h : h + 1, :] = jnp.sum(skewed, axis=0, keepdims=True)


def attend_forward(qkv, wrapped, seq_count, heads):
    width = heads * HEAD_DIM
    return pl.pallas_call(
        forward_kernel,
        grid=(seq_count,),
        out_shape=(
            jax.ShapeDtypeStruct((seq_count * SEQ_LEN, width), jnp.bfloat16),
            jax.ShapeDtypeStruct((seq_count, heads, SEQ_LEN, SEQ_LEN), jnp.bfloat16),
        ),
        in_specs=[
            pl.BlockSpec((SEQ_LEN, 3 * width), lambda s: (s, 0)),
            pl.BlockSpec((heads, SEQ_LEN), lambda s: (0, 0)),
        ],
        out_specs=(
            pl.BlockSpec((SEQ_LEN, width), lambda s: (s, 0)),
            pl.BlockSpec((None, heads, SEQ_LEN, SEQ_LEN), lambda s: (s, 0, 0, 0)),
        ),
        name="attend_forward",
    )(qkv, wrapped)


def attend_backward(qkv, probs, dcontext, seq_count, heads):
    width = heads * HEAD_DIM
    return pl.pallas_call(
        backward_kernel,
        grid=(seq_count,),
        out_shape=(
            jax.ShapeDtypeStruct((seq_count * SEQ_LEN, 3 * width), jnp.bfloat16),
            jax.ShapeDtypeStruct((seq_count, heads, SEQ_LEN), jnp.float32),
        ),
        in_specs=[
            pl.BlockSpec((SEQ_LEN, 3 * width), lambda s: (s, 0)),
            pl.BlockSpec((None, heads, SEQ_LEN, SEQ_LEN), lambda s: (s, 0, 0, 0)),
            pl.BlockSpec((SEQ_LEN, width), lambda s: (s, 0)),
        ],
        out_specs=(
            pl.BlockSpec((SEQ_LEN, 3 * width), lambda s: (s, 0)),
            pl.BlockSpec((None, heads, SEQ_LEN), lambda s: (s, 0, 0)),
        ),
        name="attend_backward",
    )(qkv, probs, dcontext)


def exchange(parcel):
    return lax.all_to_all(parcel, "dp", split_axis=0, concat_axis=0, tiled=True)


def remote(src, dst, send_sem, recv_sem, axis, index):
    return pltpu.make_async_remote_copy(
        src_ref=src,
        dst_ref=dst,
        send_sem=send_sem,
        recv_sem=recv_sem,
        device_id={axis: index},
        device_id_type=pl.DeviceIdType.MESH,
    )


def rows_at(index, count):
    return pl.ds(pl.multiple_of(index * count, count), count)


def gelu_both(u):
    slope = math.sqrt(2.0 / math.pi)
    cubic = 0.044715
    square = u * u
    t = jnp.tanh(slope * u * (1.0 + cubic * square))
    half = 0.5 + 0.5 * t
    value = u * half
    grad = half + 0.5 * u * (1.0 - t * t) * (slope * (1.0 + 3.0 * cubic * square))
    return value, grad


def layer_kernel(
    group_size,
    tensor_size,
    x_hbm,
    q_hbm,
    k_hbm,
    v_hbm,
    o_hbm,
    small_hbm,
    bias_hbm,
    ids_hbm,
    cot_hbm,
    win_hbm,
    wout_hbm,
    block_hbm_out,
    input_hbm_out,
    qkv_hbm_out,
    wo_hbm_out,
    sums_hbm_out,
    late_hbm_out,
    in_grad_hbm,
    out_grad_hbm,
    wqkv_ref,
    wo_ref,
    gains_ref,
    qkv_ref,
    probs_ref,
    context_ref,
    normed_one_ref,
    normed_ref,
    residual_ref,
    residual_t_ref,
    both_ref,
    signed_ref,
    gated_ref,
    rows_ref,
    cots_ref,
    win_ref,
    wout_ref,
    active_ref,
    drows_ref,
    dpre_ref,
    grad_ref,
    send_ref,
    cot_send_ref,
    back_send_ref,
    back_ref,
    out_send_ref,
    out_ref,
    gate_send_ref,
    gate_ref,
    small_buf,
    code_ref,
    gates_ref,
    part_ref,
    near_ref,
    middle_ref,
    total_ref,
    gate_line_ref,
    dres_ref,
    dres_low_ref,
    dkeys_ref,
    dvalues_ref,
    dqkv_ref,
    diagonal_ref,
    terms_send_ref,
    terms_ref,
    oterms_send_ref,
    oterms_ref,
    mix_send_ref,
    mix_ref,
    sums_send_ref,
    sums_ref,
    late_send_ref,
    late_ref,
    x_ref,
    q_ref,
    k_ref,
    v_ref,
    o_ref,
    small_ref,
    bias_ref,
    ids_ref,
    cot_ref,
    block_out,
    input_out,
    qkv_out,
    wo_out,
    sums_out,
    late_out,
    load_sems,
    store_sems,
    w_sems,
    a2a_sems,
    line_sems,
    z_sems,
    local_sems,
):
    me = lax.axis_index("dp")
    level = lax.axis_index("tensor")
    token_count, model_width = x_ref.shape
    experts = group_size
    capacity = rows_ref.shape[0] // group_size
    block_rows, head_width = q_ref.shape
    heads = bias_ref.shape[0]
    column_width = model_width // tensor_size
    low = jnp.bfloat16
    f32 = jnp.float32
    near = level + 1 - 2 * lax.rem(level, 2)
    across = tensor_size - 1 - level
    is_end = jnp.logical_or(level == 0, level == tensor_size - 1)
    is_middle = jnp.logical_not(is_end)
    chip = me // 2
    core = lax.rem(me, 2)
    chips = group_size // 2
    chunk = LANES
    chunks = token_count // chunk
    factor = HEAD_DIM ** (-0.5)

    def peer_of(j):
        other_chip = lax.rem(chip - j // 2 + chips, chips)
        return 2 * other_chip + lax.rem(core + j, 2)

    def each_peer(body):
        def step(j, carry):
            body(peer_of(j))
            return carry

        lax.fori_loop(1, group_size, step, 0)

    def load_in():
        return pltpu.make_async_copy(win_hbm, win_ref, local_sems.at[0])

    def load_out():
        return pltpu.make_async_copy(wout_hbm, wout_ref, local_sems.at[1])

    def loads(first, last):
        pairs = [
            (q_hbm, q_ref),
            (k_hbm, k_ref),
            (v_hbm, v_ref),
            (o_hbm, o_ref),
            (small_hbm, small_ref),
            (ids_hbm, ids_ref),
            (bias_hbm, bias_ref),
            (cot_hbm, cot_ref),
            (x_hbm, x_ref),
        ]
        return [
            pltpu.make_async_copy(src, dst, load_sems.at[place])
            for place, (src, dst) in enumerate(pairs)
            if first <= place < last
        ]

    for copy in loads(0, 9):
        copy.start()
    load_in().start()
    load_out().start()

    def stores():
        pairs = [
            (input_out, input_hbm_out),
            (qkv_out, qkv_hbm_out),
            (wo_out, wo_hbm_out),
            (block_out, block_hbm_out),
            (sums_out, sums_hbm_out),
            (late_out, late_hbm_out),
        ]
        return [
            pltpu.make_async_copy(src, dst, store_sems.at[place])
            for place, (src, dst) in enumerate(pairs)
        ]

    barrier = pltpu.get_barrier_semaphore()
    each_peer(
        lambda peer: pl.semaphore_signal(
            barrier, inc=1, device_id={"dp": peer}, device_id_type=pl.DeviceIdType.MESH
        )
    )

    def greet(step, carry):
        other = lax.rem(level + step, tensor_size)
        pl.semaphore_signal(
            barrier, inc=1, device_id={"tensor": other}, device_id_type=pl.DeviceIdType.MESH
        )
        return carry

    lax.fori_loop(1, tensor_size, greet, 0)
    mine = rows_at(me, block_rows)
    for copy in loads(0, 5):
        copy.wait()
    wqkv_ref[mine, :] = jnp.concatenate([q_ref[...], k_ref[...], v_ref[...]], axis=1)
    wo_ref[mine, :] = o_ref[...]
    small_buf[me] = small_ref[...]

    pl.semaphore_wait(barrier, group_size + tensor_size - 2)

    sibling = 2 * chip + 1 - core

    def weight_copies(peer, source, slot):
        block = rows_at(source, block_rows)
        return [
            remote(wqkv_ref.at[block], wqkv_ref.at[block], w_sems.at[0, slot], w_sems.at[1, source], "dp", peer),
            remote(wo_ref.at[block], wo_ref.at[block], w_sems.at[2, slot], w_sems.at[3, source], "dp", peer),
            remote(small_buf.at[source], small_buf.at[source], w_sems.at[4, slot], w_sems.at[5, source], "dp", peer),
        ]

    def each_chip(body):
        def step(j, carry):
            body(lax.rem(chip + j, chips))
            return carry

        lax.fori_loop(1, chips, step, 0)

    def start_all(copies):
        for copy in copies:
            copy.start()

    def recv_all(copies):
        for copy in copies:
            copy.wait_recv()

    def sent_all(copies):
        for copy in copies:
            copy.wait_send()

    def send_weights(other):
        peer = 2 * other + core
        start_all(weight_copies(peer, me, peer))

    each_chip(send_weights)
    start_all(weight_copies(sibling, me, sibling))

    def block_copy(kind, src, dst, peer, source, count):
        return remote(
            src.at[rows_at(peer, count)],
            dst.at[rows_at(source, count)],
            a2a_sems.at[2 * kind, peer],
            a2a_sems.at[2 * kind + 1, source],
            "dp",
            peer,
        )

    def cot_copy(peer, source):
        return block_copy(0, cot_send_ref, cots_ref, peer, source, capacity)

    def row_copy(peer, source):
        return block_copy(1, send_ref, rows_ref, peer, source, capacity)

    def back_copy(peer, source):
        return block_copy(2, back_send_ref, back_ref, peer, source, capacity)

    def out_copy(peer, source):
        return block_copy(3, out_send_ref, out_ref, peer, source, capacity)

    def term_copies(peer, source):
        return [
            block_copy(4, terms_send_ref, terms_ref, peer, source, block_rows),
            block_copy(5, oterms_send_ref, oterms_ref, peer, source, block_rows),
        ]

    def gate_copy(peer, source):
        return remote(
            gate_send_ref.at[peer], gate_ref.at[source], a2a_sems.at[12, peer], a2a_sems.at[13, source], "dp", peer
        )

    def late_copy(peer, source):
        return remote(
            late_send_ref, late_ref.at[source], a2a_sems.at[16, peer], a2a_sems.at[17, source], "dp", peer
        )

    def sums_copy(peer, source):
        return remote(
            sums_send_ref, sums_ref.at[source], a2a_sems.at[14, peer], a2a_sems.at[15, source], "dp", peer
        )

    for copy in loads(5, 9):
        copy.wait()
    ids_first = ids_ref[0:1, :]
    ids_second = ids_ref[1:2, :]
    labels = lax.broadcasted_iota(jnp.int32, (experts, token_count), 0)
    member = jnp.logical_or(labels == ids_first, labels == ids_second)
    tokens_r = lax.broadcasted_iota(jnp.int32, (token_count, token_count), 0)
    tokens_c = lax.broadcasted_iota(jnp.int32, (token_count, token_count), 1)
    upper = jnp.where(tokens_r < tokens_c, 1.0, 0.0).astype(low)
    counted = dot(jnp.where(member, 1.0, 0.0).astype(low), upper)
    code_ref[...] = jnp.where(member, counted, -1.0)
    slots = lax.broadcasted_iota(jnp.int32, (capacity, token_count), 0).astype(f32)
    id_total = jnp.broadcast_to((ids_first + ids_second).astype(f32), (LANES, token_count)).astype(low)

    def make_maps(expert, carry):
        block = rows_at(expert, capacity)
        hit = slots == code_ref[pl.ds(expert, 1), :]
        sign = jnp.where(ids_first == expert, 1.0, -1.0)
        both = jnp.where(hit, 1.0, 0.0).astype(low)
        both_ref[block, :] = both
        signed_ref[block, :] = jnp.where(hit, sign, 0.0).astype(low)
        cot_send_ref[block, :model_width] = dot(both, cot_ref[...]).astype(low)
        cot_send_ref[block, model_width:] = dot(both, id_total, ((1,), (1,))).astype(low)
        return carry

    lax.fori_loop(0, experts, make_maps, 0)

    inputs_f = x_ref[...].astype(f32)
    scaled = inputs_f * rms_scale(inputs_f)

    lane = lax.broadcasted_iota(jnp.int32, (heads, token_count), 1)
    wrap_bucket = bucket_vector_at(jnp.where(lane == 0, 0, token_count - lane), NB)
    wrapped = jnp.zeros((heads, token_count), f32)
    for b in range(NB):
        wrapped = jnp.where(wrap_bucket == b, bias_ref[:, b : b + 1], wrapped)

    def pass_on(other):
        source = 2 * other + core
        recv_all(weight_copies(sibling, source, source))
        start_all(weight_copies(sibling, source, 2 * other + 1 - core))

    def take_passed(other):
        source = 2 * other + 1 - core
        recv_all(weight_copies(sibling, source, source))

    each_chip(pass_on)
    recv_all(weight_copies(sibling, sibling, sibling))
    each_chip(take_passed)
    each_peer(lambda peer: cot_copy(peer, me).start())

    gains = jnp.zeros(gains_ref.shape, f32)
    for source in range(group_size):
        slab = jnp.concatenate(
            [small_buf[source].astype(f32), jnp.zeros((gains.shape[0], model_width - LANES), f32)], axis=1
        )
        gains = gains + (pltpu.roll(slab, source * block_rows, 1) if source else slab)
    gains_ref[...] = gains
    gain_one = gains_ref[0:1, :]
    gain_two = gains_ref[1:2, :]
    normed_one_ref[...] = (scaled * gain_one).astype(low)
    qkv_ref[...] = dot(normed_one_ref[...], wqkv_ref[...]).astype(low)

    def at_chunk(c):
        return slice(c * chunk, (c + 1) * chunk)

    def line_up(r, c):
        if c is None:
            src, dst, c = gate_line_ref.at[0], gate_line_ref.at[1], chunks
        else:
            src, dst = part_ref.at[at_chunk(c)], near_ref.at[at_chunk(c)]
        return remote(src, dst, line_sems.at[r, 0, c], line_sems.at[r, 1, c], "tensor", near)

    def line_over(r, c):
        if c is None:
            src, dst, c = gate_line_ref.at[0], gate_line_ref.at[2], chunks
        else:
            src, dst = part_ref.at[at_chunk(c)], middle_ref.at[r % 2, at_chunk(c)]
        return remote(src, dst, line_sems.at[r, 2, c], line_sems.at[r, 3, c], "tensor", across)

    def line_down(r, c):
        if c is None:
            src = dst = gate_line_ref.at[3]
            c = chunks
        else:
            src = dst = total_ref.at[r, at_chunk(c)]
        return remote(src, dst, line_sems.at[r, 4, c], line_sems.at[r, 5, c], "tensor", near)

    def line_start(r, c):
        @pl.when(is_end)
        def _():
            line_up(r, c).start()

    def line_first(r, c):
        @pl.when(is_middle)
        def _():
            line_up(r, c).wait_recv()
            if c is None:
                gate_line_ref[0] = (gate_line_ref[0].astype(f32) + gate_line_ref[1].astype(f32)).astype(low)
            else:
                block = at_chunk(c)
                part_ref[block, :] = (part_ref[block, :].astype(f32) + near_ref[block, :].astype(f32)).astype(low)
            line_over(r, c).start()

    def line_second(r, c):
        @pl.when(is_middle)
        def _():
            line_over(r, c).wait_recv()
            if c is None:
                gate_line_ref[3] = (gate_line_ref[0].astype(f32) + gate_line_ref[2].astype(f32)).astype(low)
            else:
                block = at_chunk(c)
                total_ref[r, block, :] = (
                    part_ref[block, :].astype(f32) + middle_ref[r % 2, block, :].astype(f32)
                ).astype(low)
            line_down(r, c).start()

    def line_take(r, c):
        @pl.when(is_end)
        def _():
            line_down(r, c).wait_recv()

    def line_drain(r, c):
        @pl.when(is_end)
        def _():
            line_up(r, c).wait_send()

        @pl.when(is_middle)
        def _():
            line_over(r, c).wait_send()
            line_down(r, c).wait_send()

    for c in range(chunks):
        lo, hi = c * chunk, (c + 1) * chunk
        causal = lax.broadcasted_iota(jnp.int32, (chunk, hi), 0) + lo >= (
            lax.broadcasted_iota(jnp.int32, (chunk, hi), 1)
        )
        pieces = []
        for h in range(heads):
            at = h * HEAD_DIM
            queries = qkv_ref[lo:hi, at : at + HEAD_DIM]
            keys = qkv_ref[0:hi, head_width + at : head_width + at + HEAD_DIM]
            values = qkv_ref[0:hi, 2 * head_width + at : 2 * head_width + at + HEAD_DIM]
            bias = jnp.broadcast_to(wrapped[h : h + 1, :], (chunk, token_count))
            bias = pltpu.roll(bias, lo, 1, stride=1, stride_axis=0)[:, :hi]
            scores = jnp.where(causal, dot(queries, keys, ((1,), (1,))) * factor + bias, MASKED)
            row_max = jnp.max(scores, axis=-1, keepdims=True)
            grown = jnp.exp(scores - row_max)
            total = jnp.sum(grown, axis=-1, keepdims=True)
            probs = (grown * (1.0 / total)).astype(low)
            probs_ref[h, lo:hi, 0:hi] = probs
            pieces.append(dot(probs, values).astype(low))
        context = jnp.concatenate(pieces, axis=1)
        context_ref[lo:hi, :] = context
        part_ref[lo:hi, :] = dot(context, wo_ref[...], ((1,), (1,))).astype(low)
        line_start(0, c)
        if c >= 1:
            line_first(0, c - 1)
        if c >= 2:
            line_second(0, c - 2)
    line_first(0, chunks - 1)
    line_second(0, chunks - 2)
    line_second(0, chunks - 1)

    for c in range(chunks):
        block = at_chunk(c)
        line_take(0, c)
        residual = x_ref[block, :].astype(f32) + total_ref[0, block, :].astype(f32)
        residual_ref[block, :] = residual
        normed_ref[block, :] = (residual * rms_scale(residual) * gain_two).astype(low)

    def send_rows(peer):
        block = rows_at(peer, capacity)
        send_ref[block, :] = dot(both_ref[block, :], normed_ref[...]).astype(low)
        row_copy(peer, me).start()

    each_peer(send_rows)
    own = rows_at(me, capacity)
    rows_ref[own, :] = dot(both_ref[own, :], normed_ref[...]).astype(low)
    cots_ref[own, :] = cot_send_ref[own, :]

    gains_low = gains_ref[...].astype(low)
    logits = dot(gains_low, normed_ref[...], ((1,), (1,)))
    label_rows = lax.broadcasted_iota(jnp.int32, logits.shape, 0) - 8
    chosen_first = jnp.sum(jnp.where(label_rows == ids_first, logits, 0.0), axis=0, keepdims=True)
    chosen_second = jnp.sum(jnp.where(label_rows == ids_second, logits, 0.0), axis=0, keepdims=True)
    gate_first = jax.nn.sigmoid(chosen_first - chosen_second)
    gate_second = 1.0 - gate_first
    gates_ref[0:1, :] = gate_first
    gates_ref[1:2, :] = gate_second

    def make_gated(expert, carry):
        block = rows_at(expert, capacity)
        sign = signed_ref[block, :].astype(f32)
        gated_ref[block, :] = jnp.where(sign > 0, gate_first, jnp.where(sign < 0, gate_second, 0.0)).astype(low)
        return carry

    lax.fori_loop(0, experts, make_gated, 0)
    for z in range(tensor_size):

        @pl.when(level == z)
        def _():
            residual_t_ref[...] = jnp.transpose(residual_ref[:, z * column_width : (z + 1) * column_width])

    load_in().wait()
    load_out().wait()

    pair = 2 * capacity
    ones = jnp.ones((16, model_width), low)

    def expert_step(step, carry):
        other = lax.rem(chip + step, chips)
        block = rows_at(other, pair)
        for c in range(2):
            source = 2 * other + c

            @pl.when(source != me)
            def _():
                cot_copy(source, source).wait_recv()
                row_copy(source, source).wait_recv()

        rows = rows_ref[block, :]
        value, slope = gelu_both(dot(rows, win_ref[...]))
        active = value.astype(low)
        active_ref[block, :] = active
        owner_logits = dot(rows, gains_low, ((1,), (1,)))
        columns = lax.broadcasted_iota(jnp.int32, owner_logits.shape, 1) - 8
        other_ids = cots_ref[block, model_width : model_width + 1].astype(f32).astype(jnp.int32) - me
        own_logit = jnp.sum(jnp.where(columns == me, owner_logits, 0.0), axis=1, keepdims=True)
        other_logit = jnp.sum(jnp.where(columns == other_ids, owner_logits, 0.0), axis=1, keepdims=True)
        row_gate = jax.nn.sigmoid(own_logit - other_logit)
        cot = cots_ref[block, :model_width].astype(f32)
        drows = (row_gate * cot).astype(low)
        drows_ref[block, :] = drows
        dpre = (dot(drows, wout_ref[...], ((1,), (1,))) * slope).astype(low)
        dpre_ref[block, :] = dpre
        back_send_ref[block, :] = dot(dpre, win_ref[...], ((1,), (1,))).astype(low)
        for c in range(2):
            source = 2 * other + c

            @pl.when(source != me)
            def _():
                back_copy(source, me).start()

        owner_out = dot(active, wout_ref[...])
        out_send_ref[block, :] = owner_out.astype(low)
        agree = (cot * owner_out).astype(low)
        for c in range(2):
            source = 2 * other + c
            gate_send_ref[source] = dot(ones, agree[c * capacity : (c + 1) * capacity, :], ((1,), (1,))).astype(low)

            @pl.when(source != me)
            def _():
                gate_copy(source, me).start()

        return carry

    lax.fori_loop(0, chips, expert_step, 0)
    back_ref[own, :] = back_send_ref[own, :]
    out_ref[own, :] = out_send_ref[own, :]
    gate_ref[me] = gate_send_ref[me]

    def grad_out(which, part):
        target = (out_grad_hbm, in_grad_hbm)[which]
        block = slice(part * 256, (part + 1) * 256)
        return pltpu.make_async_copy(grad_ref.at[which, block], target.at[block], local_sems.at[2 + which * 8 + part])

    parts = win_ref.shape[0] // 256
    for part in range(parts):
        block = slice(part * 256, (part + 1) * 256)
        grad_ref[0, block, :] = dot(active_ref[:, block], drows_ref[...], ((0,), (0,)))
        grad_out(0, part).start()
        grad_ref[1, block, :] = dot(rows_ref[:, block], dpre_ref[...], ((0,), (0,)))
        grad_out(1, part).start()

    each_peer(lambda source: gate_copy(source, source).wait_recv())
    each_peer(lambda source: back_copy(source, source).wait_recv())
    each_peer(lambda peer: out_copy(peer, me).start())
    gate_line = dot(gate_ref[0], signed_ref[0:capacity, :])
    for e in range(1, experts):
        gate_line = gate_line + dot(gate_ref[e], signed_ref[e * capacity : (e + 1) * capacity, :])
    gate_line_ref[0] = gate_line.astype(low)
    line_start(1, None)
    order = list(range(chunks))[::-1]
    queue = [None] + order
    for place, c in enumerate(queue):
        if c is not None:
            block = at_chunk(c)
            line_drain(0, c)
            part_ref[block, :] = dot(both_ref[:, block], back_ref[...], ((0,), (0,))).astype(low)
            line_start(1, c)
        if place >= 1:
            line_first(1, queue[place - 1])
        if place >= 2:
            line_second(1, queue[place - 2])
    line_first(1, queue[-1])
    line_second(1, queue[-2])
    line_second(1, queue[-1])

    each_peer(lambda source: out_copy(source, source).wait_recv())
    for part in range(model_width // 256):
        block = slice(part * 256, (part + 1) * 256)
        mix_send_ref[block, :] = dot(out_ref[:, block], gated_ref[...], ((0,), (0,))).astype(low)

    def mix_copy(target, source):
        return remote(
            mix_send_ref.at[rows_at(target, column_width)],
            mix_ref.at[source],
            z_sems.at[0, target],
            z_sems.at[1, source],
            "tensor",
            target,
        )

    def each_level(body):
        def step(j, carry):
            body(lax.rem(level + j, tensor_size))
            return carry

        lax.fori_loop(1, tensor_size, step, 0)

    each_level(lambda target: mix_copy(target, level).start())
    mix_ref[level] = mix_send_ref[rows_at(level, column_width), :]

    line_take(1, None)
    gate_diff = gate_line_ref[3, 0:1, :].astype(f32)
    dlogit = gate_diff * gates_ref[0:1, :] * gates_ref[1:2, :]
    dlogits = jnp.where(
        label_rows == ids_first, dlogit, jnp.where(label_rows == ids_second, -dlogit, 0.0)
    ).astype(low)
    sums_send_ref[...] = dot(dlogits, normed_ref[...])

    def backward_chunk(c, ffn_term):
        lo, hi = c * chunk, (c + 1) * chunk
        block = at_chunk(c)
        line_take(1, c)
        dnormed = total_ref[1, block, :].astype(f32) + dot(dlogits[:, block], gains_low, ((0,), (0,)))
        residual = residual_ref[block, :]
        scale_two = rms_scale(residual)
        ffn_term = ffn_term + jnp.sum(dnormed * residual * scale_two, axis=0, keepdims=True)
        dres = cot_ref[block, :].astype(f32) + norm_back(dnormed, residual, scale_two, gain_two)
        dres_ref[block, :] = dres
        dres_low = dres.astype(low)
        dres_low_ref[block, :] = dres_low
        dcontext = dot(dres_low, wo_ref[...]).astype(low)
        flip = (
            lax.broadcasted_iota(jnp.int32, (chunk, chunk), 0)
            + lax.broadcasted_iota(jnp.int32, (chunk, chunk), 1)
            == chunk - 1
        )
        flip = jnp.where(flip, 1.0, 0.0).astype(low)
        first, second, third = [], [], []
        for h in range(heads):
            at = h * HEAD_DIM
            queries = qkv_ref[lo:hi, at : at + HEAD_DIM]
            keys = qkv_ref[0:hi, head_width + at : head_width + at + HEAD_DIM]
            values = qkv_ref[0:hi, 2 * head_width + at : 2 * head_width + at + HEAD_DIM]
            dctx = dcontext[:, at : at + HEAD_DIM]
            probs = probs_ref[h, lo:hi, 0:hi]
            weights = probs.astype(f32)
            dweights = dot(dctx, values, ((1,), (1,)))
            agreement = jnp.sum(weights * dweights, axis=-1, keepdims=True)
            dscores = (weights * (dweights - agreement)).astype(low)
            first.append((factor * dot(dscores, keys)).astype(low))
            dkeys = dot(dscores, queries, ((0,), (0,)))
            dvalues = dot(probs, dctx, ((0,), (0,)))
            if c < chunks - 1:
                dkeys = dkeys + dkeys_ref[h, 0:hi, :]
                dvalues = dvalues + dvalues_ref[h, 0:hi, :]
            if lo:
                dkeys_ref[h, 0:lo, :] = dkeys[0:lo]
                dvalues_ref[h, 0:lo, :] = dvalues[0:lo]
            second.append((factor * dkeys[lo:hi]).astype(low))
            third.append(dvalues[lo:hi].astype(low))
            flipped = dot(flip, dscores)
            if hi < token_count:
                flipped = jnp.concatenate([flipped, jnp.zeros((chunk, token_count - hi), f32)], axis=1)
            skewed = pltpu.roll(flipped, token_count - (hi - 1), 1, stride=1, stride_axis=0)
            line = jnp.sum(skewed, axis=0, keepdims=True)
            if c < chunks - 1:
                line = line + diagonal_ref[h : h + 1, :]
            diagonal_ref[h : h + 1, :] = line
        dqkv = jnp.concatenate(first + second + third, axis=1)
        dqkv_ref[block, :] = dqkv
        line_drain(1, c)
        part_ref[block, :] = dot(dqkv, wqkv_ref[...], ((1,), (1,))).astype(low)
        line_start(2, c)
        return ffn_term

    ffn_term = jnp.zeros((1, model_width), f32)
    for place, c in enumerate(order):
        ffn_term = backward_chunk(c, ffn_term)
        if place >= 1:
            line_first(2, order[place - 1])
        if place >= 2:
            line_second(2, order[place - 2])

    for part in range(model_width // 256):
        block = slice(part * 256, (part + 1) * 256)
        terms_send_ref[block, :] = dot(normed_one_ref[:, block], dqkv_ref[...], ((0,), (0,))).astype(low)
        oterms_send_ref[block, :] = dot(dres_low_ref[:, block], context_ref[...], ((0,), (0,))).astype(low)
        if part == 0:
            line_first(2, order[-1])
            line_second(2, order[-2])
        if part == 1:
            line_second(2, order[-1])
    each_peer(lambda peer: start_all(term_copies(peer, me)))
    terms_ref[mine, :] = terms_send_ref[mine, :]
    oterms_ref[mine, :] = oterms_send_ref[mine, :]

    sums_send_ref[0:1, :] = ffn_term
    diagonal = diagonal_ref[0:heads, :]
    lanes = lax.broadcasted_iota(jnp.int32, (heads, model_width), 1)
    bias_rows = jnp.zeros((heads, model_width), f32)
    for b in range(NB):
        bucket_total = jnp.sum(jnp.where(wrap_bucket == b, diagonal, 0.0), axis=1, keepdims=True)
        bias_rows = jnp.where(lanes == b, bucket_total, bias_rows)
    sums_send_ref[2 : 2 + heads, :] = bias_rows
    each_peer(lambda peer: sums_copy(peer, me).start())
    sums_ref[me] = sums_send_ref[...]

    attn_term = jnp.zeros((1, model_width), f32)
    for c in order:
        block = at_chunk(c)
        line_take(2, c)
        dnormed = total_ref[2, block, :].astype(f32)
        values = x_ref[block, :].astype(f32)
        scale_one = rms_scale(values)
        attn_term = attn_term + jnp.sum(dnormed * values * scale_one, axis=0, keepdims=True)
        dres_ref[block, :] = dres_ref[block, :] + norm_back(dnormed, values, scale_one, gain_one)

    late_send_ref[...] = jnp.broadcast_to(attn_term, late_send_ref.shape)
    each_peer(lambda peer: late_copy(peer, me).start())
    late_ref[me] = late_send_ref[...]

    for z in range(tensor_size):

        @pl.when(level == z)
        def _():
            input_out[...] = jnp.transpose(dres_ref[:, z * column_width : (z + 1) * column_width])

    stores()[0].start()
    each_peer(lambda source: recv_all(term_copies(source, source)))
    reduced = terms_ref[0:block_rows, :].astype(f32)
    oreduced = oterms_ref[0:block_rows, :].astype(f32)
    for source in range(1, group_size):
        block = slice(source * block_rows, (source + 1) * block_rows)
        reduced = reduced + terms_ref[block, :].astype(f32)
        oreduced = oreduced + oterms_ref[block, :].astype(f32)
    for k in range(3):
        qkv_out[k] = reduced[:, k * head_width : (k + 1) * head_width]
    wo_out[...] = oreduced
    stores()[1].start()
    stores()[2].start()

    each_level(lambda source: mix_copy(source, source).wait_recv())
    mixture = mix_ref[0].astype(f32)
    for z in range(1, tensor_size):
        mixture = mixture + mix_ref[z].astype(f32)
    block_out[...] = (residual_t_ref[...] + mixture).astype(low)
    stores()[3].start()

    each_peer(lambda source: sums_copy(source, source).wait_recv())
    sums = sums_ref[0]
    for source in range(1, group_size):
        sums = sums + sums_ref[source]
    sums_out[...] = sums
    stores()[4].start()
    each_peer(lambda source: late_copy(source, source).wait_recv())
    late = late_ref[0]
    for source in range(1, group_size):
        late = late + late_ref[source]
    late_out[...] = late
    stores()[5].start()

    def drain(peer):
        late_copy(peer, me).wait_send()
        sent_all(weight_copies(peer, me, peer))
        cot_copy(peer, me).wait_send()
        row_copy(peer, me).wait_send()
        back_copy(peer, me).wait_send()
        gate_copy(peer, me).wait_send()
        out_copy(peer, me).wait_send()
        sent_all(term_copies(peer, me))
        sums_copy(peer, me).wait_send()

    each_peer(drain)
    each_level(lambda target: mix_copy(target, level).wait_send())
    line_drain(1, None)
    for c in order:
        line_drain(2, c)
    for part in range(parts):
        grad_out(0, part).wait()
        grad_out(1, part).wait()
    for copy in stores():
        copy.wait()


def run_layer(group_size, tensor_size, capacity, x, q, k, v, o, small, bias, ids, cot, w_in, w_out):
    tokens, width = x.shape
    block_rows, head_width = q.shape
    heads = bias.shape[0]
    hidden = w_in.shape[1]
    slots = group_size * capacity
    low = jnp.bfloat16
    f32 = jnp.float32
    full = group_size * block_rows
    chunks = tokens // LANES
    column_width = width // tensor_size

    def shape(dims, dtype=low):
        return jax.ShapeDtypeStruct(dims, dtype)

    def room(*dims, dtype=low):
        return pltpu.VMEM(dims, dtype)

    hbm = pl.BlockSpec(memory_space=pl.ANY)
    dma = pltpu.SemaphoreType.DMA
    return pl.pallas_call(
        functools.partial(layer_kernel, group_size, tensor_size),
        out_shape=(
            shape((column_width, tokens)),
            shape((column_width, tokens), f32),
            shape((3, block_rows, head_width), f32),
            shape((block_rows, head_width), f32),
            shape((small.shape[0], width), f32),
            shape((8, width), f32),
            shape((width, hidden), f32),
            shape((hidden, width), f32),
        ),
        in_specs=[hbm] * 11,
        out_specs=(hbm,) * 8,
        scratch_shapes=[
            room(full, 3 * head_width),
            room(full, head_width),
            room(small.shape[0], width, dtype=f32),
            room(tokens, 3 * head_width),
            room(heads, tokens, tokens),
            room(tokens, head_width),
            room(tokens, width),
            room(tokens, width),
            room(tokens, width, dtype=f32),
            room(column_width, tokens, dtype=f32),
            room(slots, tokens),
            room(slots, tokens),
            room(slots, tokens),
            room(slots, width),
            room(slots, width + LANES),
            room(width, hidden),
            room(hidden, width),
            room(slots, hidden),
            room(slots, width),
            room(slots, hidden),
            room(2, width, width, dtype=f32),
            room(slots, width),
            room(slots, width + LANES),
            room(slots, width),
            room(slots, width),
            room(slots, width),
            room(slots, width),
            room(group_size, 16, capacity),
            room(group_size, 16, capacity),
            room(group_size, *small.shape),
            room(group_size, tokens, dtype=f32),
            room(8, tokens, dtype=f32),
            room(tokens, width),
            room(tokens, width),
            room(2, tokens, width),
            room(3, tokens, width),
            room(4, 16, tokens),
            room(tokens, width, dtype=f32),
            room(tokens, width),
            room(heads, tokens, HEAD_DIM, dtype=f32),
            room(heads, tokens, HEAD_DIM, dtype=f32),
            room(tokens, 3 * head_width),
            room(8, tokens, dtype=f32),
            room(full, 3 * head_width),
            room(full, 3 * head_width),
            room(full, head_width),
            room(full, head_width),
            room(width, tokens),
            room(tensor_size, column_width, tokens),
            room(small.shape[0], width, dtype=f32),
            room(group_size, small.shape[0], width, dtype=f32),
            room(8, width, dtype=f32),
            room(group_size, 8, width, dtype=f32),
            *[room(*a.shape, dtype=a.dtype) for a in (x, q, k, v, o, small, bias, ids, cot)],
            room(column_width, tokens),
            room(column_width, tokens, dtype=f32),
            room(3, block_rows, head_width, dtype=f32),
            room(block_rows, head_width, dtype=f32),
            room(small.shape[0], width, dtype=f32),
            room(8, width, dtype=f32),
            dma((9,)),
            dma((6,)),
            dma((6, group_size)),
            dma((18, group_size)),
            dma((3, 6, chunks + 1)),
            dma((2, tensor_size)),
            dma((18,)),
        ],
        compiler_params=pltpu.CompilerParams(
            collective_id=0, has_side_effects=True, vmem_limit_bytes=VMEM_BYTES
        ),
        name="layer",
    )(x, q, k, v, o, small, bias, ids, cot, w_in, w_out)


def finish_kernel(group_size, *refs):
    sources, targets = refs[:8], refs[8:20]
    held, built = refs[20:28], refs[28:36]
    in_sems, out_sems = refs[36:]
    me = lax.axis_index("dp")

    def pieces(src, dst, sems, at):
        count = 4 if at >= 6 else 1
        rows = src.shape[0] // count
        return [
            pltpu.make_async_copy(src.at[pl.ds(p * rows, rows)], dst.at[pl.ds(p * rows, rows)], sems.at[at, p])
            for p in range(count)
        ]

    taken = [pieces(src, dst, in_sems, at) for at, (src, dst) in enumerate(zip(sources, held))]
    for group in taken:
        for copy in group:
            copy.start()
    block, inputs, qkv, wo, sums, late, in_grad, out_grad = held
    q_o, k_o, v_o, attn_o, ffn_o, router_o, bias_o = built[:7]
    (block_out, input_out, q_out, k_out, v_out, wo_out, attn_out, ffn_out, router_out, bias_out, in_out, out_out) = targets
    given = []

    def give(src, dst, at):
        for copy in pieces(src, dst, out_sems, at):
            copy.start()
            given.append(copy)

    for at in range(6):
        for copy in taken[at]:
            copy.wait()
    give(block, block_out, 0)
    give(inputs, input_out, 1)
    for k, (src, dst) in enumerate(((q_o, q_out), (k_o, k_out), (v_o, v_out))):
        src[...] = qkv[k]
        give(src, dst, 2 + k)
    give(wo, wo_out, 5)
    for at, (src, dst) in ((6, (in_grad, in_out)), (7, (out_grad, out_out))):
        for p, copy in enumerate(taken[at]):
            copy.wait()
            out = pieces(src, dst, out_sems, at)[p]
            out.start()
            given.append(out)
    block_rows = wo.shape[0]
    heads, buckets = bias_o.shape
    features = sums.shape[1]
    shift = lax.rem((group_size - me) * block_rows, features)
    total = sums[...]
    bias_o[...] = total[2 : 2 + heads, :buckets]
    total = pltpu.roll(total, shift, 1)
    ffn_o[...] = total[0:1, :block_rows]
    router_o[...] = total[8:, :block_rows]
    attn_o[...] = pltpu.roll(late[...], shift, 1)[0:1, :block_rows]
    for k, (src, dst) in enumerate(((attn_o, attn_out), (ffn_o, ffn_out), (router_o, router_out), (bias_o, bias_out))):
        copy = pltpu.make_async_copy(src, dst, out_sems.at[8 + k, 0])
        copy.start()
        given.append(copy)
    for copy in given:
        copy.wait()


def finish(group_size, heads, buckets, *results):
    f32 = jnp.float32
    block, inputs, qkv, wo, sums, late, in_grad, out_grad = results
    block_rows = wo.shape[0]

    def shape(*dims):
        return jax.ShapeDtypeStruct(dims, f32)

    small = [(1, block_rows), (1, block_rows), (sums.shape[0] - 8, block_rows), (heads, buckets)]
    hbm = pl.BlockSpec(memory_space=pl.ANY)
    return pl.pallas_call(
        functools.partial(finish_kernel, group_size),
        out_shape=(
            jax.ShapeDtypeStruct(block.shape, block.dtype),
            shape(*inputs.shape),
            *[shape(*wo.shape)] * 4,
            *[shape(*dims) for dims in small],
            shape(*in_grad.shape),
            shape(*out_grad.shape),
        ),
        in_specs=[hbm] * 8,
        out_specs=(hbm,) * 12,
        scratch_shapes=[
            *[pltpu.VMEM(a.shape, a.dtype) for a in results],
            *[pltpu.VMEM(wo.shape, f32)] * 3,
            *[pltpu.VMEM(dims, f32) for dims in small],
            pltpu.VMEM((8, LANES), f32),
            pltpu.SemaphoreType.DMA((8, 4)),
            pltpu.SemaphoreType.DMA((12, 4)),
        ],
        compiler_params=pltpu.CompilerParams(vmem_limit_bytes=VMEM_BYTES),
        name="finish",
    )(*results)


def on_device_general(
    block_input,
    attn_gain,
    query_weight,
    key_weight,
    value_weight,
    output_weight,
    bias_table,
    ffn_gain,
    router_weight,
    expert_in,
    expert_out,
    expert_ids,
    out_cotangent,
):
    tensor_size = lax.axis_size("tensor")
    group_size = lax.axis_size("dp")
    tensor_index = lax.axis_index("tensor")
    own_expert = lax.axis_index("dp")
    token_count, model_width = block_input.shape
    column_width = model_width // tensor_size
    column_start = tensor_index * column_width
    expert_count = group_size * expert_in.shape[0]
    capacity = tensor_size * max(1, 3 * token_count // (5 * expert_count))
    slot_rows = expert_count * capacity
    seq_count = token_count // SEQ_LEN
    head_local = bias_table.shape[0]
    head_width = head_local * HEAD_DIM
    block_rows = query_weight.shape[0]
    low = jnp.bfloat16

    def own_columns(matrix):
        return lax.dynamic_slice_in_dim(matrix, column_start, column_width, 1)

    packed = jnp.concatenate(
        [
            query_weight,
            key_weight,
            value_weight,
            output_weight,
            router_weight,
            attn_gain[:, None],
            ffn_gain[:, None],
        ],
        axis=1,
    )
    packed = lax.all_gather(packed, "dp", axis=0, tiled=True)

    labels = jnp.arange(expert_count, dtype=jnp.int32)
    flat_ids = expert_ids.reshape(-1)
    ids_onehot = (flat_ids[:, None] == labels[None, :]).astype(jnp.int32)
    pair_rows = lax.broadcasted_iota(jnp.int32, (2 * token_count, 2 * token_count), 0)
    pair_cols = lax.broadcasted_iota(jnp.int32, (2 * token_count, 2 * token_count), 1)
    before = (pair_cols < pair_rows).astype(low)
    earlier = dot(before, ids_onehot.astype(low)).astype(jnp.int32)
    slot_index = jnp.sum(earlier * ids_onehot, axis=1)
    places = (flat_ids * capacity + slot_index).reshape(token_count, 2)
    place_rows = jnp.arange(slot_rows, dtype=jnp.int32)
    at_first = places[:, 0][None, :] == place_rows[:, None]
    at_second = places[:, 1][None, :] == place_rows[:, None]
    map_first = at_first.astype(low)
    map_second = at_second.astype(low)
    map_both = (at_first | at_second).astype(low)

    ids_low = jnp.broadcast_to(expert_ids.astype(low)[:, :, None], (token_count, 2, LANES))
    cot_source = jnp.concatenate(
        [
            jnp.concatenate([out_cotangent, ids_low[:, 1]], axis=1),
            jnp.concatenate([out_cotangent, ids_low[:, 0]], axis=1),
        ],
        axis=0,
    )
    cot_parcel = dot(jnp.concatenate([map_first, map_second], axis=1), cot_source).astype(low)
    packed, cot_parcel = lax.optimization_barrier((packed, cot_parcel))
    cot_arrived = exchange(
        cot_parcel.reshape(expert_count, capacity, model_width + LANES)
    ).reshape(slot_rows, model_width + LANES)
    cot_rows = cot_arrived[:, :model_width].astype(jnp.float32)
    other_ids = cot_arrived[:, model_width].astype(jnp.int32)

    qkv_full = packed[:, : 3 * head_width]
    output_full = packed[:, 3 * head_width : 4 * head_width]
    at = 4 * head_width
    router_full = packed[:, at : at + expert_count]
    gain_one = packed[:, at + expert_count].astype(jnp.float32)
    gain_two = packed[:, at + expert_count + 1].astype(jnp.float32)
    inputs_f = block_input.astype(jnp.float32)
    scale_one = rms_scale(inputs_f)
    normed_one = (inputs_f * scale_one * gain_one).astype(low)
    qkv = dot(normed_one, qkv_full).astype(low)
    bucket_vec = bucket_vector_at(jnp.arange(SEQ_LEN, dtype=jnp.int32), NB)
    bucket_labels = jnp.arange(NB, dtype=jnp.int32)
    wrap = (SEQ_LEN - jnp.arange(SEQ_LEN, dtype=jnp.int32)) % SEQ_LEN
    wrapped_onehot = bucket_vector_at(wrap, NB)[None, :] == bucket_labels[:, None]
    wrapped = jnp.sum(
        jnp.where(wrapped_onehot[None], bias_table[:, :, None], 0.0), axis=1
    )
    context, probs = attend_forward(qkv, wrapped, seq_count, head_local)
    attn_part = dot(context, output_full, ((1,), (1,))).astype(low)
    attn_out = lax.psum(attn_part, "tensor").astype(jnp.float32)
    residual = inputs_f + attn_out
    scale_two = rms_scale(residual)
    normed_two = (residual * scale_two * gain_two).astype(low)

    logits = dot(normed_two, router_full)
    picked = (expert_ids[:, :, None] == labels[None, None, :]).astype(jnp.float32)
    chosen = jnp.sum(picked * logits[:, None, :], axis=2)
    first_gate = jax.nn.sigmoid(chosen[:, 0] - chosen[:, 1])
    second_gate = 1.0 - first_gate

    weight_in = expert_in[0]
    weight_out = expert_out[0]
    parcel = dot(map_both, normed_two).astype(low)
    expert_rows = exchange(parcel.reshape(expert_count, capacity, model_width)).reshape(
        slot_rows, model_width
    )
    pre_act = dot(expert_rows, weight_in)
    active, pullback = jax.vjp(jax.nn.gelu, pre_act)
    active = active.astype(low)
    owner_out = dot(active, weight_out)
    owner_logits = dot(expert_rows, router_full)
    own_logit = jnp.sum(
        jnp.where(labels[None, :] == own_expert, owner_logits, 0.0), axis=1
    )
    other_logit = jnp.sum(
        jnp.where(labels[None, :] == other_ids[:, None], owner_logits, 0.0), axis=1
    )
    row_gate = jax.nn.sigmoid(own_logit - other_logit)
    expert_drows = (row_gate[:, None] * cot_rows).astype(low)
    dpre = pullback(dot(expert_drows, weight_out, ((1,), (1,))))[0].astype(low)
    owner_back = dot(dpre, weight_in, ((1,), (1,))).astype(low)
    gate_part = jnp.sum(cot_rows * owner_out, axis=1, keepdims=True).astype(low)
    back_parcel = jnp.concatenate(
        [owner_back, jnp.broadcast_to(gate_part, (slot_rows, LANES))], axis=1
    )
    back_rows = exchange(
        back_parcel.reshape(group_size, capacity, model_width + LANES)
    ).reshape(slot_rows, model_width + LANES)
    out_rows = exchange(
        owner_out.astype(low).reshape(group_size, capacity, model_width)
    ).reshape(slot_rows, model_width)
    out_grad = dot(active, expert_drows, ((0,), (0,)))
    in_grad = dot(expert_rows, dpre, ((0,), (0,)))

    dnormed_part = dot(map_both, back_rows[:, :model_width], ((0,), (0,)))
    gate_diff_part = dot(map_first - map_second, back_rows[:, model_width:], ((0,), (0,)))
    gate_rows = -(-token_count // model_width)
    gate_line = jnp.pad(gate_diff_part[:, 0], (0, gate_rows * model_width - token_count))
    summed = lax.psum(
        jnp.concatenate(
            [dnormed_part, gate_line.reshape(gate_rows, model_width)], axis=0
        ).astype(low),
        "tensor",
    ).astype(jnp.float32)
    gate_diff = summed[token_count:].reshape(-1)[:token_count]
    mixture_part = first_gate[:, None] * dot(map_first, out_rows, ((0,), (0,)))
    mixture_part = mixture_part + second_gate[:, None] * dot(
        map_second, out_rows, ((0,), (0,))
    )
    mixture_parts = mixture_part.astype(low).reshape(token_count, tensor_size, column_width)
    mixture_parts = jnp.swapaxes(mixture_parts, 0, 1)

    dlogit = gate_diff * first_gate * second_gate
    signed = jnp.stack([dlogit, -dlogit], axis=1)
    dlogits = jnp.sum(picked * signed[:, :, None], axis=1).astype(low)
    router_term = dot(normed_two, dlogits, ((0,), (0,)))
    dnormed_two = summed[:token_count] + dot(dlogits, router_full, ((1,), (1,)))
    ffn_term = jnp.sum(dnormed_two * residual * scale_two, axis=0)
    cot_f = out_cotangent.astype(jnp.float32)
    dresidual = cot_f + norm_back(dnormed_two, residual, scale_two, gain_two)
    dres_low = dresidual.astype(low)
    mixture_parts, dres_low = lax.optimization_barrier((mixture_parts, dres_low))
    mixture_parts = lax.all_to_all(
        mixture_parts, "tensor", split_axis=0, concat_axis=0, tiled=True
    )

    output_term = dot(dres_low, context, ((0,), (0,)))
    dcontext = dot(dres_low, output_full).astype(low)
    dqkv, diagonal = attend_backward(qkv, probs, dcontext, seq_count, head_local)
    reverse_onehot = (bucket_vec[::-1][:, None] == bucket_labels[None, :]).astype(jnp.float32)
    bias_term = jnp.dot(
        jnp.sum(diagonal, axis=0),
        reverse_onehot,
        precision=lax.Precision.HIGHEST,
        preferred_element_type=jnp.float32,
    )
    dnormed_part = dot(dqkv, qkv_full, ((1,), (1,))).astype(low)
    dnormed_part, mixture_parts = lax.optimization_barrier((dnormed_part, mixture_parts))
    dnormed_one = lax.psum(dnormed_part, "tensor").astype(jnp.float32)
    qkv_term = dot(normed_one, dqkv, ((0,), (0,)))
    bias_count = bias_term.size
    bias_cols = -(-bias_count // block_rows)
    bias_block = jnp.pad(bias_term.reshape(-1), (0, bias_cols * block_rows - bias_count))
    bias_block = jnp.tile(bias_block.reshape(block_rows, bias_cols), (group_size, 1))
    terms = jnp.concatenate(
        [qkv_term, output_term, router_term, ffn_term[:, None], bias_block],
        axis=1,
    ).astype(low)
    term_width = terms.shape[1]
    arrived = exchange(terms.reshape(group_size, block_rows, term_width))
    arrived, dnormed_one = lax.optimization_barrier((arrived, dnormed_one))
    mixture = jnp.sum(mixture_parts.astype(jnp.float32), axis=0)
    block_output = (own_columns(residual) + mixture).astype(low)
    reduced = jnp.sum(arrived.astype(jnp.float32), axis=0)
    at = 4 * head_width
    grads = [reduced[:, k * head_width : (k + 1) * head_width] for k in range(4)]
    router_grad = reduced[:, at : at + expert_count]
    at = at + expert_count
    bias_grad = reduced[:, at + 1 :].reshape(-1)[:bias_count].reshape(bias_term.shape)
    attn_term = jnp.sum(dnormed_one * inputs_f * scale_one, axis=0)
    attn_gain_grad = jnp.sum(exchange(attn_term.reshape(group_size, block_rows)), axis=0)
    first_back = norm_back(dnormed_one, inputs_f, scale_one, gain_one)
    input_grad = own_columns(dresidual + first_back)
    return (
        block_output,
        input_grad,
        attn_gain_grad,
        grads[0],
        grads[1],
        grads[2],
        grads[3],
        bias_grad,
        reduced[:, at],
        router_grad,
        in_grad[None],
        out_grad[None],
    )


def on_device(
    block_input,
    attn_gain,
    query_weight,
    key_weight,
    value_weight,
    output_weight,
    bias_table,
    ffn_gain,
    router_weight,
    expert_in,
    expert_out,
    expert_ids,
    out_cotangent,
):
    tensor_size = lax.axis_size("tensor")
    group_size = lax.axis_size("dp")
    token_count = block_input.shape[0]
    block_rows = query_weight.shape[0]
    head_local = bias_table.shape[0]
    low = jnp.bfloat16
    capacity = tensor_size * max(1, 3 * token_count // (5 * group_size))
    capacity = -(-capacity // 16) * 16
    small = jnp.concatenate(
        [attn_gain[None, :], ffn_gain[None, :], jnp.zeros((6, block_rows), low), router_weight.T],
        axis=0,
    )
    small = jnp.pad(small, ((0, 0), (0, LANES - block_rows)))
    results = run_layer(
        group_size,
        tensor_size,
        capacity,
        block_input,
        query_weight,
        key_weight,
        value_weight,
        output_weight,
        small,
        bias_table,
        expert_ids.T,
        out_cotangent,
        expert_in[0],
        expert_out[0],
    )
    block, inputs, query, key, value, output, attn, ffn, router, bias, in_grad, out_grad = finish(
        group_size, head_local, NB, *results
    )
    return (
        block.T,
        inputs.T,
        attn[0],
        query,
        key,
        value,
        output,
        bias,
        ffn[0],
        router.T,
        in_grad[None],
        out_grad[None],
    )


def choose(mesh):
    def run(*arrays):
        tokens, width = arrays[0].shape
        block_rows = arrays[2].shape[0]
        hidden = arrays[9].shape[2]
        group_size = mesh.shape["dp"]
        fits = (
            block_rows % 16 == 0
            and block_rows <= LANES
            and arrays[9].shape[0] == 1
            and mesh.shape["tensor"] == 4
            and group_size == 8
            and arrays[6].shape[0] <= 6
            and tokens == SEQ_LEN
            and hidden == width
            and width % 256 == 0
            and width % 64 == 0
        )
        return (on_device if fits else on_device_general)(*arrays)

    return run


def solution(mesh):
    placed = (
        P("dp", None),
        P("dp"),
        P("dp", "tensor"),
        P("dp", "tensor"),
        P("dp", "tensor"),
        P("dp", "tensor"),
        P("tensor", None),
        P("dp"),
        P("dp", None),
        P("dp", None, "tensor"),
        P("dp", "tensor", None),
        P("dp", None),
        P("dp", None),
    )
    return jax.shard_map(
        choose(mesh),
        mesh=mesh,
        in_specs=placed,
        out_specs=(
            P("dp", "tensor"),
            P("dp", "tensor"),
            P("dp"),
            P("dp", "tensor"),
            P("dp", "tensor"),
            P("dp", "tensor"),
            P("dp", "tensor"),
            P("tensor", None),
            P("dp"),
            P("dp", None),
            P("dp", None, "tensor"),
            P("dp", "tensor", None),
        ),
        check_vma=False,
    )
```

```python
import functools
import math

import jax
import jax.numpy as jnp
from jax import lax
from jax.experimental import pallas as pl
from jax.experimental.pallas import tpu as pltpu
from jax.sharding import PartitionSpec as P

HEAD_DIM = 64
NB = 32
SEQ_LEN = 512
LANES = 128
VMEM_BYTES = 63 * 1024 * 1024
PIECE = 32
LAG = 4


EPSILON = 1e-06
MASKED = -1e30


def bucket_vector_at(steps_ids, bucket_count):
    exact_count = bucket_count // 2
    distant = jnp.full(steps_ids.shape, exact_count, jnp.int32)
    for level_index in range(1, bucket_count - exact_count):
        border = int(math.ceil(exact_count * 8.0 ** (level_index / (bucket_count - exact_count))))
        distant = distant + (steps_ids >= border).astype(jnp.int32)
    return jnp.where(steps_ids < exact_count, steps_ids, distant)


def norm_back(dnormed, row_values, row_scale, gain_row):
    inner_mean = jnp.mean(gain_row * dnormed * row_values, axis=-1, keepdims=True)
    return row_scale * (gain_row * dnormed - row_values * row_scale * row_scale * inner_mean)


def rms_scale(matrix):
    return lax.rsqrt(jnp.mean(matrix * matrix, axis=-1, keepdims=True) + EPSILON)


def dot(left, right, dims=((1,), (0,))):
    return lax.dot_general(left, right, (dims, ((), ())), preferred_element_type=jnp.float32)


def forward_kernel(qkv_ref, wrapped_ref, context_ref, probs_ref):
    length = qkv_ref.shape[0]
    heads = probs_ref.shape[0]
    width = heads * HEAD_DIM
    factor = HEAD_DIM ** (-0.5)
    rows = lax.broadcasted_iota(jnp.int32, (length, length), 0)
    cols = lax.broadcasted_iota(jnp.int32, (length, length), 1)
    causal = rows >= cols
    for h in range(heads):
        lo, hi = h * HEAD_DIM, (h + 1) * HEAD_DIM
        queries = qkv_ref[:, lo:hi]
        keys = qkv_ref[:, width + lo : width + hi]
        values = qkv_ref[:, 2 * width + lo : 2 * width + hi]
        bias = jnp.broadcast_to(wrapped_ref[h : h + 1, :], (length, length))
        bias = pltpu.roll(bias, 0, 1, stride=1, stride_axis=0)
        scores = jnp.where(causal, dot(queries, keys, ((1,), (1,))) * factor + bias, MASKED)
        row_max = jnp.max(scores, axis=-1, keepdims=True)
        row_total = jnp.sum(jnp.exp(scores - row_max), axis=-1, keepdims=True)
        probs = jnp.exp(scores - (row_max + jnp.log(row_total))).astype(jnp.bfloat16)
        probs_ref[h] = probs
        context_ref[:, lo:hi] = dot(probs, values).astype(jnp.bfloat16)


def backward_kernel(qkv_ref, probs_ref, dcontext_ref, dqkv_ref, diagonal_ref):
    length = qkv_ref.shape[0]
    heads = probs_ref.shape[0]
    width = heads * HEAD_DIM
    factor = HEAD_DIM ** (-0.5)
    rows = lax.broadcasted_iota(jnp.int32, (length, length), 0)
    cols = lax.broadcasted_iota(jnp.int32, (length, length), 1)
    flip = (rows + cols == length - 1).astype(jnp.float32).astype(jnp.bfloat16)
    for h in range(heads):
        lo, hi = h * HEAD_DIM, (h + 1) * HEAD_DIM
        queries = qkv_ref[:, lo:hi]
        keys = qkv_ref[:, width + lo : width + hi]
        values = qkv_ref[:, 2 * width + lo : 2 * width + hi]
        dcontext = dcontext_ref[:, lo:hi]
        probs = probs_ref[h]
        weights = probs.astype(jnp.float32)
        dweights = dot(dcontext, values, ((1,), (1,)))
        agreement = jnp.sum(weights * dweights, axis=-1, keepdims=True)
        dscores = (weights * (dweights - agreement)).astype(jnp.bfloat16)
        dqkv_ref[:, lo:hi] = (factor * dot(dscores, keys)).astype(jnp.bfloat16)
        dqkv_ref[:, width + lo : width + hi] = (
            factor * dot(dscores, queries, ((0,), (0,)))
        ).astype(jnp.bfloat16)
        dqkv_ref[:, 2 * width + lo : 2 * width + hi] = dot(
            probs, dcontext, ((0,), (0,))
        ).astype(jnp.bfloat16)
        skewed = pltpu.roll(dot(flip, dscores), 0, 1, stride=1, stride_axis=0)
        diagonal_ref[h : h + 1, :] = jnp.sum(skewed, axis=0, keepdims=True)


def attend_forward(qkv, wrapped, seq_count, heads):
    width = heads * HEAD_DIM
    return pl.pallas_call(
        forward_kernel,
        grid=(seq_count,),
        out_shape=(
            jax.ShapeDtypeStruct((seq_count * SEQ_LEN, width), jnp.bfloat16),
            jax.ShapeDtypeStruct((seq_count, heads, SEQ_LEN, SEQ_LEN), jnp.bfloat16),
        ),
        in_specs=[
            pl.BlockSpec((SEQ_LEN, 3 * width), lambda s: (s, 0)),
            pl.BlockSpec((heads, SEQ_LEN), lambda s: (0, 0)),
        ],
        out_specs=(
            pl.BlockSpec((SEQ_LEN, width), lambda s: (s, 0)),
            pl.BlockSpec((None, heads, SEQ_LEN, SEQ_LEN), lambda s: (s, 0, 0, 0)),
        ),
        name="attend_forward",
    )(qkv, wrapped)


def attend_backward(qkv, probs, dcontext, seq_count, heads):
    width = heads * HEAD_DIM
    return pl.pallas_call(
        backward_kernel,
        grid=(seq_count,),
        out_shape=(
            jax.ShapeDtypeStruct((seq_count * SEQ_LEN, 3 * width), jnp.bfloat16),
            jax.ShapeDtypeStruct((seq_count, heads, SEQ_LEN), jnp.float32),
        ),
        in_specs=[
            pl.BlockSpec((SEQ_LEN, 3 * width), lambda s: (s, 0)),
            pl.BlockSpec((None, heads, SEQ_LEN, SEQ_LEN), lambda s: (s, 0, 0, 0)),
            pl.BlockSpec((SEQ_LEN, width), lambda s: (s, 0)),
        ],
        out_specs=(
            pl.BlockSpec((SEQ_LEN, 3 * width), lambda s: (s, 0)),
            pl.BlockSpec((None, heads, SEQ_LEN), lambda s: (s, 0, 0)),
        ),
        name="attend_backward",
    )(qkv, probs, dcontext)


def exchange(parcel):
    return lax.all_to_all(parcel, "dp", split_axis=0, concat_axis=0, tiled=True)


def remote(src, dst, send_sem, recv_sem, axis, index):
    return pltpu.make_async_remote_copy(
        src_ref=src,
        dst_ref=dst,
        send_sem=send_sem,
        recv_sem=recv_sem,
        device_id={axis: index},
        device_id_type=pl.DeviceIdType.MESH,
    )


def rows_at(index, count):
    return pl.ds(pl.multiple_of(index * count, count), count)


def gelu_both(u):
    slope = math.sqrt(2.0 / math.pi)
    cubic = 0.044715
    square = u * u
    t = jnp.tanh(slope * u * (1.0 + cubic * square))
    half = 0.5 + 0.5 * t
    value = u * half
    grad = half + 0.5 * u * (1.0 - t * t) * (slope * (1.0 + 3.0 * cubic * square))
    return value, grad


def layer_kernel(
    group_size,
    tensor_size,
    x_hbm,
    q_hbm,
    k_hbm,
    v_hbm,
    o_hbm,
    small_hbm,
    bias_hbm,
    ids_hbm,
    cot_hbm,
    win_hbm,
    wout_hbm,
    block_hbm_out,
    input_hbm_out,
    qkv_hbm_out,
    wo_hbm_out,
    sums_hbm_out,
    late_hbm_out,
    in_grad_hbm,
    out_grad_hbm,
    wqkv_ref,
    wo_ref,
    gains_ref,
    qkv_ref,
    probs_ref,
    context_ref,
    normed_one_ref,
    normed_ref,
    residual_ref,
    residual_t_ref,
    both_ref,
    signed_ref,
    gated_ref,
    strips_ref,
    rows_ref,
    cots_ref,
    win_ref,
    wout_ref,
    active_ref,
    drows_ref,
    dpre_ref,
    grad_ref,
    send_ref,
    cot_send_ref,
    back_send_ref,
    back_ref,
    out_send_ref,
    out_ref,
    gate_send_ref,
    gate_ref,
    small_buf,
    code_ref,
    gates_ref,
    part_ref,
    near_ref,
    middle_ref,
    total_ref,
    gate_line_ref,
    dres_ref,
    dres_low_ref,
    dkeys_ref,
    dvalues_ref,
    dqkv_ref,
    diagonal_ref,
    terms_send_ref,
    terms_ref,
    oterms_send_ref,
    oterms_ref,
    mix_send_ref,
    mix_ref,
    sums_send_ref,
    sums_ref,
    late_send_ref,
    late_ref,
    x_ref,
    q_ref,
    k_ref,
    v_ref,
    o_ref,
    small_ref,
    bias_ref,
    ids_ref,
    cot_ref,
    block_out,
    input_out,
    qkv_out,
    wo_out,
    sums_out,
    late_out,
    load_sems,
    store_sems,
    row_sems,
    w_sems,
    a2a_sems,
    line_sems,
    z_sems,
    local_sems,
):
    me = lax.axis_index("dp")
    level = lax.axis_index("tensor")
    token_count, model_width = x_ref.shape
    experts = group_size
    capacity = both_ref.shape[0] // group_size
    half = lax.rem(level, 2)
    strip = 256
    block_rows, head_width = q_ref.shape
    heads = bias_ref.shape[0]
    column_width = model_width // tensor_size
    low = jnp.bfloat16
    f32 = jnp.float32
    near = level + 1 - 2 * lax.rem(level, 2)
    across = tensor_size - 1 - level
    is_end = jnp.logical_or(level == 0, level == tensor_size - 1)
    is_middle = jnp.logical_not(is_end)
    chip = me // 2
    core = lax.rem(me, 2)
    chips = group_size // 2
    chunk = LANES
    chunks = token_count // chunk
    factor = HEAD_DIM ** (-0.5)

    def peer_of(j):
        other_chip = lax.rem(chip - j // 2 + chips, chips)
        return 2 * other_chip + lax.rem(core + j, 2)

    def each_peer(body):
        def step(j, carry):
            body(peer_of(j))
            return carry

        lax.fori_loop(1, group_size, step, 0)

    def load_in():
        return pltpu.make_async_copy(win_hbm, win_ref, local_sems.at[0])

    def load_out():
        return pltpu.make_async_copy(wout_hbm, wout_ref, local_sems.at[1])

    def loads(first, last):
        pairs = [
            (q_hbm, q_ref),
            (k_hbm, k_ref),
            (v_hbm, v_ref),
            (o_hbm, o_ref),
            (small_hbm, small_ref),
            (ids_hbm, ids_ref),
            (bias_hbm, bias_ref),
            (cot_hbm, cot_ref),
            (x_hbm, x_ref),
        ]
        return [
            pltpu.make_async_copy(src, dst, load_sems.at[place])
            for place, (src, dst) in enumerate(pairs)
            if first <= place < last
        ]

    for copy in loads(0, 9):
        copy.start()
    load_in().start()
    load_out().start()

    def stores():
        pairs = [
            (input_out, input_hbm_out),
            (qkv_out, qkv_hbm_out),
            (wo_out, wo_hbm_out),
            (block_out, block_hbm_out),
            (sums_out, sums_hbm_out),
            (late_out, late_hbm_out),
        ]
        return [
            pltpu.make_async_copy(src, dst, store_sems.at[place])
            for place, (src, dst) in enumerate(pairs)
        ]

    barrier = pltpu.get_barrier_semaphore()
    each_peer(
        lambda peer: pl.semaphore_signal(
            barrier, inc=1, device_id={"dp": peer}, device_id_type=pl.DeviceIdType.MESH
        )
    )

    def greet(step, carry):
        other = lax.rem(level + step, tensor_size)
        pl.semaphore_signal(
            barrier, inc=1, device_id={"tensor": other}, device_id_type=pl.DeviceIdType.MESH
        )
        return carry

    lax.fori_loop(1, tensor_size, greet, 0)
    mine = rows_at(me, block_rows)
    for copy in loads(0, 5):
        copy.wait()
    wqkv_ref[mine, :] = jnp.concatenate([q_ref[...], k_ref[...], v_ref[...]], axis=1)
    wo_ref[mine, :] = o_ref[...]
    small_buf[me] = small_ref[...]

    pl.semaphore_wait(barrier, group_size + tensor_size - 2)

    sibling = 2 * chip + 1 - core

    def weight_copies(peer, source, slot):
        block = rows_at(source, block_rows)
        return [
            remote(wqkv_ref.at[block], wqkv_ref.at[block], w_sems.at[0, slot], w_sems.at[1, source], "dp", peer),
            remote(wo_ref.at[block], wo_ref.at[block], w_sems.at[2, slot], w_sems.at[3, source], "dp", peer),
            remote(small_buf.at[source], small_buf.at[source], w_sems.at[4, slot], w_sems.at[5, source], "dp", peer),
        ]

    def each_chip(body):
        def step(j, carry):
            body(lax.rem(chip + j, chips))
            return carry

        lax.fori_loop(1, chips, step, 0)

    def start_all(copies):
        for copy in copies:
            copy.start()

    def recv_all(copies):
        for copy in copies:
            copy.wait_recv()

    def sent_all(copies):
        for copy in copies:
            copy.wait_send()

    def send_weights(other):
        peer = 2 * other + core
        start_all(weight_copies(peer, me, peer))

    each_chip(send_weights)
    start_all(weight_copies(sibling, me, sibling))

    def block_copy(kind, src, dst, peer, source, count):
        return remote(
            src.at[rows_at(peer, count)],
            dst.at[rows_at(source, count)],
            a2a_sems.at[2 * kind, peer],
            a2a_sems.at[2 * kind + 1, source],
            "dp",
            peer,
        )

    def cot_copy(peer, source):
        return block_copy(0, cot_send_ref, cots_ref, peer, source, capacity)

    def row_copy(peer, source, strip_index, place):
        return remote(
            send_ref.at[strip_index, rows_at(peer, capacity)],
            rows_ref.at[strip_index, rows_at(source, capacity)],
            row_sems.at[2 * place, peer],
            row_sems.at[2 * place + 1, source],
            "dp",
            peer,
        )

    def hand_over(source, strip_index):
        block = rows_ref.at[strip_index, rows_at(source, capacity)]
        return remote(block, block, row_sems.at[4, source], row_sems.at[5, source], "tensor", near)

    def each_source(body):
        def step(j, carry):
            other_chip = lax.rem(chip + j // 2, chips)
            body(2 * other_chip + lax.rem(core + j, 2))
            return carry

        lax.fori_loop(1, group_size, step, 0)

    def back_copy(peer, source):
        return block_copy(2, back_send_ref, back_ref, peer, source, capacity)

    def out_copy(peer, source):
        return block_copy(3, out_send_ref, out_ref, peer, source, capacity)

    def term_copies(peer, source):
        return [
            block_copy(4, terms_send_ref, terms_ref, peer, source, block_rows),
            block_copy(5, oterms_send_ref, oterms_ref, peer, source, block_rows),
        ]

    def gate_copy(peer, source):
        return remote(
            gate_send_ref.at[peer], gate_ref.at[source], a2a_sems.at[12, peer], a2a_sems.at[13, source], "dp", peer
        )

    def late_copy(peer, source):
        return remote(
            late_send_ref, late_ref.at[source], a2a_sems.at[16, peer], a2a_sems.at[17, source], "dp", peer
        )

    def sums_copy(peer, source):
        return remote(
            sums_send_ref, sums_ref.at[source], a2a_sems.at[14, peer], a2a_sems.at[15, source], "dp", peer
        )

    for copy in loads(5, 9):
        copy.wait()
    ids_first = ids_ref[0:1, :]
    ids_second = ids_ref[1:2, :]
    labels = lax.broadcasted_iota(jnp.int32, (experts, token_count), 0)
    member = jnp.logical_or(labels == ids_first, labels == ids_second)
    tokens_r = lax.broadcasted_iota(jnp.int32, (token_count, token_count), 0)
    tokens_c = lax.broadcasted_iota(jnp.int32, (token_count, token_count), 1)
    upper = jnp.where(tokens_r < tokens_c, 1.0, 0.0).astype(low)
    counted = dot(jnp.where(member, 1.0, 0.0).astype(low), upper)
    code_ref[...] = jnp.where(member, counted, -1.0)
    slots = lax.broadcasted_iota(jnp.int32, (capacity, token_count), 0).astype(f32)
    id_total = jnp.broadcast_to((ids_first + ids_second).astype(f32), (LANES, token_count)).astype(low)

    def make_maps(expert, carry):
        block = rows_at(expert, capacity)
        hit = slots == code_ref[pl.ds(expert, 1), :]
        sign = jnp.where(ids_first == expert, 1.0, -1.0)
        both = jnp.where(hit, 1.0, 0.0).astype(low)
        both_ref[block, :] = both
        signed_ref[block, :] = jnp.where(hit, sign, 0.0).astype(low)
        cot_send_ref[block, :model_width] = dot(both, cot_ref[...]).astype(low)
        cot_send_ref[block, model_width:] = dot(both, id_total, ((1,), (1,))).astype(low)
        return carry

    lax.fori_loop(0, experts, make_maps, 0)

    inputs_f = x_ref[...].astype(f32)
    scaled = inputs_f * rms_scale(inputs_f)

    lane = lax.broadcasted_iota(jnp.int32, (heads, token_count), 1)
    wrap_bucket = bucket_vector_at(jnp.where(lane == 0, 0, token_count - lane), NB)
    wrapped = jnp.zeros((heads, token_count), f32)
    for b in range(NB):
        wrapped = jnp.where(wrap_bucket == b, bias_ref[:, b : b + 1], wrapped)

    def pass_on(other):
        source = 2 * other + core
        recv_all(weight_copies(sibling, source, source))
        start_all(weight_copies(sibling, source, 2 * other + 1 - core))

    def take_passed(other):
        source = 2 * other + 1 - core
        recv_all(weight_copies(sibling, source, source))

    each_chip(pass_on)
    recv_all(weight_copies(sibling, sibling, sibling))
    each_chip(take_passed)
    each_peer(lambda peer: cot_copy(peer, me).start())

    gains = jnp.zeros(gains_ref.shape, f32)
    for source in range(group_size):
        slab = jnp.concatenate(
            [small_buf[source].astype(f32), jnp.zeros((gains.shape[0], model_width - LANES), f32)], axis=1
        )
        gains = gains + (pltpu.roll(slab, source * block_rows, 1) if source else slab)
    gains_ref[...] = gains
    gain_one = gains_ref[0:1, :]
    gain_two = gains_ref[1:2, :]
    normed_one_ref[...] = (scaled * gain_one).astype(low)
    qkv_ref[...] = dot(normed_one_ref[...], wqkv_ref[...]).astype(low)

    def at_chunk(c):
        return slice(c * chunk, (c + 1) * chunk)

    per_chunk = chunk // PIECE
    pieces_all = chunks * per_chunk

    def at_piece(i):
        return slice(i * PIECE, (i + 1) * PIECE)

    def pieces_of(c):
        return [None] if c is None else range(c * per_chunk, (c + 1) * per_chunk)

    def line_copy(r, i, hop):
        at = pieces_all if i is None else i
        if hop == 0:
            peer = near
            src, dst = (
                (gate_line_ref.at[0], gate_line_ref.at[1])
                if i is None
                else (part_ref.at[at_piece(i)], near_ref.at[at_piece(i)])
            )
        elif hop == 1:
            peer = across
            src, dst = (
                (gate_line_ref.at[0], gate_line_ref.at[2])
                if i is None
                else (part_ref.at[at_piece(i)], middle_ref.at[r % 2, at_piece(i)])
            )
        else:
            peer = near
            src = dst = gate_line_ref.at[3] if i is None else total_ref.at[r, at_piece(i)]
        return remote(src, dst, line_sems.at[r, 2 * hop, at], line_sems.at[r, 2 * hop + 1, at], "tensor", peer)

    def line_start(r, c):
        @pl.when(is_end)
        def _():
            for i in pieces_of(c):
                line_copy(r, i, 0).start()

    def line_first(r, i):
        line_copy(r, i, 0).wait_recv()
        if i is None:
            gate_line_ref[0] = (gate_line_ref[0].astype(f32) + gate_line_ref[1].astype(f32)).astype(low)
        else:
            block = at_piece(i)
            part_ref[block, :] = (part_ref[block, :].astype(f32) + near_ref[block, :].astype(f32)).astype(low)
        line_copy(r, i, 1).start()

    def line_second(r, i):
        line_copy(r, i, 1).wait_recv()
        if i is None:
            gate_line_ref[3] = (gate_line_ref[0].astype(f32) + gate_line_ref[2].astype(f32)).astype(low)
        else:
            block = at_piece(i)
            total_ref[r, block, :] = (
                part_ref[block, :].astype(f32) + middle_ref[r % 2, block, :].astype(f32)
            ).astype(low)
        line_copy(r, i, 2).start()

    pending = {0: [], 1: [], 2: []}

    def line_serve(r, c):
        @pl.when(is_middle)
        def _():
            for i in pieces_of(c):
                line_first(r, i)
                pending[r].append(i)
                if len(pending[r]) > LAG:
                    line_second(r, pending[r].pop(0))

    def line_flush(r):
        @pl.when(is_middle)
        def _():
            while pending[r]:
                line_second(r, pending[r].pop(0))

    def line_take(r, c):
        @pl.when(is_end)
        def _():
            for i in pieces_of(c):
                line_copy(r, i, 2).wait_recv()

    def line_drain(r, c):
        @pl.when(is_end)
        def _():
            for i in pieces_of(c):
                line_copy(r, i, 0).wait_send()

        @pl.when(is_middle)
        def _():
            for i in pieces_of(c):
                line_copy(r, i, 1).wait_send()
                line_copy(r, i, 2).wait_send()

    for c in range(chunks):
        lo, hi = c * chunk, (c + 1) * chunk
        causal = lax.broadcasted_iota(jnp.int32, (chunk, hi), 0) + lo >= (
            lax.broadcasted_iota(jnp.int32, (chunk, hi), 1)
        )
        pieces = []
        for h in range(heads):
            at = h * HEAD_DIM
            queries = qkv_ref[lo:hi, at : at + HEAD_DIM]
            keys = qkv_ref[0:hi, head_width + at : head_width + at + HEAD_DIM]
            values = qkv_ref[0:hi, 2 * head_width + at : 2 * head_width + at + HEAD_DIM]
            bias = jnp.broadcast_to(wrapped[h : h + 1, :], (chunk, token_count))
            bias = pltpu.roll(bias, lo, 1, stride=1, stride_axis=0)[:, :hi]
            scores = jnp.where(causal, dot(queries, keys, ((1,), (1,))) * factor + bias, MASKED)
            row_max = jnp.max(scores, axis=-1, keepdims=True)
            grown = jnp.exp(scores - row_max)
            total = jnp.sum(grown, axis=-1, keepdims=True)
            probs = (grown * (1.0 / total)).astype(low)
            probs_ref[h, lo:hi, 0:hi] = probs
            pieces.append(dot(probs, values).astype(low))
        context = jnp.concatenate(pieces, axis=1)
        context_ref[lo:hi, :] = context
        part_ref[lo:hi, :] = dot(context, wo_ref[...], ((1,), (1,))).astype(low)
        line_start(0, c)
        if c >= 1:
            line_serve(0, c - 1)
    line_serve(0, chunks - 1)
    line_flush(0)

    for c in range(chunks):
        block = at_chunk(c)
        line_take(0, c)
        residual = x_ref[block, :].astype(f32) + total_ref[0, block, :].astype(f32)
        residual_ref[block, :] = residual
        normed = (residual * rms_scale(residual) * gain_two).astype(low)
        normed_ref[block, :] = normed
        for k in range(model_width // strip):
            strips_ref[k, block, :] = normed[:, k * strip : (k + 1) * strip]

    def send_strip(strip_index, place):
        def body(peer):
            block = rows_at(peer, capacity)
            send_ref[strip_index, block, :] = dot(both_ref[block, :], strips_ref[strip_index]).astype(low)
            row_copy(peer, me, strip_index, place).start()

        each_peer(body)

    shared = 1 + half
    send_strip(shared, 0)
    send_strip(0, 1)

    def forward(source):
        row_copy(source, source, shared, 0).wait_recv()
        hand_over(source, shared).start()

    each_source(forward)
    own = rows_at(me, capacity)
    for k in range(model_width // strip):
        rows_ref[k, own, :] = dot(both_ref[own, :], strips_ref[k]).astype(low)
    cots_ref[own, :] = cot_send_ref[own, :]

    gains_low = gains_ref[...].astype(low)
    logits = dot(gains_low, normed_ref[...], ((1,), (1,)))
    label_rows = lax.broadcasted_iota(jnp.int32, logits.shape, 0) - 8
    chosen_first = jnp.sum(jnp.where(label_rows == ids_first, logits, 0.0), axis=0, keepdims=True)
    chosen_second = jnp.sum(jnp.where(label_rows == ids_second, logits, 0.0), axis=0, keepdims=True)
    gate_first = jax.nn.sigmoid(chosen_first - chosen_second)
    gate_second = 1.0 - gate_first
    gates_ref[0:1, :] = gate_first
    gates_ref[1:2, :] = gate_second

    def make_gated(expert, carry):
        block = rows_at(expert, capacity)
        sign = signed_ref[block, :].astype(f32)
        gated_ref[block, :] = jnp.where(sign > 0, gate_first, jnp.where(sign < 0, gate_second, 0.0)).astype(low)
        return carry

    lax.fori_loop(0, experts, make_gated, 0)
    for z in range(tensor_size):

        @pl.when(level == z)
        def _():
            residual_t_ref[...] = jnp.transpose(residual_ref[:, z * column_width : (z + 1) * column_width])

    load_in().wait()
    load_out().wait()

    pair = 2 * capacity
    ones = jnp.ones((16, model_width), low)

    def expert_step(step, carry):
        other = lax.rem(chip + step, chips)
        block = rows_at(other, pair)
        for c in range(2):
            source = 2 * other + c

            @pl.when(source != me)
            def _():
                cot_copy(source, source).wait_recv()
                row_copy(source, source, 0, 1).wait_recv()
                hand_over(source, 2 - half).wait_recv()

        rows = jnp.concatenate([rows_ref[k, block, :] for k in range(model_width // strip)], axis=1)
        value, slope = gelu_both(dot(rows, win_ref[...]))
        active = value.astype(low)
        active_ref[block, :] = active
        owner_logits = dot(rows, gains_low, ((1,), (1,)))
        columns = lax.broadcasted_iota(jnp.int32, owner_logits.shape, 1) - 8
        other_ids = cots_ref[block, model_width : model_width + 1].astype(f32).astype(jnp.int32) - me
        own_logit = jnp.sum(jnp.where(columns == me, owner_logits, 0.0), axis=1, keepdims=True)
        other_logit = jnp.sum(jnp.where(columns == other_ids, owner_logits, 0.0), axis=1, keepdims=True)
        row_gate = jax.nn.sigmoid(own_logit - other_logit)
        cot = cots_ref[block, :model_width].astype(f32)
        drows = (row_gate * cot).astype(low)
        drows_ref[block, :] = drows
        dpre = (dot(drows, wout_ref[...], ((1,), (1,))) * slope).astype(low)
        dpre_ref[block, :] = dpre
        back_send_ref[block, :] = dot(dpre, win_ref[...], ((1,), (1,))).astype(low)
        for c in range(2):
            source = 2 * other + c

            @pl.when(source != me)
            def _():
                back_copy(source, me).start()

        owner_out = dot(active, wout_ref[...])
        out_send_ref[block, :] = owner_out.astype(low)
        agree = (cot * owner_out).astype(low)
        for c in range(2):
            source = 2 * other + c
            gate_send_ref[source] = dot(ones, agree[c * capacity : (c + 1) * capacity, :], ((1,), (1,))).astype(low)

            @pl.when(source != me)
            def _():
                gate_copy(source, me).start()

        return carry

    lax.fori_loop(0, chips, expert_step, 0)
    back_ref[own, :] = back_send_ref[own, :]
    out_ref[own, :] = out_send_ref[own, :]
    gate_ref[me] = gate_send_ref[me]

    def grad_out(which, part):
        target = (out_grad_hbm, in_grad_hbm)[which]
        block = slice(part * 256, (part + 1) * 256)
        return pltpu.make_async_copy(grad_ref.at[which, block], target.at[block], local_sems.at[2 + which * 8 + part])

    parts = win_ref.shape[0] // 256
    for part in range(parts):
        block = slice(part * 256, (part + 1) * 256)
        grad_ref[0, block, :] = dot(active_ref[:, block], drows_ref[...], ((0,), (0,)))
        grad_out(0, part).start()
        grad_ref[1, block, :] = dot(rows_ref[part], dpre_ref[...], ((0,), (0,)))
        grad_out(1, part).start()

    each_peer(lambda source: gate_copy(source, source).wait_recv())
    each_peer(lambda source: back_copy(source, source).wait_recv())
    each_peer(lambda peer: out_copy(peer, me).start())
    gate_line = dot(gate_ref[0], signed_ref[0:capacity, :])
    for e in range(1, experts):
        gate_line = gate_line + dot(gate_ref[e], signed_ref[e * capacity : (e + 1) * capacity, :])
    gate_line_ref[0] = gate_line.astype(low)
    line_start(1, None)
    order = list(range(chunks))[::-1]
    queue = [None] + order
    for place, c in enumerate(queue):
        if c is not None:
            block = at_chunk(c)
            line_drain(0, c)
            part_ref[block, :] = dot(both_ref[:, block], back_ref[...], ((0,), (0,))).astype(low)
            line_start(1, c)
        if place >= 1:
            line_serve(1, queue[place - 1])
    line_serve(1, queue[-1])
    line_flush(1)

    line_take(1, None)
    gate_diff = gate_line_ref[3, 0:1, :].astype(f32)
    dlogit = gate_diff * gates_ref[0:1, :] * gates_ref[1:2, :]
    dlogits = jnp.where(
        label_rows == ids_first, dlogit, jnp.where(label_rows == ids_second, -dlogit, 0.0)
    ).astype(low)
    sums_send_ref[...] = dot(dlogits, normed_ref[...])

    def backward_chunk(c, ffn_term):
        lo, hi = c * chunk, (c + 1) * chunk
        block = at_chunk(c)
        line_take(1, c)
        dnormed = total_ref[1, block, :].astype(f32) + dot(dlogits[:, block], gains_low, ((0,), (0,)))
        residual = residual_ref[block, :]
        scale_two = rms_scale(residual)
        ffn_term = ffn_term + jnp.sum(dnormed * residual * scale_two, axis=0, keepdims=True)
        dres = cot_ref[block, :].astype(f32) + norm_back(dnormed, residual, scale_two, gain_two)
        dres_ref[block, :] = dres
        dres_low = dres.astype(low)
        dres_low_ref[block, :] = dres_low
        dcontext = dot(dres_low, wo_ref[...]).astype(low)
        flip = (
            lax.broadcasted_iota(jnp.int32, (chunk, chunk), 0)
            + lax.broadcasted_iota(jnp.int32, (chunk, chunk), 1)
            == chunk - 1
        )
        flip = jnp.where(flip, 1.0, 0.0).astype(low)
        first, second, third = [], [], []
        for h in range(heads):
            at = h * HEAD_DIM
            queries = qkv_ref[lo:hi, at : at + HEAD_DIM]
            keys = qkv_ref[0:hi, head_width + at : head_width + at + HEAD_DIM]
            values = qkv_ref[0:hi, 2 * head_width + at : 2 * head_width + at + HEAD_DIM]
            dctx = dcontext[:, at : at + HEAD_DIM]
            probs = probs_ref[h, lo:hi, 0:hi]
            weights = probs.astype(f32)
            dweights = dot(dctx, values, ((1,), (1,)))
            agreement = jnp.sum(weights * dweights, axis=-1, keepdims=True)
            dscores = (weights * (dweights - agreement)).astype(low)
            first.append((factor * dot(dscores, keys)).astype(low))
            dkeys = dot(dscores, queries, ((0,), (0,)))
            dvalues = dot(probs, dctx, ((0,), (0,)))
            if c < chunks - 1:
                dkeys = dkeys + dkeys_ref[h, 0:hi, :]
                dvalues = dvalues + dvalues_ref[h, 0:hi, :]
            if lo:
                dkeys_ref[h, 0:lo, :] = dkeys[0:lo]
                dvalues_ref[h, 0:lo, :] = dvalues[0:lo]
            second.append((factor * dkeys[lo:hi]).astype(low))
            third.append(dvalues[lo:hi].astype(low))
            flipped = dot(flip, dscores)
            if hi < token_count:
                flipped = jnp.concatenate([flipped, jnp.zeros((chunk, token_count - hi), f32)], axis=1)
            skewed = pltpu.roll(flipped, token_count - (hi - 1), 1, stride=1, stride_axis=0)
            line = jnp.sum(skewed, axis=0, keepdims=True)
            if c < chunks - 1:
                line = line + diagonal_ref[h : h + 1, :]
            diagonal_ref[h : h + 1, :] = line
        dqkv = jnp.concatenate(first + second + third, axis=1)
        dqkv_ref[block, :] = dqkv
        line_drain(1, c)
        part_ref[block, :] = dot(dqkv, wqkv_ref[...], ((1,), (1,))).astype(low)
        line_start(2, c)
        return ffn_term

    ffn_term = jnp.zeros((1, model_width), f32)
    for place, c in enumerate(order):
        ffn_term = backward_chunk(c, ffn_term)
        if place >= 1:
            line_serve(2, order[place - 1])

    for part in range(model_width // 256):
        block = slice(part * 256, (part + 1) * 256)
        terms_send_ref[block, :] = dot(normed_one_ref[:, block], dqkv_ref[...], ((0,), (0,))).astype(low)
        oterms_send_ref[block, :] = dot(dres_low_ref[:, block], context_ref[...], ((0,), (0,))).astype(low)
        if part == 0:
            line_serve(2, order[-1])
        if part == 1:
            line_flush(2)
    each_peer(lambda peer: start_all(term_copies(peer, me)))
    terms_ref[mine, :] = terms_send_ref[mine, :]
    oterms_ref[mine, :] = oterms_send_ref[mine, :]

    sums_send_ref[0:1, :] = ffn_term
    diagonal = diagonal_ref[0:heads, :]
    lanes = lax.broadcasted_iota(jnp.int32, (heads, model_width), 1)
    bias_rows = jnp.zeros((heads, model_width), f32)
    for b in range(NB):
        bucket_total = jnp.sum(jnp.where(wrap_bucket == b, diagonal, 0.0), axis=1, keepdims=True)
        bias_rows = jnp.where(lanes == b, bucket_total, bias_rows)
    sums_send_ref[2 : 2 + heads, :] = bias_rows
    each_peer(lambda peer: sums_copy(peer, me).start())
    sums_ref[me] = sums_send_ref[...]

    each_peer(lambda source: out_copy(source, source).wait_recv())
    for part in range(model_width // 256):
        block = slice(part * 256, (part + 1) * 256)
        mix_send_ref[block, :] = dot(out_ref[:, block], gated_ref[...], ((0,), (0,))).astype(low)
    side = level // 2
    end_level = side * (tensor_size - 1)
    middle_level = 1 + side
    away = [2 * (1 - side), 2 * (1 - side) + 1]

    def mix_at(target):
        return rows_at(target, column_width)

    def mix_copy(place, target, peer):
        return remote(
            mix_send_ref.at[mix_at(target)],
            mix_ref.at[place],
            z_sems.at[0, place],
            z_sems.at[1, place],
            "tensor",
            peer,
        )

    def mix_add(target, place):
        mix_send_ref[mix_at(target), :] = (
            mix_send_ref[mix_at(target), :].astype(f32) + mix_ref[place].astype(f32)
        ).astype(low)

    up_order = [away[0], away[1], middle_level]

    @pl.when(is_end)
    def _():
        for place, target in enumerate(up_order):
            mix_copy(place, target, near).start()

    attn_term = jnp.zeros((1, model_width), f32)
    for c in order:
        block = at_chunk(c)
        line_take(2, c)
        dnormed = total_ref[2, block, :].astype(f32)
        values = x_ref[block, :].astype(f32)
        scale_one = rms_scale(values)
        attn_term = attn_term + jnp.sum(dnormed * values * scale_one, axis=0, keepdims=True)
        dres_ref[block, :] = dres_ref[block, :] + norm_back(dnormed, values, scale_one, gain_one)

    late_send_ref[...] = jnp.broadcast_to(attn_term, late_send_ref.shape)
    each_peer(lambda peer: late_copy(peer, me).start())
    late_ref[me] = late_send_ref[...]

    for z in range(tensor_size):

        @pl.when(level == z)
        def _():
            input_out[...] = jnp.transpose(dres_ref[:, z * column_width : (z + 1) * column_width])

    @pl.when(is_middle)
    def _():
        for place in range(2):
            mix_copy(place, up_order[place], near).wait_recv()
            mix_add(up_order[place], place)
            mix_copy(3 + place, up_order[place], across).start()
        own_side = [2 * side, 2 * side + 1]
        for place in range(2):
            mix_copy(3 + place, own_side[place], across).wait_recv()
            mix_add(own_side[place], 3 + place)
        mix_copy(5, end_level, near).start()
        mix_copy(2, middle_level, near).wait_recv()
        mix_add(middle_level, 2)

    stores()[0].start()
    each_peer(lambda source: recv_all(term_copies(source, source)))
    reduced = terms_ref[0:block_rows, :].astype(f32)
    oreduced = oterms_ref[0:block_rows, :].astype(f32)
    for source in range(1, group_size):
        block = slice(source * block_rows, (source + 1) * block_rows)
        reduced = reduced + terms_ref[block, :].astype(f32)
        oreduced = oreduced + oterms_ref[block, :].astype(f32)
    for k in range(3):
        qkv_out[k] = reduced[:, k * head_width : (k + 1) * head_width]
    wo_out[...] = oreduced
    stores()[1].start()
    stores()[2].start()

    @pl.when(is_end)
    def _():
        mix_copy(5, level, near).wait_recv()
        mix_add(level, 5)

    mixture = mix_send_ref[mix_at(level), :].astype(f32)
    block_out[...] = (residual_t_ref[...] + mixture).astype(low)
    stores()[3].start()

    each_peer(lambda source: sums_copy(source, source).wait_recv())
    sums = sums_ref[0]
    for source in range(1, group_size):
        sums = sums + sums_ref[source]
    sums_out[...] = sums
    stores()[4].start()
    each_peer(lambda source: late_copy(source, source).wait_recv())
    late = late_ref[0]
    for source in range(1, group_size):
        late = late + late_ref[source]
    late_out[...] = late
    stores()[5].start()

    def drain(peer):
        late_copy(peer, me).wait_send()
        sent_all(weight_copies(peer, me, peer))
        cot_copy(peer, me).wait_send()
        row_copy(peer, me, shared, 0).wait_send()
        row_copy(peer, me, 0, 1).wait_send()
        hand_over(peer, shared).wait_send()
        back_copy(peer, me).wait_send()
        gate_copy(peer, me).wait_send()
        out_copy(peer, me).wait_send()
        sent_all(term_copies(peer, me))
        sums_copy(peer, me).wait_send()

    each_peer(drain)

    @pl.when(is_end)
    def _():
        for place, target in enumerate(up_order):
            mix_copy(place, target, near).wait_send()

    @pl.when(is_middle)
    def _():
        for place in range(2):
            mix_copy(3 + place, up_order[place], across).wait_send()
        mix_copy(5, end_level, near).wait_send()

    line_drain(1, None)
    for c in order:
        line_drain(2, c)
    for part in range(parts):
        grad_out(0, part).wait()
        grad_out(1, part).wait()
    for copy in stores():
        copy.wait()


def run_layer(group_size, tensor_size, capacity, x, q, k, v, o, small, bias, ids, cot, w_in, w_out):
    tokens, width = x.shape
    block_rows, head_width = q.shape
    heads = bias.shape[0]
    hidden = w_in.shape[1]
    slots = group_size * capacity
    low = jnp.bfloat16
    f32 = jnp.float32
    full = group_size * block_rows
    chunks = tokens // LANES
    column_width = width // tensor_size

    def shape(dims, dtype=low):
        return jax.ShapeDtypeStruct(dims, dtype)

    def room(*dims, dtype=low):
        return pltpu.VMEM(dims, dtype)

    hbm = pl.BlockSpec(memory_space=pl.ANY)
    dma = pltpu.SemaphoreType.DMA
    return pl.pallas_call(
        functools.partial(layer_kernel, group_size, tensor_size),
        out_shape=(
            shape((column_width, tokens)),
            shape((column_width, tokens), f32),
            shape((3, block_rows, head_width), f32),
            shape((block_rows, head_width), f32),
            shape((small.shape[0], width), f32),
            shape((8, width), f32),
            shape((width, hidden), f32),
            shape((hidden, width), f32),
        ),
        in_specs=[hbm] * 11,
        out_specs=(hbm,) * 8,
        scratch_shapes=[
            room(full, 3 * head_width),
            room(full, head_width),
            room(small.shape[0], width, dtype=f32),
            room(tokens, 3 * head_width),
            room(heads, tokens, tokens),
            room(tokens, head_width),
            room(tokens, width),
            room(tokens, width),
            room(tokens, width, dtype=f32),
            room(column_width, tokens, dtype=f32),
            room(slots, tokens),
            room(slots, tokens),
            room(slots, tokens),
            room(width // 256, tokens, 256),
            room(width // 256, slots, 256),
            room(slots, width + LANES),
            room(width, hidden),
            room(hidden, width),
            room(slots, hidden),
            room(slots, width),
            room(slots, hidden),
            room(2, width, width, dtype=f32),
            room(width // 256, slots, 256),
            room(slots, width + LANES),
            room(slots, width),
            room(slots, width),
            room(slots, width),
            room(slots, width),
            room(group_size, 16, capacity),
            room(group_size, 16, capacity),
            room(group_size, *small.shape),
            room(group_size, tokens, dtype=f32),
            room(8, tokens, dtype=f32),
            room(tokens, width),
            room(tokens, width),
            room(2, tokens, width),
            room(3, tokens, width),
            room(4, 16, tokens),
            room(tokens, width, dtype=f32),
            room(tokens, width),
            room(heads, tokens, HEAD_DIM, dtype=f32),
            room(heads, tokens, HEAD_DIM, dtype=f32),
            room(tokens, 3 * head_width),
            room(8, tokens, dtype=f32),
            room(full, 3 * head_width),
            room(full, 3 * head_width),
            room(full, head_width),
            room(full, head_width),
            room(width, tokens),
            room(6, column_width, tokens),
            room(small.shape[0], width, dtype=f32),
            room(group_size, small.shape[0], width, dtype=f32),
            room(8, width, dtype=f32),
            room(group_size, 8, width, dtype=f32),
            *[room(*a.shape, dtype=a.dtype) for a in (x, q, k, v, o, small, bias, ids, cot)],
            room(column_width, tokens),
            room(column_width, tokens, dtype=f32),
            room(3, block_rows, head_width, dtype=f32),
            room(block_rows, head_width, dtype=f32),
            room(small.shape[0], width, dtype=f32),
            room(8, width, dtype=f32),
            dma((9,)),
            dma((6,)),
            dma((6, group_size)),
            dma((6, group_size)),
            dma((18, group_size)),
            dma((3, 6, tokens // PIECE + 1)),
            dma((2, 6)),
            dma((18,)),
        ],
        compiler_params=pltpu.CompilerParams(
            collective_id=0, has_side_effects=True, vmem_limit_bytes=VMEM_BYTES
        ),
        name="layer",
    )(x, q, k, v, o, small, bias, ids, cot, w_in, w_out)


def finish_kernel(group_size, *refs):
    sources, targets = refs[:8], refs[8:20]
    held, built = refs[20:28], refs[28:36]
    in_sems, out_sems = refs[36:]
    me = lax.axis_index("dp")

    def pieces(src, dst, sems, at):
        count = 4 if at >= 6 else 1
        rows = src.shape[0] // count
        return [
            pltpu.make_async_copy(src.at[pl.ds(p * rows, rows)], dst.at[pl.ds(p * rows, rows)], sems.at[at, p])
            for p in range(count)
        ]

    taken = [pieces(src, dst, in_sems, at) for at, (src, dst) in enumerate(zip(sources, held))]
    for group in taken:
        for copy in group:
            copy.start()
    block, inputs, qkv, wo, sums, late, in_grad, out_grad = held
    q_o, k_o, v_o, attn_o, ffn_o, router_o, bias_o = built[:7]
    (block_out, input_out, q_out, k_out, v_out, wo_out, attn_out, ffn_out, router_out, bias_out, in_out, out_out) = targets
    given = []

    def give(src, dst, at):
        for copy in pieces(src, dst, out_sems, at):
            copy.start()
            given.append(copy)

    for at in range(6):
        for copy in taken[at]:
            copy.wait()
    give(block, block_out, 0)
    give(inputs, input_out, 1)
    for k, (src, dst) in enumerate(((q_o, q_out), (k_o, k_out), (v_o, v_out))):
        src[...] = qkv[k]
        give(src, dst, 2 + k)
    give(wo, wo_out, 5)
    for at, (src, dst) in ((6, (in_grad, in_out)), (7, (out_grad, out_out))):
        for p, copy in enumerate(taken[at]):
            copy.wait()
            out = pieces(src, dst, out_sems, at)[p]
            out.start()
            given.append(out)
    block_rows = wo.shape[0]
    heads, buckets = bias_o.shape
    features = sums.shape[1]
    shift = lax.rem((group_size - me) * block_rows, features)
    total = sums[...]
    bias_o[...] = total[2 : 2 + heads, :buckets]
    total = pltpu.roll(total, shift, 1)
    ffn_o[...] = total[0:1, :block_rows]
    router_o[...] = total[8:, :block_rows]
    attn_o[...] = pltpu.roll(late[...], shift, 1)[0:1, :block_rows]
    for k, (src, dst) in enumerate(((attn_o, attn_out), (ffn_o, ffn_out), (router_o, router_out), (bias_o, bias_out))):
        copy = pltpu.make_async_copy(src, dst, out_sems.at[8 + k, 0])
        copy.start()
        given.append(copy)
    for copy in given:
        copy.wait()


def finish(group_size, heads, buckets, *results):
    f32 = jnp.float32
    block, inputs, qkv, wo, sums, late, in_grad, out_grad = results
    block_rows = wo.shape[0]

    def shape(*dims):
        return jax.ShapeDtypeStruct(dims, f32)

    small = [(1, block_rows), (1, block_rows), (sums.shape[0] - 8, block_rows), (heads, buckets)]
    hbm = pl.BlockSpec(memory_space=pl.ANY)
    return pl.pallas_call(
        functools.partial(finish_kernel, group_size),
        out_shape=(
            jax.ShapeDtypeStruct(block.shape, block.dtype),
            shape(*inputs.shape),
            *[shape(*wo.shape)] * 4,
            *[shape(*dims) for dims in small],
            shape(*in_grad.shape),
            shape(*out_grad.shape),
        ),
        in_specs=[hbm] * 8,
        out_specs=(hbm,) * 12,
        scratch_shapes=[
            *[pltpu.VMEM(a.shape, a.dtype) for a in results],
            *[pltpu.VMEM(wo.shape, f32)] * 3,
            *[pltpu.VMEM(dims, f32) for dims in small],
            pltpu.VMEM((8, LANES), f32),
            pltpu.SemaphoreType.DMA((8, 4)),
            pltpu.SemaphoreType.DMA((12, 4)),
        ],
        compiler_params=pltpu.CompilerParams(vmem_limit_bytes=VMEM_BYTES),
        name="finish",
    )(*results)


def on_device_general(
    block_input,
    attn_gain,
    query_weight,
    key_weight,
    value_weight,
    output_weight,
    bias_table,
    ffn_gain,
    router_weight,
    expert_in,
    expert_out,
    expert_ids,
    out_cotangent,
):
    tensor_size = lax.axis_size("tensor")
    group_size = lax.axis_size("dp")
    tensor_index = lax.axis_index("tensor")
    own_expert = lax.axis_index("dp")
    token_count, model_width = block_input.shape
    column_width = model_width // tensor_size
    column_start = tensor_index * column_width
    expert_count = group_size * expert_in.shape[0]
    capacity = tensor_size * max(1, 3 * token_count // (5 * expert_count))
    slot_rows = expert_count * capacity
    seq_count = token_count // SEQ_LEN
    head_local = bias_table.shape[0]
    head_width = head_local * HEAD_DIM
    block_rows = query_weight.shape[0]
    low = jnp.bfloat16

    def own_columns(matrix):
        return lax.dynamic_slice_in_dim(matrix, column_start, column_width, 1)

    packed = jnp.concatenate(
        [
            query_weight,
            key_weight,
            value_weight,
            output_weight,
            router_weight,
            attn_gain[:, None],
            ffn_gain[:, None],
        ],
        axis=1,
    )
    packed = lax.all_gather(packed, "dp", axis=0, tiled=True)

    labels = jnp.arange(expert_count, dtype=jnp.int32)
    flat_ids = expert_ids.reshape(-1)
    ids_onehot = (flat_ids[:, None] == labels[None, :]).astype(jnp.int32)
    pair_rows = lax.broadcasted_iota(jnp.int32, (2 * token_count, 2 * token_count), 0)
    pair_cols = lax.broadcasted_iota(jnp.int32, (2 * token_count, 2 * token_count), 1)
    before = (pair_cols < pair_rows).astype(low)
    earlier = dot(before, ids_onehot.astype(low)).astype(jnp.int32)
    slot_index = jnp.sum(earlier * ids_onehot, axis=1)
    places = (flat_ids * capacity + slot_index).reshape(token_count, 2)
    place_rows = jnp.arange(slot_rows, dtype=jnp.int32)
    at_first = places[:, 0][None, :] == place_rows[:, None]
    at_second = places[:, 1][None, :] == place_rows[:, None]
    map_first = at_first.astype(low)
    map_second = at_second.astype(low)
    map_both = (at_first | at_second).astype(low)

    ids_low = jnp.broadcast_to(expert_ids.astype(low)[:, :, None], (token_count, 2, LANES))
    cot_source = jnp.concatenate(
        [
            jnp.concatenate([out_cotangent, ids_low[:, 1]], axis=1),
            jnp.concatenate([out_cotangent, ids_low[:, 0]], axis=1),
        ],
        axis=0,
    )
    cot_parcel = dot(jnp.concatenate([map_first, map_second], axis=1), cot_source).astype(low)
    packed, cot_parcel = lax.optimization_barrier((packed, cot_parcel))
    cot_arrived = exchange(
        cot_parcel.reshape(expert_count, capacity, model_width + LANES)
    ).reshape(slot_rows, model_width + LANES)
    cot_rows = cot_arrived[:, :model_width].astype(jnp.float32)
    other_ids = cot_arrived[:, model_width].astype(jnp.int32)

    qkv_full = packed[:, : 3 * head_width]
    output_full = packed[:, 3 * head_width : 4 * head_width]
    at = 4 * head_width
    router_full = packed[:, at : at + expert_count]
    gain_one = packed[:, at + expert_count].astype(jnp.float32)
    gain_two = packed[:, at + expert_count + 1].astype(jnp.float32)
    inputs_f = block_input.astype(jnp.float32)
    scale_one = rms_scale(inputs_f)
    normed_one = (inputs_f * scale_one * gain_one).astype(low)
    qkv = dot(normed_one, qkv_full).astype(low)
    bucket_vec = bucket_vector_at(jnp.arange(SEQ_LEN, dtype=jnp.int32), NB)
    bucket_labels = jnp.arange(NB, dtype=jnp.int32)
    wrap = (SEQ_LEN - jnp.arange(SEQ_LEN, dtype=jnp.int32)) % SEQ_LEN
    wrapped_onehot = bucket_vector_at(wrap, NB)[None, :] == bucket_labels[:, None]
    wrapped = jnp.sum(
        jnp.where(wrapped_onehot[None], bias_table[:, :, None], 0.0), axis=1
    )
    context, probs = attend_forward(qkv, wrapped, seq_count, head_local)
    attn_part = dot(context, output_full, ((1,), (1,))).astype(low)
    attn_out = lax.psum(attn_part, "tensor").astype(jnp.float32)
    residual = inputs_f + attn_out
    scale_two = rms_scale(residual)
    normed_two = (residual * scale_two * gain_two).astype(low)

    logits = dot(normed_two, router_full)
    picked = (expert_ids[:, :, None] == labels[None, None, :]).astype(jnp.float32)
    chosen = jnp.sum(picked * logits[:, None, :], axis=2)
    first_gate = jax.nn.sigmoid(chosen[:, 0] - chosen[:, 1])
    second_gate = 1.0 - first_gate

    weight_in = expert_in[0]
    weight_out = expert_out[0]
    parcel = dot(map_both, normed_two).astype(low)
    expert_rows = exchange(parcel.reshape(expert_count, capacity, model_width)).reshape(
        slot_rows, model_width
    )
    pre_act = dot(expert_rows, weight_in)
    active, pullback = jax.vjp(jax.nn.gelu, pre_act)
    active = active.astype(low)
    owner_out = dot(active, weight_out)
    owner_logits = dot(expert_rows, router_full)
    own_logit = jnp.sum(
        jnp.where(labels[None, :] == own_expert, owner_logits, 0.0), axis=1
    )
    other_logit = jnp.sum(
        jnp.where(labels[None, :] == other_ids[:, None], owner_logits, 0.0), axis=1
    )
    row_gate = jax.nn.sigmoid(own_logit - other_logit)
    expert_drows = (row_gate[:, None] * cot_rows).astype(low)
    dpre = pullback(dot(expert_drows, weight_out, ((1,), (1,))))[0].astype(low)
    owner_back = dot(dpre, weight_in, ((1,), (1,))).astype(low)
    gate_part = jnp.sum(cot_rows * owner_out, axis=1, keepdims=True).astype(low)
    back_parcel = jnp.concatenate(
        [owner_back, jnp.broadcast_to(gate_part, (slot_rows, LANES))], axis=1
    )
    back_rows = exchange(
        back_parcel.reshape(group_size, capacity, model_width + LANES)
    ).reshape(slot_rows, model_width + LANES)
    out_rows = exchange(
        owner_out.astype(low).reshape(group_size, capacity, model_width)
    ).reshape(slot_rows, model_width)
    out_grad = dot(active, expert_drows, ((0,), (0,)))
    in_grad = dot(expert_rows, dpre, ((0,), (0,)))

    dnormed_part = dot(map_both, back_rows[:, :model_width], ((0,), (0,)))
    gate_diff_part = dot(map_first - map_second, back_rows[:, model_width:], ((0,), (0,)))
    gate_rows = -(-token_count // model_width)
    gate_line = jnp.pad(gate_diff_part[:, 0], (0, gate_rows * model_width - token_count))
    summed = lax.psum(
        jnp.concatenate(
            [dnormed_part, gate_line.reshape(gate_rows, model_width)], axis=0
        ).astype(low),
        "tensor",
    ).astype(jnp.float32)
    gate_diff = summed[token_count:].reshape(-1)[:token_count]
    mixture_part = first_gate[:, None] * dot(map_first, out_rows, ((0,), (0,)))
    mixture_part = mixture_part + second_gate[:, None] * dot(
        map_second, out_rows, ((0,), (0,))
    )
    mixture_parts = mixture_part.astype(low).reshape(token_count, tensor_size, column_width)
    mixture_parts = jnp.swapaxes(mixture_parts, 0, 1)

    dlogit = gate_diff * first_gate * second_gate
    signed = jnp.stack([dlogit, -dlogit], axis=1)
    dlogits = jnp.sum(picked * signed[:, :, None], axis=1).astype(low)
    router_term = dot(normed_two, dlogits, ((0,), (0,)))
    dnormed_two = summed[:token_count] + dot(dlogits, router_full, ((1,), (1,)))
    ffn_term = jnp.sum(dnormed_two * residual * scale_two, axis=0)
    cot_f = out_cotangent.astype(jnp.float32)
    dresidual = cot_f + norm_back(dnormed_two, residual, scale_two, gain_two)
    dres_low = dresidual.astype(low)
    mixture_parts, dres_low = lax.optimization_barrier((mixture_parts, dres_low))
    mixture_parts = lax.all_to_all(
        mixture_parts, "tensor", split_axis=0, concat_axis=0, tiled=True
    )

    output_term = dot(dres_low, context, ((0,), (0,)))
    dcontext = dot(dres_low, output_full).astype(low)
    dqkv, diagonal = attend_backward(qkv, probs, dcontext, seq_count, head_local)
    reverse_onehot = (bucket_vec[::-1][:, None] == bucket_labels[None, :]).astype(jnp.float32)
    bias_term = jnp.dot(
        jnp.sum(diagonal, axis=0),
        reverse_onehot,
        precision=lax.Precision.HIGHEST,
        preferred_element_type=jnp.float32,
    )
    dnormed_part = dot(dqkv, qkv_full, ((1,), (1,))).astype(low)
    dnormed_part, mixture_parts = lax.optimization_barrier((dnormed_part, mixture_parts))
    dnormed_one = lax.psum(dnormed_part, "tensor").astype(jnp.float32)
    qkv_term = dot(normed_one, dqkv, ((0,), (0,)))
    bias_count = bias_term.size
    bias_cols = -(-bias_count // block_rows)
    bias_block = jnp.pad(bias_term.reshape(-1), (0, bias_cols * block_rows - bias_count))
    bias_block = jnp.tile(bias_block.reshape(block_rows, bias_cols), (group_size, 1))
    terms = jnp.concatenate(
        [qkv_term, output_term, router_term, ffn_term[:, None], bias_block],
        axis=1,
    ).astype(low)
    term_width = terms.shape[1]
    arrived = exchange(terms.reshape(group_size, block_rows, term_width))
    arrived, dnormed_one = lax.optimization_barrier((arrived, dnormed_one))
    mixture = jnp.sum(mixture_parts.astype(jnp.float32), axis=0)
    block_output = (own_columns(residual) + mixture).astype(low)
    reduced = jnp.sum(arrived.astype(jnp.float32), axis=0)
    at = 4 * head_width
    grads = [reduced[:, k * head_width : (k + 1) * head_width] for k in range(4)]
    router_grad = reduced[:, at : at + expert_count]
    at = at + expert_count
    bias_grad = reduced[:, at + 1 :].reshape(-1)[:bias_count].reshape(bias_term.shape)
    attn_term = jnp.sum(dnormed_one * inputs_f * scale_one, axis=0)
    attn_gain_grad = jnp.sum(exchange(attn_term.reshape(group_size, block_rows)), axis=0)
    first_back = norm_back(dnormed_one, inputs_f, scale_one, gain_one)
    input_grad = own_columns(dresidual + first_back)
    return (
        block_output,
        input_grad,
        attn_gain_grad,
        grads[0],
        grads[1],
        grads[2],
        grads[3],
        bias_grad,
        reduced[:, at],
        router_grad,
        in_grad[None],
        out_grad[None],
    )


def on_device(
    block_input,
    attn_gain,
    query_weight,
    key_weight,
    value_weight,
    output_weight,
    bias_table,
    ffn_gain,
    router_weight,
    expert_in,
    expert_out,
    expert_ids,
    out_cotangent,
):
    tensor_size = lax.axis_size("tensor")
    group_size = lax.axis_size("dp")
    token_count = block_input.shape[0]
    block_rows = query_weight.shape[0]
    head_local = bias_table.shape[0]
    low = jnp.bfloat16
    capacity = tensor_size * max(1, 3 * token_count // (5 * group_size))
    capacity = -(-capacity // 16) * 16
    small = jnp.concatenate(
        [attn_gain[None, :], ffn_gain[None, :], jnp.zeros((6, block_rows), low), router_weight.T],
        axis=0,
    )
    small = jnp.pad(small, ((0, 0), (0, LANES - block_rows)))
    results = run_layer(
        group_size,
        tensor_size,
        capacity,
        block_input,
        query_weight,
        key_weight,
        value_weight,
        output_weight,
        small,
        bias_table,
        expert_ids.T,
        out_cotangent,
        expert_in[0],
        expert_out[0],
    )
    block, inputs, query, key, value, output, attn, ffn, router, bias, in_grad, out_grad = finish(
        group_size, head_local, NB, *results
    )
    return (
        block.T,
        inputs.T,
        attn[0],
        query,
        key,
        value,
        output,
        bias,
        ffn[0],
        router.T,
        in_grad[None],
        out_grad[None],
    )


def choose(mesh):
    def run(*arrays):
        tokens, width = arrays[0].shape
        block_rows = arrays[2].shape[0]
        hidden = arrays[9].shape[2]
        group_size = mesh.shape["dp"]
        fits = (
            block_rows % 16 == 0
            and block_rows <= LANES
            and arrays[9].shape[0] == 1
            and mesh.shape["tensor"] == 4
            and group_size == 8
            and arrays[6].shape[0] <= 6
            and tokens == SEQ_LEN
            and hidden == width
            and width % 256 == 0
            and width == 3 * 256
        )
        return (on_device if fits else on_device_general)(*arrays)

    return run


def solution(mesh):
    placed = (
        P("dp", None),
        P("dp"),
        P("dp", "tensor"),
        P("dp", "tensor"),
        P("dp", "tensor"),
        P("dp", "tensor"),
        P("tensor", None),
        P("dp"),
        P("dp", None),
        P("dp", None, "tensor"),
        P("dp", "tensor", None),
        P("dp", None),
        P("dp", None),
    )
    return jax.shard_map(
        choose(mesh),
        mesh=mesh,
        in_specs=placed,
        out_specs=(
            P("dp", "tensor"),
            P("dp", "tensor"),
            P("dp"),
            P("dp", "tensor"),
            P("dp", "tensor"),
            P("dp", "tensor"),
            P("dp", "tensor"),
            P("tensor", None),
            P("dp"),
            P("dp", None),
            P("dp", None, "tensor"),
            P("dp", "tensor", None),
        ),
        check_vma=False,
    )
```

```python
import functools
import math

import jax
import jax.numpy as jnp
from jax import lax
from jax.experimental import pallas as pl
from jax.experimental.pallas import tpu as pltpu
from jax.sharding import PartitionSpec as P

HEAD_DIM = 64
NB = 32
SEQ_LEN = 512
LANES = 128
VMEM_BYTES = 63 * 1024 * 1024
PIECE = 32
LAG = 4


EPSILON = 1e-06
MASKED = -1e30


def bucket_vector_at(steps_ids, bucket_count):
    exact_count = bucket_count // 2
    distant = jnp.full(steps_ids.shape, exact_count, jnp.int32)
    for level_index in range(1, bucket_count - exact_count):
        border = int(math.ceil(exact_count * 8.0 ** (level_index / (bucket_count - exact_count))))
        distant = distant + (steps_ids >= border).astype(jnp.int32)
    return jnp.where(steps_ids < exact_count, steps_ids, distant)


def norm_back(dnormed, row_values, row_scale, gain_row):
    inner_mean = jnp.mean(gain_row * dnormed * row_values, axis=-1, keepdims=True)
    return row_scale * (gain_row * dnormed - row_values * row_scale * row_scale * inner_mean)


def rms_scale(matrix):
    return lax.rsqrt(jnp.mean(matrix * matrix, axis=-1, keepdims=True) + EPSILON)


def dot(left, right, dims=((1,), (0,))):
    return lax.dot_general(left, right, (dims, ((), ())), preferred_element_type=jnp.float32)


def forward_kernel(qkv_ref, wrapped_ref, context_ref, probs_ref):
    length = qkv_ref.shape[0]
    heads = probs_ref.shape[0]
    width = heads * HEAD_DIM
    factor = HEAD_DIM ** (-0.5)
    rows = lax.broadcasted_iota(jnp.int32, (length, length), 0)
    cols = lax.broadcasted_iota(jnp.int32, (length, length), 1)
    causal = rows >= cols
    for h in range(heads):
        lo, hi = h * HEAD_DIM, (h + 1) * HEAD_DIM
        queries = qkv_ref[:, lo:hi]
        keys = qkv_ref[:, width + lo : width + hi]
        values = qkv_ref[:, 2 * width + lo : 2 * width + hi]
        bias = jnp.broadcast_to(wrapped_ref[h : h + 1, :], (length, length))
        bias = pltpu.roll(bias, 0, 1, stride=1, stride_axis=0)
        scores = jnp.where(causal, dot(queries, keys, ((1,), (1,))) * factor + bias, MASKED)
        row_max = jnp.max(scores, axis=-1, keepdims=True)
        row_total = jnp.sum(jnp.exp(scores - row_max), axis=-1, keepdims=True)
        probs = jnp.exp(scores - (row_max + jnp.log(row_total))).astype(jnp.bfloat16)
        probs_ref[h] = probs
        context_ref[:, lo:hi] = dot(probs, values).astype(jnp.bfloat16)


def backward_kernel(qkv_ref, probs_ref, dcontext_ref, dqkv_ref, diagonal_ref):
    length = qkv_ref.shape[0]
    heads = probs_ref.shape[0]
    width = heads * HEAD_DIM
    factor = HEAD_DIM ** (-0.5)
    rows = lax.broadcasted_iota(jnp.int32, (length, length), 0)
    cols = lax.broadcasted_iota(jnp.int32, (length, length), 1)
    flip = (rows + cols == length - 1).astype(jnp.float32).astype(jnp.bfloat16)
    for h in range(heads):
        lo, hi = h * HEAD_DIM, (h + 1) * HEAD_DIM
        queries = qkv_ref[:, lo:hi]
        keys = qkv_ref[:, width + lo : width + hi]
        values = qkv_ref[:, 2 * width + lo : 2 * width + hi]
        dcontext = dcontext_ref[:, lo:hi]
        probs = probs_ref[h]
        weights = probs.astype(jnp.float32)
        dweights = dot(dcontext, values, ((1,), (1,)))
        agreement = jnp.sum(weights * dweights, axis=-1, keepdims=True)
        dscores = (weights * (dweights - agreement)).astype(jnp.bfloat16)
        dqkv_ref[:, lo:hi] = (factor * dot(dscores, keys)).astype(jnp.bfloat16)
        dqkv_ref[:, width + lo : width + hi] = (
            factor * dot(dscores, queries, ((0,), (0,)))
        ).astype(jnp.bfloat16)
        dqkv_ref[:, 2 * width + lo : 2 * width + hi] = dot(
            probs, dcontext, ((0,), (0,))
        ).astype(jnp.bfloat16)
        skewed = pltpu.roll(dot(flip, dscores), 0, 1, stride=1, stride_axis=0)
        diagonal_ref[h : h + 1, :] = jnp.sum(skewed, axis=0, keepdims=True)


def attend_forward(qkv, wrapped, seq_count, heads):
    width = heads * HEAD_DIM
    return pl.pallas_call(
        forward_kernel,
        grid=(seq_count,),
        out_shape=(
            jax.ShapeDtypeStruct((seq_count * SEQ_LEN, width), jnp.bfloat16),
            jax.ShapeDtypeStruct((seq_count, heads, SEQ_LEN, SEQ_LEN), jnp.bfloat16),
        ),
        in_specs=[
            pl.BlockSpec((SEQ_LEN, 3 * width), lambda s: (s, 0)),
            pl.BlockSpec((heads, SEQ_LEN), lambda s: (0, 0)),
        ],
        out_specs=(
            pl.BlockSpec((SEQ_LEN, width), lambda s: (s, 0)),
            pl.BlockSpec((None, heads, SEQ_LEN, SEQ_LEN), lambda s: (s, 0, 0, 0)),
        ),
        name="attend_forward",
    )(qkv, wrapped)


def attend_backward(qkv, probs, dcontext, seq_count, heads):
    width = heads * HEAD_DIM
    return pl.pallas_call(
        backward_kernel,
        grid=(seq_count,),
        out_shape=(
            jax.ShapeDtypeStruct((seq_count * SEQ_LEN, 3 * width), jnp.bfloat16),
            jax.ShapeDtypeStruct((seq_count, heads, SEQ_LEN), jnp.float32),
        ),
        in_specs=[
            pl.BlockSpec((SEQ_LEN, 3 * width), lambda s: (s, 0)),
            pl.BlockSpec((None, heads, SEQ_LEN, SEQ_LEN), lambda s: (s, 0, 0, 0)),
            pl.BlockSpec((SEQ_LEN, width), lambda s: (s, 0)),
        ],
        out_specs=(
            pl.BlockSpec((SEQ_LEN, 3 * width), lambda s: (s, 0)),
            pl.BlockSpec((None, heads, SEQ_LEN), lambda s: (s, 0, 0)),
        ),
        name="attend_backward",
    )(qkv, probs, dcontext)


def exchange(parcel):
    return lax.all_to_all(parcel, "dp", split_axis=0, concat_axis=0, tiled=True)


def remote(src, dst, send_sem, recv_sem, axis, index):
    return pltpu.make_async_remote_copy(
        src_ref=src,
        dst_ref=dst,
        send_sem=send_sem,
        recv_sem=recv_sem,
        device_id={axis: index},
        device_id_type=pl.DeviceIdType.MESH,
    )


def rows_at(index, count):
    return pl.ds(pl.multiple_of(index * count, count), count)


def gelu_both(u):
    slope = math.sqrt(2.0 / math.pi)
    cubic = 0.044715
    square = u * u
    t = jnp.tanh(slope * u * (1.0 + cubic * square))
    half = 0.5 + 0.5 * t
    value = u * half
    grad = half + 0.5 * u * (1.0 - t * t) * (slope * (1.0 + 3.0 * cubic * square))
    return value, grad


def layer_kernel(
    group_size,
    tensor_size,
    x_hbm,
    q_hbm,
    k_hbm,
    v_hbm,
    o_hbm,
    attn_gain_hbm,
    ffn_gain_hbm,
    router_hbm,
    bias_hbm,
    ids_hbm,
    cot_hbm,
    win_hbm,
    wout_hbm,
    block_hbm_out,
    input_hbm_out,
    qkv_hbm_out,
    wo_hbm_out,
    sums_hbm_out,
    late_hbm_out,
    in_grad_hbm,
    out_grad_hbm,
    wqkv_ref,
    wo_ref,
    gains_ref,
    qkv_ref,
    probs_ref,
    context_ref,
    normed_one_ref,
    normed_ref,
    residual_ref,
    residual_t_ref,
    both_ref,
    signed_ref,
    gated_ref,
    strips_ref,
    rows_ref,
    cots_ref,
    win_ref,
    wout_ref,
    active_ref,
    drows_ref,
    dpre_ref,
    grad_ref,
    send_ref,
    cot_send_ref,
    back_send_ref,
    back_ref,
    out_send_ref,
    out_ref,
    gate_send_ref,
    gate_ref,
    small_buf,
    code_ref,
    gates_ref,
    part_ref,
    near_ref,
    middle_ref,
    total_ref,
    gate_line_ref,
    dres_ref,
    dres_low_ref,
    dkeys_ref,
    dvalues_ref,
    dqkv_ref,
    diagonal_ref,
    terms_send_ref,
    terms_ref,
    oterms_send_ref,
    oterms_ref,
    pair_ref,
    opair_ref,
    mix_send_ref,
    mix_ref,
    sums_send_ref,
    sums_ref,
    late_send_ref,
    late_ref,
    x_ref,
    q_ref,
    k_ref,
    v_ref,
    o_ref,
    attn_gain_ref,
    ffn_gain_ref,
    router_ref,
    bias_ref,
    ids_ref,
    cot_ref,
    block_out,
    input_out,
    qkv_out,
    wo_out,
    sums_out,
    late_out,
    load_sems,
    store_sems,
    row_sems,
    t_sems,
    w_sems,
    a2a_sems,
    line_sems,
    z_sems,
    local_sems,
):
    me = lax.axis_index("dp")
    level = lax.axis_index("tensor")
    token_count, model_width = x_ref.shape
    experts = group_size
    capacity = both_ref.shape[0] // group_size
    half = lax.rem(level, 2)
    strip = 256
    block_rows, head_width = q_ref.shape
    heads = bias_ref.shape[0]
    column_width = model_width // tensor_size
    low = jnp.bfloat16
    f32 = jnp.float32
    near = level + 1 - 2 * lax.rem(level, 2)
    across = tensor_size - 1 - level
    is_end = jnp.logical_or(level == 0, level == tensor_size - 1)
    is_middle = jnp.logical_not(is_end)
    chip = me // 2
    core = lax.rem(me, 2)
    chips = group_size // 2
    chunk = LANES
    chunks = token_count // chunk
    factor = HEAD_DIM ** (-0.5)

    def peer_of(j):
        other_chip = lax.rem(chip - j // 2 + chips, chips)
        return 2 * other_chip + lax.rem(core + j, 2)

    def each_peer(body):
        def step(j, carry):
            body(peer_of(j))
            return carry

        lax.fori_loop(1, group_size, step, 0)

    def load_in():
        return pltpu.make_async_copy(win_hbm, win_ref, local_sems.at[0])

    def load_out():
        return pltpu.make_async_copy(wout_hbm, wout_ref, local_sems.at[1])

    def loads(first, last):
        pairs = [
            (q_hbm, q_ref),
            (k_hbm, k_ref),
            (v_hbm, v_ref),
            (o_hbm, o_ref),
            (attn_gain_hbm, attn_gain_ref),
            (ffn_gain_hbm, ffn_gain_ref),
            (router_hbm, router_ref),
            (ids_hbm, ids_ref),
            (bias_hbm, bias_ref),
            (cot_hbm, cot_ref),
            (x_hbm, x_ref),
        ]
        return [
            pltpu.make_async_copy(src, dst, load_sems.at[place])
            for place, (src, dst) in enumerate(pairs)
            if first <= place < last
        ]

    for copy in loads(0, 11):
        copy.start()
    load_in().start()
    load_out().start()

    def stores():
        pairs = [
            (input_out, input_hbm_out),
            (qkv_out, qkv_hbm_out),
            (wo_out, wo_hbm_out),
            (block_out, block_hbm_out),
            (sums_out, sums_hbm_out),
            (late_out, late_hbm_out),
        ]
        return [
            pltpu.make_async_copy(src, dst, store_sems.at[place])
            for place, (src, dst) in enumerate(pairs)
        ]

    barrier = pltpu.get_barrier_semaphore()
    each_peer(
        lambda peer: pl.semaphore_signal(
            barrier, inc=1, device_id={"dp": peer}, device_id_type=pl.DeviceIdType.MESH
        )
    )

    def greet(step, carry):
        other = lax.rem(level + step, tensor_size)
        pl.semaphore_signal(
            barrier, inc=1, device_id={"tensor": other}, device_id_type=pl.DeviceIdType.MESH
        )
        return carry

    lax.fori_loop(1, tensor_size, greet, 0)
    mine = rows_at(me, block_rows)
    for copy in loads(0, 7):
        copy.wait()
    wqkv_ref[mine, :] = jnp.concatenate([q_ref[...], k_ref[...], v_ref[...]], axis=1)
    wo_ref[mine, :] = o_ref[...]
    slab = jnp.concatenate(
        [
            attn_gain_ref[...].astype(f32),
            ffn_gain_ref[...].astype(f32),
            jnp.zeros((6, block_rows), f32),
            router_ref[...].astype(f32),
        ],
        axis=0,
    )
    slab = jnp.concatenate([slab, jnp.zeros((slab.shape[0], LANES - block_rows), f32)], axis=1)
    small_buf[me] = slab.astype(low)

    pl.semaphore_wait(barrier, group_size + tensor_size - 2)

    sibling = 2 * chip + 1 - core

    def weight_copies(peer, source, slot):
        block = rows_at(source, block_rows)
        return [
            remote(wqkv_ref.at[block], wqkv_ref.at[block], w_sems.at[0, slot], w_sems.at[1, source], "dp", peer),
            remote(wo_ref.at[block], wo_ref.at[block], w_sems.at[2, slot], w_sems.at[3, source], "dp", peer),
            remote(small_buf.at[source], small_buf.at[source], w_sems.at[4, slot], w_sems.at[5, source], "dp", peer),
        ]

    def each_chip(body):
        def step(j, carry):
            body(lax.rem(chip + j, chips))
            return carry

        lax.fori_loop(1, chips, step, 0)

    def start_all(copies):
        for copy in copies:
            copy.start()

    def recv_all(copies):
        for copy in copies:
            copy.wait_recv()

    def sent_all(copies):
        for copy in copies:
            copy.wait_send()

    def send_weights(other):
        peer = 2 * other + core
        start_all(weight_copies(peer, me, peer))

    each_chip(send_weights)
    start_all(weight_copies(sibling, me, sibling))

    def block_copy(kind, src, dst, peer, source, count):
        return remote(
            src.at[rows_at(peer, count)],
            dst.at[rows_at(source, count)],
            a2a_sems.at[2 * kind, peer],
            a2a_sems.at[2 * kind + 1, source],
            "dp",
            peer,
        )

    def cot_copy(peer, source):
        return block_copy(0, cot_send_ref, cots_ref, peer, source, capacity)

    def row_copy(peer, source, strip_index, place):
        return remote(
            send_ref.at[strip_index, rows_at(peer, capacity)],
            rows_ref.at[strip_index, rows_at(source, capacity)],
            row_sems.at[2 * place, peer],
            row_sems.at[2 * place + 1, source],
            "dp",
            peer,
        )

    def hand_over(source, strip_index):
        block = rows_ref.at[strip_index, rows_at(source, capacity)]
        return remote(block, block, row_sems.at[4, source], row_sems.at[5, source], "tensor", near)

    def each_source(body):
        def step(j, carry):
            other_chip = lax.rem(chip + j // 2, chips)
            body(2 * other_chip + lax.rem(core + j, 2))
            return carry

        lax.fori_loop(1, group_size, step, 0)

    def back_copy(peer, source):
        return block_copy(2, back_send_ref, back_ref, peer, source, capacity)

    def out_copy(peer, source):
        return block_copy(3, out_send_ref, out_ref, peer, source, capacity)

    def pair_copies(place):
        block = rows_at(2 * place + 1 - core, block_rows)
        return [
            remote(terms_send_ref.at[block], pair_ref.at[place], t_sems.at[0, place], t_sems.at[1, place], "dp", sibling),
            remote(oterms_send_ref.at[block], opair_ref.at[place], t_sems.at[2, place], t_sems.at[3, place], "dp", sibling),
        ]

    def term_copies(target, source):
        peer = 2 * target + core
        block = rows_at(peer, block_rows)
        landing = rows_at(source, block_rows)
        return [
            remote(terms_send_ref.at[block], terms_ref.at[landing], t_sems.at[4, target], t_sems.at[5, source], "dp", peer),
            remote(oterms_send_ref.at[block], oterms_ref.at[landing], t_sems.at[6, target], t_sems.at[7, source], "dp", peer),
        ]

    def gate_copy(peer, source):
        return remote(
            gate_send_ref.at[peer], gate_ref.at[source], a2a_sems.at[12, peer], a2a_sems.at[13, source], "dp", peer
        )

    def late_copy(peer, source):
        return remote(
            late_send_ref, late_ref.at[source], a2a_sems.at[16, peer], a2a_sems.at[17, source], "dp", peer
        )

    def sums_copy(peer, source):
        return remote(
            sums_send_ref, sums_ref.at[source], a2a_sems.at[14, peer], a2a_sems.at[15, source], "dp", peer
        )

    for copy in loads(7, 11):
        copy.wait()
    ids_first = ids_ref[0:1, :]
    ids_second = ids_ref[1:2, :]
    labels = lax.broadcasted_iota(jnp.int32, (experts, token_count), 0)
    member = jnp.logical_or(labels == ids_first, labels == ids_second)
    tokens_r = lax.broadcasted_iota(jnp.int32, (token_count, token_count), 0)
    tokens_c = lax.broadcasted_iota(jnp.int32, (token_count, token_count), 1)
    upper = jnp.where(tokens_r < tokens_c, 1.0, 0.0).astype(low)
    counted = dot(jnp.where(member, 1.0, 0.0).astype(low), upper)
    code_ref[...] = jnp.where(member, counted, -1.0)
    slots = lax.broadcasted_iota(jnp.int32, (capacity, token_count), 0).astype(f32)
    id_total = jnp.broadcast_to((ids_first + ids_second).astype(f32), (LANES, token_count)).astype(low)

    def make_maps(expert, carry):
        block = rows_at(expert, capacity)
        hit = slots == code_ref[pl.ds(expert, 1), :]
        sign = jnp.where(ids_first == expert, 1.0, -1.0)
        both = jnp.where(hit, 1.0, 0.0).astype(low)
        both_ref[block, :] = both
        signed_ref[block, :] = jnp.where(hit, sign, 0.0).astype(low)
        cot_send_ref[block, :model_width] = dot(both, cot_ref[...]).astype(low)
        cot_send_ref[block, model_width:] = dot(both, id_total, ((1,), (1,))).astype(low)
        return carry

    lax.fori_loop(0, experts, make_maps, 0)

    inputs_f = x_ref[...].astype(f32)
    scaled = inputs_f * rms_scale(inputs_f)

    lane = lax.broadcasted_iota(jnp.int32, (heads, token_count), 1)
    wrap_bucket = bucket_vector_at(jnp.where(lane == 0, 0, token_count - lane), NB)
    wrapped = jnp.zeros((heads, token_count), f32)
    for b in range(NB):
        wrapped = jnp.where(wrap_bucket == b, bias_ref[:, b : b + 1], wrapped)

    def pass_on(other):
        source = 2 * other + core
        recv_all(weight_copies(sibling, source, source))
        start_all(weight_copies(sibling, source, 2 * other + 1 - core))

    def take_passed(other):
        source = 2 * other + 1 - core
        recv_all(weight_copies(sibling, source, source))

    each_chip(pass_on)
    recv_all(weight_copies(sibling, sibling, sibling))
    each_chip(take_passed)
    each_peer(lambda peer: cot_copy(peer, me).start())

    gains = jnp.zeros(gains_ref.shape, f32)
    for source in range(group_size):
        slab = jnp.concatenate(
            [small_buf[source].astype(f32), jnp.zeros((gains.shape[0], model_width - LANES), f32)], axis=1
        )
        gains = gains + (pltpu.roll(slab, source * block_rows, 1) if source else slab)
    gains_ref[...] = gains
    gain_one = gains_ref[0:1, :]
    gain_two = gains_ref[1:2, :]
    normed_one_ref[...] = (scaled * gain_one).astype(low)
    qkv_ref[...] = dot(normed_one_ref[...], wqkv_ref[...]).astype(low)

    def at_chunk(c):
        return slice(c * chunk, (c + 1) * chunk)

    per_chunk = chunk // PIECE
    pieces_all = chunks * per_chunk

    def at_piece(i):
        return slice(i * PIECE, (i + 1) * PIECE)

    def pieces_of(c):
        return [None] if c is None else range(c * per_chunk, (c + 1) * per_chunk)

    def line_copy(r, i, hop):
        at = pieces_all if i is None else i
        if hop == 0:
            peer = near
            src, dst = (
                (gate_line_ref.at[0], gate_line_ref.at[1])
                if i is None
                else (part_ref.at[at_piece(i)], near_ref.at[at_piece(i)])
            )
        elif hop == 1:
            peer = across
            src, dst = (
                (gate_line_ref.at[0], gate_line_ref.at[2])
                if i is None
                else (part_ref.at[at_piece(i)], middle_ref.at[r % 2, at_piece(i)])
            )
        else:
            peer = near
            src = dst = gate_line_ref.at[3] if i is None else total_ref.at[r, at_piece(i)]
        return remote(src, dst, line_sems.at[r, 2 * hop, at], line_sems.at[r, 2 * hop + 1, at], "tensor", peer)

    def line_start(r, c):
        @pl.when(is_end)
        def _():
            for i in pieces_of(c):
                line_copy(r, i, 0).start()

    def line_first(r, i):
        line_copy(r, i, 0).wait_recv()
        if i is None:
            gate_line_ref[0] = (gate_line_ref[0].astype(f32) + gate_line_ref[1].astype(f32)).astype(low)
        else:
            block = at_piece(i)
            part_ref[block, :] = (part_ref[block, :].astype(f32) + near_ref[block, :].astype(f32)).astype(low)
        line_copy(r, i, 1).start()

    def line_second(r, i):
        line_copy(r, i, 1).wait_recv()
        if i is None:
            gate_line_ref[3] = (gate_line_ref[0].astype(f32) + gate_line_ref[2].astype(f32)).astype(low)
        else:
            block = at_piece(i)
            total_ref[r, block, :] = (
                part_ref[block, :].astype(f32) + middle_ref[r % 2, block, :].astype(f32)
            ).astype(low)
        line_copy(r, i, 2).start()

    pending = {0: [], 1: [], 2: []}

    def line_serve(r, c):
        @pl.when(is_middle)
        def _():
            for i in pieces_of(c):
                line_first(r, i)
                pending[r].append(i)
                if len(pending[r]) > LAG:
                    line_second(r, pending[r].pop(0))

    def line_flush(r):
        @pl.when(is_middle)
        def _():
            while pending[r]:
                line_second(r, pending[r].pop(0))

    def line_take(r, c):
        @pl.when(is_end)
        def _():
            for i in pieces_of(c):
                line_copy(r, i, 2).wait_recv()

    def line_drain(r, c):
        @pl.when(is_end)
        def _():
            for i in pieces_of(c):
                line_copy(r, i, 0).wait_send()

        @pl.when(is_middle)
        def _():
            for i in pieces_of(c):
                line_copy(r, i, 1).wait_send()
                line_copy(r, i, 2).wait_send()

    for c in range(chunks):
        lo, hi = c * chunk, (c + 1) * chunk
        causal = lax.broadcasted_iota(jnp.int32, (chunk, hi), 0) + lo >= (
            lax.broadcasted_iota(jnp.int32, (chunk, hi), 1)
        )
        pieces = []
        for h in range(heads):
            at = h * HEAD_DIM
            queries = qkv_ref[lo:hi, at : at + HEAD_DIM]
            keys = qkv_ref[0:hi, head_width + at : head_width + at + HEAD_DIM]
            values = qkv_ref[0:hi, 2 * head_width + at : 2 * head_width + at + HEAD_DIM]
            bias = jnp.broadcast_to(wrapped[h : h + 1, :], (chunk, token_count))
            bias = pltpu.roll(bias, lo, 1, stride=1, stride_axis=0)[:, :hi]
            scores = jnp.where(causal, dot(queries, keys, ((1,), (1,))) * factor + bias, MASKED)
            row_max = jnp.max(scores, axis=-1, keepdims=True)
            grown = jnp.exp(scores - row_max)
            total = jnp.sum(grown, axis=-1, keepdims=True)
            probs = (grown * (1.0 / total)).astype(low)
            probs_ref[h, lo:hi, 0:hi] = probs
            pieces.append(dot(probs, values).astype(low))
        context = jnp.concatenate(pieces, axis=1)
        context_ref[lo:hi, :] = context
        part_ref[lo:hi, :] = dot(context, wo_ref[...], ((1,), (1,))).astype(low)
        line_start(0, c)
        if c >= 1:
            line_serve(0, c - 1)
    line_serve(0, chunks - 1)
    line_flush(0)

    for c in range(chunks):
        block = at_chunk(c)
        line_take(0, c)
        residual = x_ref[block, :].astype(f32) + total_ref[0, block, :].astype(f32)
        residual_ref[block, :] = residual
        normed = (residual * rms_scale(residual) * gain_two).astype(low)
        normed_ref[block, :] = normed
        for k in range(model_width // strip):
            strips_ref[k, block, :] = normed[:, k * strip : (k + 1) * strip]

    def send_strip(strip_index, place):
        def body(peer):
            block = rows_at(peer, capacity)
            send_ref[strip_index, block, :] = dot(both_ref[block, :], strips_ref[strip_index]).astype(low)
            row_copy(peer, me, strip_index, place).start()

        each_peer(body)

    shared = 1 + half
    send_strip(shared, 0)
    send_strip(0, 1)

    def forward(source):
        row_copy(source, source, shared, 0).wait_recv()
        hand_over(source, shared).start()

    each_source(forward)
    own = rows_at(me, capacity)
    for k in range(model_width // strip):
        rows_ref[k, own, :] = dot(both_ref[own, :], strips_ref[k]).astype(low)
    cots_ref[own, :] = cot_send_ref[own, :]

    gains_low = gains_ref[...].astype(low)
    logits = dot(gains_low, normed_ref[...], ((1,), (1,)))
    label_rows = lax.broadcasted_iota(jnp.int32, logits.shape, 0) - 8
    chosen_first = jnp.sum(jnp.where(label_rows == ids_first, logits, 0.0), axis=0, keepdims=True)
    chosen_second = jnp.sum(jnp.where(label_rows == ids_second, logits, 0.0), axis=0, keepdims=True)
    gate_first = jax.nn.sigmoid(chosen_first - chosen_second)
    gate_second = 1.0 - gate_first
    gates_ref[0:1, :] = gate_first
    gates_ref[1:2, :] = gate_second

    def make_gated(expert, carry):
        block = rows_at(expert, capacity)
        sign = signed_ref[block, :].astype(f32)
        gated_ref[block, :] = jnp.where(sign > 0, gate_first, jnp.where(sign < 0, gate_second, 0.0)).astype(low)
        return carry

    lax.fori_loop(0, experts, make_gated, 0)
    for z in range(tensor_size):

        @pl.when(level == z)
        def _():
            residual_t_ref[...] = jnp.transpose(residual_ref[:, z * column_width : (z + 1) * column_width])

    load_in().wait()
    load_out().wait()

    pair = 2 * capacity
    ones = jnp.ones((16, model_width), low)

    def expert_step(step, carry):
        other = lax.rem(chip + step, chips)
        block = rows_at(other, pair)
        for c in range(2):
            source = 2 * other + c

            @pl.when(source != me)
            def _():
                cot_copy(source, source).wait_recv()
                row_copy(source, source, 0, 1).wait_recv()
                hand_over(source, 2 - half).wait_recv()

        rows = jnp.concatenate([rows_ref[k, block, :] for k in range(model_width // strip)], axis=1)
        value, slope = gelu_both(dot(rows, win_ref[...]))
        active = value.astype(low)
        active_ref[block, :] = active
        owner_logits = dot(rows, gains_low, ((1,), (1,)))
        columns = lax.broadcasted_iota(jnp.int32, owner_logits.shape, 1) - 8
        other_ids = cots_ref[block, model_width : model_width + 1].astype(f32).astype(jnp.int32) - me
        own_logit = jnp.sum(jnp.where(columns == me, owner_logits, 0.0), axis=1, keepdims=True)
        other_logit = jnp.sum(jnp.where(columns == other_ids, owner_logits, 0.0), axis=1, keepdims=True)
        row_gate = jax.nn.sigmoid(own_logit - other_logit)
        cot = cots_ref[block, :model_width].astype(f32)
        drows = (row_gate * cot).astype(low)
        drows_ref[block, :] = drows
        dpre = (dot(drows, wout_ref[...], ((1,), (1,))) * slope).astype(low)
        dpre_ref[block, :] = dpre
        back_send_ref[block, :] = dot(dpre, win_ref[...], ((1,), (1,))).astype(low)
        for c in range(2):
            source = 2 * other + c

            @pl.when(source != me)
            def _():
                back_copy(source, me).start()

        owner_out = dot(active, wout_ref[...])
        out_send_ref[block, :] = owner_out.astype(low)
        agree = (cot * owner_out).astype(low)
        for c in range(2):
            source = 2 * other + c
            gate_send_ref[source] = dot(ones, agree[c * capacity : (c + 1) * capacity, :], ((1,), (1,))).astype(low)

            @pl.when(source != me)
            def _():
                gate_copy(source, me).start()

        return carry

    lax.fori_loop(0, chips, expert_step, 0)
    back_ref[own, :] = back_send_ref[own, :]
    out_ref[own, :] = out_send_ref[own, :]
    gate_ref[me] = gate_send_ref[me]

    def grad_out(which, part):
        target = (out_grad_hbm, in_grad_hbm)[which]
        block = slice(part * 256, (part + 1) * 256)
        return pltpu.make_async_copy(grad_ref.at[which, block], target.at[block], local_sems.at[2 + which * 8 + part])

    parts = win_ref.shape[0] // 256
    for part in range(parts):
        block = slice(part * 256, (part + 1) * 256)
        grad_ref[0, block, :] = dot(active_ref[:, block], drows_ref[...], ((0,), (0,)))
        grad_out(0, part).start()
        grad_ref[1, block, :] = dot(rows_ref[part], dpre_ref[...], ((0,), (0,)))
        grad_out(1, part).start()

    each_peer(lambda source: gate_copy(source, source).wait_recv())
    each_peer(lambda source: back_copy(source, source).wait_recv())
    each_peer(lambda peer: out_copy(peer, me).start())
    gate_line = dot(gate_ref[0], signed_ref[0:capacity, :])
    for e in range(1, experts):
        gate_line = gate_line + dot(gate_ref[e], signed_ref[e * capacity : (e + 1) * capacity, :])
    gate_line_ref[0] = gate_line.astype(low)
    line_start(1, None)
    order = list(range(chunks))[::-1]
    queue = [None] + order
    for place, c in enumerate(queue):
        if c is not None:
            block = at_chunk(c)
            line_drain(0, c)
            part_ref[block, :] = dot(both_ref[:, block], back_ref[...], ((0,), (0,))).astype(low)
            line_start(1, c)
        if place >= 1:
            line_serve(1, queue[place - 1])
    line_serve(1, queue[-1])
    line_flush(1)

    line_take(1, None)
    gate_diff = gate_line_ref[3, 0:1, :].astype(f32)
    dlogit = gate_diff * gates_ref[0:1, :] * gates_ref[1:2, :]
    dlogits = jnp.where(
        label_rows == ids_first, dlogit, jnp.where(label_rows == ids_second, -dlogit, 0.0)
    ).astype(low)
    sums_send_ref[...] = dot(dlogits, normed_ref[...])

    def backward_chunk(c, ffn_term):
        lo, hi = c * chunk, (c + 1) * chunk
        block = at_chunk(c)
        line_take(1, c)
        dnormed = total_ref[1, block, :].astype(f32) + dot(dlogits[:, block], gains_low, ((0,), (0,)))
        residual = residual_ref[block, :]
        scale_two = rms_scale(residual)
        ffn_term = ffn_term + jnp.sum(dnormed * residual * scale_two, axis=0, keepdims=True)
        dres = cot_ref[block, :].astype(f32) + norm_back(dnormed, residual, scale_two, gain_two)
        dres_ref[block, :] = dres
        dres_low = dres.astype(low)
        dres_low_ref[block, :] = dres_low
        dcontext = dot(dres_low, wo_ref[...]).astype(low)
        flip = (
            lax.broadcasted_iota(jnp.int32, (chunk, chunk), 0)
            + lax.broadcasted_iota(jnp.int32, (chunk, chunk), 1)
            == chunk - 1
        )
        flip = jnp.where(flip, 1.0, 0.0).astype(low)
        first, second, third = [], [], []
        for h in range(heads):
            at = h * HEAD_DIM
            queries = qkv_ref[lo:hi, at : at + HEAD_DIM]
            keys = qkv_ref[0:hi, head_width + at : head_width + at + HEAD_DIM]
            values = qkv_ref[0:hi, 2 * head_width + at : 2 * head_width + at + HEAD_DIM]
            dctx = dcontext[:, at : at + HEAD_DIM]
            probs = probs_ref[h, lo:hi, 0:hi]
            weights = probs.astype(f32)
            dweights = dot(dctx, values, ((1,), (1,)))
            agreement = jnp.sum(weights * dweights, axis=-1, keepdims=True)
            dscores = (weights * (dweights - agreement)).astype(low)
            first.append((factor * dot(dscores, keys)).astype(low))
            dkeys = dot(dscores, queries, ((0,), (0,)))
            dvalues = dot(probs, dctx, ((0,), (0,)))
            if c < chunks - 1:
                dkeys = dkeys + dkeys_ref[h, 0:hi, :]
                dvalues = dvalues + dvalues_ref[h, 0:hi, :]
            if lo:
                dkeys_ref[h, 0:lo, :] = dkeys[0:lo]
                dvalues_ref[h, 0:lo, :] = dvalues[0:lo]
            second.append((factor * dkeys[lo:hi]).astype(low))
            third.append(dvalues[lo:hi].astype(low))
            flipped = dot(flip, dscores)
            if hi < token_count:
                flipped = jnp.concatenate([flipped, jnp.zeros((chunk, token_count - hi), f32)], axis=1)
            skewed = pltpu.roll(flipped, token_count - (hi - 1), 1, stride=1, stride_axis=0)
            line = jnp.sum(skewed, axis=0, keepdims=True)
            if c < chunks - 1:
                line = line + diagonal_ref[h : h + 1, :]
            diagonal_ref[h : h + 1, :] = line
        dqkv = jnp.concatenate(first + second + third, axis=1)
        dqkv_ref[block, :] = dqkv
        line_drain(1, c)
        part_ref[block, :] = dot(dqkv, wqkv_ref[...], ((1,), (1,))).astype(low)
        line_start(2, c)
        return ffn_term

    ffn_term = jnp.zeros((1, model_width), f32)
    for place, c in enumerate(order):
        ffn_term = backward_chunk(c, ffn_term)
        if place >= 1:
            line_serve(2, order[place - 1])

    for part in range(model_width // 256):
        block = slice(part * 256, (part + 1) * 256)
        terms_send_ref[block, :] = dot(normed_one_ref[:, block], dqkv_ref[...], ((0,), (0,))).astype(low)
        oterms_send_ref[block, :] = dot(dres_low_ref[:, block], context_ref[...], ((0,), (0,))).astype(low)
        if part == 0:
            line_serve(2, order[-1])
        if part == 1:
            line_flush(2)
    for place in range(chips):
        start_all(pair_copies(place))

    def pass_terms():
        for place in range(chips):
            recv_all(pair_copies(place))
            block = rows_at(2 * place + core, block_rows)
            terms_send_ref[block, :] = (
                terms_send_ref[block, :].astype(f32) + pair_ref[place].astype(f32)
            ).astype(low)
            oterms_send_ref[block, :] = (
                oterms_send_ref[block, :].astype(f32) + opair_ref[place].astype(f32)
            ).astype(low)
        each_chip(lambda other: start_all(term_copies(other, chip)))
        terms_ref[rows_at(chip, block_rows), :] = terms_send_ref[mine, :]
        oterms_ref[rows_at(chip, block_rows), :] = oterms_send_ref[mine, :]

    each_peer(lambda source: out_copy(source, source).wait_recv())
    for part in range(model_width // 256):
        block = slice(part * 256, (part + 1) * 256)
        mix_send_ref[block, :] = dot(out_ref[:, block], gated_ref[...], ((0,), (0,))).astype(low)
        if part == 0:
            pass_terms()
    side = level // 2
    end_level = side * (tensor_size - 1)
    middle_level = 1 + side
    away = [2 * (1 - side), 2 * (1 - side) + 1]

    def mix_at(target):
        return rows_at(target, column_width)

    def mix_copy(place, target, peer):
        return remote(
            mix_send_ref.at[mix_at(target)],
            mix_ref.at[place],
            z_sems.at[0, place],
            z_sems.at[1, place],
            "tensor",
            peer,
        )

    def mix_add(target, place):
        mix_send_ref[mix_at(target), :] = (
            mix_send_ref[mix_at(target), :].astype(f32) + mix_ref[place].astype(f32)
        ).astype(low)

    up_order = [away[0], away[1], middle_level]

    @pl.when(is_end)
    def _():
        for place, target in enumerate(up_order):
            mix_copy(place, target, near).start()

    sums_send_ref[0:1, :] = ffn_term
    diagonal = diagonal_ref[0:heads, :]
    lanes = lax.broadcasted_iota(jnp.int32, (heads, model_width), 1)
    bias_rows = jnp.zeros((heads, model_width), f32)
    for b in range(NB):
        bucket_total = jnp.sum(jnp.where(wrap_bucket == b, diagonal, 0.0), axis=1, keepdims=True)
        bias_rows = jnp.where(lanes == b, bucket_total, bias_rows)
    sums_send_ref[2 : 2 + heads, :] = bias_rows
    each_peer(lambda peer: sums_copy(peer, me).start())
    sums_ref[me] = sums_send_ref[...]

    attn_term = jnp.zeros((1, model_width), f32)
    for c in order:
        block = at_chunk(c)
        line_take(2, c)
        dnormed = total_ref[2, block, :].astype(f32)
        values = x_ref[block, :].astype(f32)
        scale_one = rms_scale(values)
        attn_term = attn_term + jnp.sum(dnormed * values * scale_one, axis=0, keepdims=True)
        dres_ref[block, :] = dres_ref[block, :] + norm_back(dnormed, values, scale_one, gain_one)

    late_send_ref[...] = jnp.broadcast_to(attn_term, late_send_ref.shape)
    each_peer(lambda peer: late_copy(peer, me).start())
    late_ref[me] = late_send_ref[...]

    for z in range(tensor_size):

        @pl.when(level == z)
        def _():
            input_out[...] = jnp.transpose(dres_ref[:, z * column_width : (z + 1) * column_width])

    @pl.when(is_middle)
    def _():
        for place in range(2):
            mix_copy(place, up_order[place], near).wait_recv()
            mix_add(up_order[place], place)
            mix_copy(3 + place, up_order[place], across).start()
        own_side = [2 * side, 2 * side + 1]
        for place in range(2):
            mix_copy(3 + place, own_side[place], across).wait_recv()
            mix_add(own_side[place], 3 + place)
        mix_copy(5, end_level, near).start()
        mix_copy(2, middle_level, near).wait_recv()
        mix_add(middle_level, 2)

    stores()[0].start()
    each_chip(lambda source: recv_all(term_copies(source, source)))
    reduced = terms_ref[0:block_rows, :].astype(f32)
    oreduced = oterms_ref[0:block_rows, :].astype(f32)
    for source in range(1, chips):
        block = slice(source * block_rows, (source + 1) * block_rows)
        reduced = reduced + terms_ref[block, :].astype(f32)
        oreduced = oreduced + oterms_ref[block, :].astype(f32)
    for k in range(3):
        qkv_out[k] = reduced[:, k * head_width : (k + 1) * head_width]
    wo_out[...] = oreduced
    stores()[1].start()
    stores()[2].start()

    @pl.when(is_end)
    def _():
        mix_copy(5, level, near).wait_recv()
        mix_add(level, 5)

    mixture = mix_send_ref[mix_at(level), :].astype(f32)
    block_out[...] = (residual_t_ref[...] + mixture).astype(low)
    stores()[3].start()

    each_peer(lambda source: sums_copy(source, source).wait_recv())
    sums = sums_ref[0]
    for source in range(1, group_size):
        sums = sums + sums_ref[source]
    sums_out[...] = sums
    stores()[4].start()
    each_peer(lambda source: late_copy(source, source).wait_recv())
    late = late_ref[0]
    for source in range(1, group_size):
        late = late + late_ref[source]
    late_out[...] = late
    stores()[5].start()

    def drain(peer):
        late_copy(peer, me).wait_send()
        sent_all(weight_copies(peer, me, peer))
        cot_copy(peer, me).wait_send()
        row_copy(peer, me, shared, 0).wait_send()
        row_copy(peer, me, 0, 1).wait_send()
        hand_over(peer, shared).wait_send()
        back_copy(peer, me).wait_send()
        gate_copy(peer, me).wait_send()
        out_copy(peer, me).wait_send()
        sums_copy(peer, me).wait_send()

    each_peer(drain)
    each_chip(lambda other: sent_all(term_copies(other, chip)))
    for place in range(chips):
        sent_all(pair_copies(place))

    @pl.when(is_end)
    def _():
        for place, target in enumerate(up_order):
            mix_copy(place, target, near).wait_send()

    @pl.when(is_middle)
    def _():
        for place in range(2):
            mix_copy(3 + place, up_order[place], across).wait_send()
        mix_copy(5, end_level, near).wait_send()

    line_drain(1, None)
    for c in order:
        line_drain(2, c)
    for part in range(parts):
        grad_out(0, part).wait()
        grad_out(1, part).wait()
    for copy in stores():
        copy.wait()


def run_layer(group_size, tensor_size, capacity, x, q, k, v, o, attn_gain, ffn_gain, router, bias, ids, cot, w_in, w_out):
    tokens, width = x.shape
    block_rows, head_width = q.shape
    small_rows = 8 + router.shape[0]
    heads = bias.shape[0]
    hidden = w_in.shape[1]
    slots = group_size * capacity
    low = jnp.bfloat16
    f32 = jnp.float32
    full = group_size * block_rows
    chunks = tokens // LANES
    column_width = width // tensor_size

    def shape(dims, dtype=low):
        return jax.ShapeDtypeStruct(dims, dtype)

    def room(*dims, dtype=low):
        return pltpu.VMEM(dims, dtype)

    hbm = pl.BlockSpec(memory_space=pl.ANY)
    dma = pltpu.SemaphoreType.DMA
    return pl.pallas_call(
        functools.partial(layer_kernel, group_size, tensor_size),
        out_shape=(
            shape((column_width, tokens)),
            shape((column_width, tokens), f32),
            shape((3, block_rows, head_width), f32),
            shape((block_rows, head_width), f32),
            shape((small_rows, width), f32),
            shape((8, width), f32),
            shape((width, hidden), f32),
            shape((hidden, width), f32),
        ),
        in_specs=[hbm] * 13,
        out_specs=(hbm,) * 8,
        scratch_shapes=[
            room(full, 3 * head_width),
            room(full, head_width),
            room(small_rows, width, dtype=f32),
            room(tokens, 3 * head_width),
            room(heads, tokens, tokens),
            room(tokens, head_width),
            room(tokens, width),
            room(tokens, width),
            room(tokens, width, dtype=f32),
            room(column_width, tokens, dtype=f32),
            room(slots, tokens),
            room(slots, tokens),
            room(slots, tokens),
            room(width // 256, tokens, 256),
            room(width // 256, slots, 256),
            room(slots, width + LANES),
            room(width, hidden),
            room(hidden, width),
            room(slots, hidden),
            room(slots, width),
            room(slots, hidden),
            room(2, width, width, dtype=f32),
            room(width // 256, slots, 256),
            room(slots, width + LANES),
            room(slots, width),
            room(slots, width),
            room(slots, width),
            room(slots, width),
            room(group_size, 16, capacity),
            room(group_size, 16, capacity),
            room(group_size, small_rows, LANES),
            room(group_size, tokens, dtype=f32),
            room(8, tokens, dtype=f32),
            room(tokens, width),
            room(tokens, width),
            room(2, tokens, width),
            room(3, tokens, width),
            room(4, 16, tokens),
            room(tokens, width, dtype=f32),
            room(tokens, width),
            room(heads, tokens, HEAD_DIM, dtype=f32),
            room(heads, tokens, HEAD_DIM, dtype=f32),
            room(tokens, 3 * head_width),
            room(8, tokens, dtype=f32),
            room(full, 3 * head_width),
            room(full // 2, 3 * head_width),
            room(full, head_width),
            room(full // 2, head_width),
            room(group_size // 2, block_rows, 3 * head_width),
            room(group_size // 2, block_rows, head_width),
            room(width, tokens),
            room(6, column_width, tokens),
            room(small_rows, width, dtype=f32),
            room(group_size, small_rows, width, dtype=f32),
            room(8, width, dtype=f32),
            room(group_size, 8, width, dtype=f32),
            *[room(*a.shape, dtype=a.dtype) for a in (x, q, k, v, o, attn_gain, ffn_gain, router, bias, ids, cot)],
            room(column_width, tokens),
            room(column_width, tokens, dtype=f32),
            room(3, block_rows, head_width, dtype=f32),
            room(block_rows, head_width, dtype=f32),
            room(small_rows, width, dtype=f32),
            room(8, width, dtype=f32),
            dma((11,)),
            dma((6,)),
            dma((6, group_size)),
            dma((8, group_size // 2)),
            dma((6, group_size)),
            dma((18, group_size)),
            dma((3, 6, tokens // PIECE + 1)),
            dma((2, 6)),
            dma((18,)),
        ],
        compiler_params=pltpu.CompilerParams(
            collective_id=0, has_side_effects=True, vmem_limit_bytes=VMEM_BYTES
        ),
        name="layer",
    )(x, q, k, v, o, attn_gain, ffn_gain, router, bias, ids, cot, w_in, w_out)


def finish_kernel(group_size, *refs):
    sources, targets = refs[:8], refs[8:20]
    held, built = refs[20:28], refs[28:36]
    in_sems, out_sems = refs[36:]
    me = lax.axis_index("dp")

    def pieces(src, dst, sems, at):
        count = 4 if at >= 6 else 1
        rows = src.shape[0] // count
        return [
            pltpu.make_async_copy(src.at[pl.ds(p * rows, rows)], dst.at[pl.ds(p * rows, rows)], sems.at[at, p])
            for p in range(count)
        ]

    taken = [pieces(src, dst, in_sems, at) for at, (src, dst) in enumerate(zip(sources, held))]
    for group in taken:
        for copy in group:
            copy.start()
    block, inputs, qkv, wo, sums, late, in_grad, out_grad = held
    q_o, k_o, v_o, attn_o, ffn_o, router_o, bias_o = built[:7]
    (block_out, input_out, q_out, k_out, v_out, wo_out, attn_out, ffn_out, router_out, bias_out, in_out, out_out) = targets
    given = []

    def give(src, dst, at):
        for copy in pieces(src, dst, out_sems, at):
            copy.start()
            given.append(copy)

    for at in range(6):
        for copy in taken[at]:
            copy.wait()
    give(block, block_out, 0)
    give(inputs, input_out, 1)
    for k, (src, dst) in enumerate(((q_o, q_out), (k_o, k_out), (v_o, v_out))):
        src[...] = qkv[k]
        give(src, dst, 2 + k)
    give(wo, wo_out, 5)
    for at, (src, dst) in ((6, (in_grad, in_out)), (7, (out_grad, out_out))):
        for p, copy in enumerate(taken[at]):
            copy.wait()
            out = pieces(src, dst, out_sems, at)[p]
            out.start()
            given.append(out)
    block_rows = wo.shape[0]
    heads, buckets = bias_o.shape
    features = sums.shape[1]
    shift = lax.rem((group_size - me) * block_rows, features)
    total = sums[...]
    bias_o[...] = total[2 : 2 + heads, :buckets]
    total = pltpu.roll(total, shift, 1)
    ffn_o[...] = total[0:1, :block_rows]
    router_o[...] = total[8:, :block_rows]
    attn_o[...] = pltpu.roll(late[...], shift, 1)[0:1, :block_rows]
    for k, (src, dst) in enumerate(((attn_o, attn_out), (ffn_o, ffn_out), (router_o, router_out), (bias_o, bias_out))):
        copy = pltpu.make_async_copy(src, dst, out_sems.at[8 + k, 0])
        copy.start()
        given.append(copy)
    for copy in given:
        copy.wait()


def finish(group_size, heads, buckets, *results):
    f32 = jnp.float32
    block, inputs, qkv, wo, sums, late, in_grad, out_grad = results
    block_rows = wo.shape[0]

    def shape(*dims):
        return jax.ShapeDtypeStruct(dims, f32)

    small = [(1, block_rows), (1, block_rows), (sums.shape[0] - 8, block_rows), (heads, buckets)]
    hbm = pl.BlockSpec(memory_space=pl.ANY)
    return pl.pallas_call(
        functools.partial(finish_kernel, group_size),
        out_shape=(
            jax.ShapeDtypeStruct(block.shape, block.dtype),
            shape(*inputs.shape),
            *[shape(*wo.shape)] * 4,
            *[shape(*dims) for dims in small],
            shape(*in_grad.shape),
            shape(*out_grad.shape),
        ),
        in_specs=[hbm] * 8,
        out_specs=(hbm,) * 12,
        scratch_shapes=[
            *[pltpu.VMEM(a.shape, a.dtype) for a in results],
            *[pltpu.VMEM(wo.shape, f32)] * 3,
            *[pltpu.VMEM(dims, f32) for dims in small],
            pltpu.VMEM((8, LANES), f32),
            pltpu.SemaphoreType.DMA((8, 4)),
            pltpu.SemaphoreType.DMA((12, 4)),
        ],
        compiler_params=pltpu.CompilerParams(vmem_limit_bytes=VMEM_BYTES),
        name="finish",
    )(*results)


def on_device_general(
    block_input,
    attn_gain,
    query_weight,
    key_weight,
    value_weight,
    output_weight,
    bias_table,
    ffn_gain,
    router_weight,
    expert_in,
    expert_out,
    expert_ids,
    out_cotangent,
):
    tensor_size = lax.axis_size("tensor")
    group_size = lax.axis_size("dp")
    tensor_index = lax.axis_index("tensor")
    own_expert = lax.axis_index("dp")
    token_count, model_width = block_input.shape
    column_width = model_width // tensor_size
    column_start = tensor_index * column_width
    expert_count = group_size * expert_in.shape[0]
    capacity = tensor_size * max(1, 3 * token_count // (5 * expert_count))
    slot_rows = expert_count * capacity
    seq_count = token_count // SEQ_LEN
    head_local = bias_table.shape[0]
    head_width = head_local * HEAD_DIM
    block_rows = query_weight.shape[0]
    low = jnp.bfloat16

    def own_columns(matrix):
        return lax.dynamic_slice_in_dim(matrix, column_start, column_width, 1)

    packed = jnp.concatenate(
        [
            query_weight,
            key_weight,
            value_weight,
            output_weight,
            router_weight,
            attn_gain[:, None],
            ffn_gain[:, None],
        ],
        axis=1,
    )
    packed = lax.all_gather(packed, "dp", axis=0, tiled=True)

    labels = jnp.arange(expert_count, dtype=jnp.int32)
    flat_ids = expert_ids.reshape(-1)
    ids_onehot = (flat_ids[:, None] == labels[None, :]).astype(jnp.int32)
    pair_rows = lax.broadcasted_iota(jnp.int32, (2 * token_count, 2 * token_count), 0)
    pair_cols = lax.broadcasted_iota(jnp.int32, (2 * token_count, 2 * token_count), 1)
    before = (pair_cols < pair_rows).astype(low)
    earlier = dot(before, ids_onehot.astype(low)).astype(jnp.int32)
    slot_index = jnp.sum(earlier * ids_onehot, axis=1)
    places = (flat_ids * capacity + slot_index).reshape(token_count, 2)
    place_rows = jnp.arange(slot_rows, dtype=jnp.int32)
    at_first = places[:, 0][None, :] == place_rows[:, None]
    at_second = places[:, 1][None, :] == place_rows[:, None]
    map_first = at_first.astype(low)
    map_second = at_second.astype(low)
    map_both = (at_first | at_second).astype(low)

    ids_low = jnp.broadcast_to(expert_ids.astype(low)[:, :, None], (token_count, 2, LANES))
    cot_source = jnp.concatenate(
        [
            jnp.concatenate([out_cotangent, ids_low[:, 1]], axis=1),
            jnp.concatenate([out_cotangent, ids_low[:, 0]], axis=1),
        ],
        axis=0,
    )
    cot_parcel = dot(jnp.concatenate([map_first, map_second], axis=1), cot_source).astype(low)
    packed, cot_parcel = lax.optimization_barrier((packed, cot_parcel))
    cot_arrived = exchange(
        cot_parcel.reshape(expert_count, capacity, model_width + LANES)
    ).reshape(slot_rows, model_width + LANES)
    cot_rows = cot_arrived[:, :model_width].astype(jnp.float32)
    other_ids = cot_arrived[:, model_width].astype(jnp.int32)

    qkv_full = packed[:, : 3 * head_width]
    output_full = packed[:, 3 * head_width : 4 * head_width]
    at = 4 * head_width
    router_full = packed[:, at : at + expert_count]
    gain_one = packed[:, at + expert_count].astype(jnp.float32)
    gain_two = packed[:, at + expert_count + 1].astype(jnp.float32)
    inputs_f = block_input.astype(jnp.float32)
    scale_one = rms_scale(inputs_f)
    normed_one = (inputs_f * scale_one * gain_one).astype(low)
    qkv = dot(normed_one, qkv_full).astype(low)
    bucket_vec = bucket_vector_at(jnp.arange(SEQ_LEN, dtype=jnp.int32), NB)
    bucket_labels = jnp.arange(NB, dtype=jnp.int32)
    wrap = (SEQ_LEN - jnp.arange(SEQ_LEN, dtype=jnp.int32)) % SEQ_LEN
    wrapped_onehot = bucket_vector_at(wrap, NB)[None, :] == bucket_labels[:, None]
    wrapped = jnp.sum(
        jnp.where(wrapped_onehot[None], bias_table[:, :, None], 0.0), axis=1
    )
    context, probs = attend_forward(qkv, wrapped, seq_count, head_local)
    attn_part = dot(context, output_full, ((1,), (1,))).astype(low)
    attn_out = lax.psum(attn_part, "tensor").astype(jnp.float32)
    residual = inputs_f + attn_out
    scale_two = rms_scale(residual)
    normed_two = (residual * scale_two * gain_two).astype(low)

    logits = dot(normed_two, router_full)
    picked = (expert_ids[:, :, None] == labels[None, None, :]).astype(jnp.float32)
    chosen = jnp.sum(picked * logits[:, None, :], axis=2)
    first_gate = jax.nn.sigmoid(chosen[:, 0] - chosen[:, 1])
    second_gate = 1.0 - first_gate

    weight_in = expert_in[0]
    weight_out = expert_out[0]
    parcel = dot(map_both, normed_two).astype(low)
    expert_rows = exchange(parcel.reshape(expert_count, capacity, model_width)).reshape(
        slot_rows, model_width
    )
    pre_act = dot(expert_rows, weight_in)
    active, pullback = jax.vjp(jax.nn.gelu, pre_act)
    active = active.astype(low)
    owner_out = dot(active, weight_out)
    owner_logits = dot(expert_rows, router_full)
    own_logit = jnp.sum(
        jnp.where(labels[None, :] == own_expert, owner_logits, 0.0), axis=1
    )
    other_logit = jnp.sum(
        jnp.where(labels[None, :] == other_ids[:, None], owner_logits, 0.0), axis=1
    )
    row_gate = jax.nn.sigmoid(own_logit - other_logit)
    expert_drows = (row_gate[:, None] * cot_rows).astype(low)
    dpre = pullback(dot(expert_drows, weight_out, ((1,), (1,))))[0].astype(low)
    owner_back = dot(dpre, weight_in, ((1,), (1,))).astype(low)
    gate_part = jnp.sum(cot_rows * owner_out, axis=1, keepdims=True).astype(low)
    back_parcel = jnp.concatenate(
        [owner_back, jnp.broadcast_to(gate_part, (slot_rows, LANES))], axis=1
    )
    back_rows = exchange(
        back_parcel.reshape(group_size, capacity, model_width + LANES)
    ).reshape(slot_rows, model_width + LANES)
    out_rows = exchange(
        owner_out.astype(low).reshape(group_size, capacity, model_width)
    ).reshape(slot_rows, model_width)
    out_grad = dot(active, expert_drows, ((0,), (0,)))
    in_grad = dot(expert_rows, dpre, ((0,), (0,)))

    dnormed_part = dot(map_both, back_rows[:, :model_width], ((0,), (0,)))
    gate_diff_part = dot(map_first - map_second, back_rows[:, model_width:], ((0,), (0,)))
    gate_rows = -(-token_count // model_width)
    gate_line = jnp.pad(gate_diff_part[:, 0], (0, gate_rows * model_width - token_count))
    summed = lax.psum(
        jnp.concatenate(
            [dnormed_part, gate_line.reshape(gate_rows, model_width)], axis=0
        ).astype(low),
        "tensor",
    ).astype(jnp.float32)
    gate_diff = summed[token_count:].reshape(-1)[:token_count]
    mixture_part = first_gate[:, None] * dot(map_first, out_rows, ((0,), (0,)))
    mixture_part = mixture_part + second_gate[:, None] * dot(
        map_second, out_rows, ((0,), (0,))
    )
    mixture_parts = mixture_part.astype(low).reshape(token_count, tensor_size, column_width)
    mixture_parts = jnp.swapaxes(mixture_parts, 0, 1)

    dlogit = gate_diff * first_gate * second_gate
    signed = jnp.stack([dlogit, -dlogit], axis=1)
    dlogits = jnp.sum(picked * signed[:, :, None], axis=1).astype(low)
    router_term = dot(normed_two, dlogits, ((0,), (0,)))
    dnormed_two = summed[:token_count] + dot(dlogits, router_full, ((1,), (1,)))
    ffn_term = jnp.sum(dnormed_two * residual * scale_two, axis=0)
    cot_f = out_cotangent.astype(jnp.float32)
    dresidual = cot_f + norm_back(dnormed_two, residual, scale_two, gain_two)
    dres_low = dresidual.astype(low)
    mixture_parts, dres_low = lax.optimization_barrier((mixture_parts, dres_low))
    mixture_parts = lax.all_to_all(
        mixture_parts, "tensor", split_axis=0, concat_axis=0, tiled=True
    )

    output_term = dot(dres_low, context, ((0,), (0,)))
    dcontext = dot(dres_low, output_full).astype(low)
    dqkv, diagonal = attend_backward(qkv, probs, dcontext, seq_count, head_local)
    reverse_onehot = (bucket_vec[::-1][:, None] == bucket_labels[None, :]).astype(jnp.float32)
    bias_term = jnp.dot(
        jnp.sum(diagonal, axis=0),
        reverse_onehot,
        precision=lax.Precision.HIGHEST,
        preferred_element_type=jnp.float32,
    )
    dnormed_part = dot(dqkv, qkv_full, ((1,), (1,))).astype(low)
    dnormed_part, mixture_parts = lax.optimization_barrier((dnormed_part, mixture_parts))
    dnormed_one = lax.psum(dnormed_part, "tensor").astype(jnp.float32)
    qkv_term = dot(normed_one, dqkv, ((0,), (0,)))
    bias_count = bias_term.size
    bias_cols = -(-bias_count // block_rows)
    bias_block = jnp.pad(bias_term.reshape(-1), (0, bias_cols * block_rows - bias_count))
    bias_block = jnp.tile(bias_block.reshape(block_rows, bias_cols), (group_size, 1))
    terms = jnp.concatenate(
        [qkv_term, output_term, router_term, ffn_term[:, None], bias_block],
        axis=1,
    ).astype(low)
    term_width = terms.shape[1]
    arrived = exchange(terms.reshape(group_size, block_rows, term_width))
    arrived, dnormed_one = lax.optimization_barrier((arrived, dnormed_one))
    mixture = jnp.sum(mixture_parts.astype(jnp.float32), axis=0)
    block_output = (own_columns(residual) + mixture).astype(low)
    reduced = jnp.sum(arrived.astype(jnp.float32), axis=0)
    at = 4 * head_width
    grads = [reduced[:, k * head_width : (k + 1) * head_width] for k in range(4)]
    router_grad = reduced[:, at : at + expert_count]
    at = at + expert_count
    bias_grad = reduced[:, at + 1 :].reshape(-1)[:bias_count].reshape(bias_term.shape)
    attn_term = jnp.sum(dnormed_one * inputs_f * scale_one, axis=0)
    attn_gain_grad = jnp.sum(exchange(attn_term.reshape(group_size, block_rows)), axis=0)
    first_back = norm_back(dnormed_one, inputs_f, scale_one, gain_one)
    input_grad = own_columns(dresidual + first_back)
    return (
        block_output,
        input_grad,
        attn_gain_grad,
        grads[0],
        grads[1],
        grads[2],
        grads[3],
        bias_grad,
        reduced[:, at],
        router_grad,
        in_grad[None],
        out_grad[None],
    )


def on_device(
    block_input,
    attn_gain,
    query_weight,
    key_weight,
    value_weight,
    output_weight,
    bias_table,
    ffn_gain,
    router_weight,
    expert_in,
    expert_out,
    expert_ids,
    out_cotangent,
):
    tensor_size = lax.axis_size("tensor")
    group_size = lax.axis_size("dp")
    token_count = block_input.shape[0]
    block_rows = query_weight.shape[0]
    head_local = bias_table.shape[0]
    low = jnp.bfloat16
    capacity = tensor_size * max(1, 3 * token_count // (5 * group_size))
    capacity = -(-capacity // 16) * 16
    results = run_layer(
        group_size,
        tensor_size,
        capacity,
        block_input,
        query_weight,
        key_weight,
        value_weight,
        output_weight,
        attn_gain[None, :],
        ffn_gain[None, :],
        router_weight.T,
        bias_table,
        expert_ids.T,
        out_cotangent,
        expert_in[0],
        expert_out[0],
    )
    block, inputs, query, key, value, output, attn, ffn, router, bias, in_grad, out_grad = finish(
        group_size, head_local, NB, *results
    )
    return (
        block.T,
        inputs.T,
        attn[0],
        query,
        key,
        value,
        output,
        bias,
        ffn[0],
        router.T,
        in_grad[None],
        out_grad[None],
    )


def choose(mesh):
    def run(*arrays):
        tokens, width = arrays[0].shape
        block_rows = arrays[2].shape[0]
        hidden = arrays[9].shape[2]
        group_size = mesh.shape["dp"]
        fits = (
            block_rows % 16 == 0
            and block_rows <= LANES
            and arrays[9].shape[0] == 1
            and mesh.shape["tensor"] == 4
            and group_size == 8
            and arrays[6].shape[0] <= 6
            and tokens == SEQ_LEN
            and hidden == width
            and width % 256 == 0
            and width == 3 * 256
        )
        return (on_device if fits else on_device_general)(*arrays)

    return run


def solution(mesh):
    placed = (
        P("dp", None),
        P("dp"),
        P("dp", "tensor"),
        P("dp", "tensor"),
        P("dp", "tensor"),
        P("dp", "tensor"),
        P("tensor", None),
        P("dp"),
        P("dp", None),
        P("dp", None, "tensor"),
        P("dp", "tensor", None),
        P("dp", None),
        P("dp", None),
    )
    return jax.shard_map(
        choose(mesh),
        mesh=mesh,
        in_specs=placed,
        out_specs=(
            P("dp", "tensor"),
            P("dp", "tensor"),
            P("dp"),
            P("dp", "tensor"),
            P("dp", "tensor"),
            P("dp", "tensor"),
            P("dp", "tensor"),
            P("tensor", None),
            P("dp"),
            P("dp", None),
            P("dp", None, "tensor"),
            P("dp", "tensor", None),
        ),
        check_vma=False,
    )
```

```python
import functools
import math

import jax
import jax.numpy as jnp
from jax import lax
from jax.experimental import pallas as pl
from jax.experimental.pallas import tpu as pltpu
from jax.sharding import PartitionSpec as P

HEAD_DIM = 64
NB = 32
SEQ_LEN = 512
LANES = 128
VMEM_BYTES = 63 * 1024 * 1024
PIECE = 32
LAG = 4


EPSILON = 1e-06
MASKED = -1e30


def bucket_vector_at(steps_ids, bucket_count):
    exact_count = bucket_count // 2
    distant = jnp.full(steps_ids.shape, exact_count, jnp.int32)
    for level_index in range(1, bucket_count - exact_count):
        border = int(math.ceil(exact_count * 8.0 ** (level_index / (bucket_count - exact_count))))
        distant = distant + (steps_ids >= border).astype(jnp.int32)
    return jnp.where(steps_ids < exact_count, steps_ids, distant)


def norm_back(dnormed, row_values, row_scale, gain_row):
    inner_mean = jnp.mean(gain_row * dnormed * row_values, axis=-1, keepdims=True)
    return row_scale * (gain_row * dnormed - row_values * row_scale * row_scale * inner_mean)


def rms_scale(matrix):
    return lax.rsqrt(jnp.mean(matrix * matrix, axis=-1, keepdims=True) + EPSILON)


def dot(left, right, dims=((1,), (0,))):
    return lax.dot_general(left, right, (dims, ((), ())), preferred_element_type=jnp.float32)


def forward_kernel(qkv_ref, wrapped_ref, context_ref, probs_ref):
    length = qkv_ref.shape[0]
    heads = probs_ref.shape[0]
    width = heads * HEAD_DIM
    factor = HEAD_DIM ** (-0.5)
    rows = lax.broadcasted_iota(jnp.int32, (length, length), 0)
    cols = lax.broadcasted_iota(jnp.int32, (length, length), 1)
    causal = rows >= cols
    for h in range(heads):
        lo, hi = h * HEAD_DIM, (h + 1) * HEAD_DIM
        queries = qkv_ref[:, lo:hi]
        keys = qkv_ref[:, width + lo : width + hi]
        values = qkv_ref[:, 2 * width + lo : 2 * width + hi]
        bias = jnp.broadcast_to(wrapped_ref[h : h + 1, :], (length, length))
        bias = pltpu.roll(bias, 0, 1, stride=1, stride_axis=0)
        scores = jnp.where(causal, dot(queries, keys, ((1,), (1,))) * factor + bias, MASKED)
        row_max = jnp.max(scores, axis=-1, keepdims=True)
        row_total = jnp.sum(jnp.exp(scores - row_max), axis=-1, keepdims=True)
        probs = jnp.exp(scores - (row_max + jnp.log(row_total))).astype(jnp.bfloat16)
        probs_ref[h] = probs
        context_ref[:, lo:hi] = dot(probs, values).astype(jnp.bfloat16)


def backward_kernel(qkv_ref, probs_ref, dcontext_ref, dqkv_ref, diagonal_ref):
    length = qkv_ref.shape[0]
    heads = probs_ref.shape[0]
    width = heads * HEAD_DIM
    factor = HEAD_DIM ** (-0.5)
    rows = lax.broadcasted_iota(jnp.int32, (length, length), 0)
    cols = lax.broadcasted_iota(jnp.int32, (length, length), 1)
    flip = (rows + cols == length - 1).astype(jnp.float32).astype(jnp.bfloat16)
    for h in range(heads):
        lo, hi = h * HEAD_DIM, (h + 1) * HEAD_DIM
        queries = qkv_ref[:, lo:hi]
        keys = qkv_ref[:, width + lo : width + hi]
        values = qkv_ref[:, 2 * width + lo : 2 * width + hi]
        dcontext = dcontext_ref[:, lo:hi]
        probs = probs_ref[h]
        weights = probs.astype(jnp.float32)
        dweights = dot(dcontext, values, ((1,), (1,)))
        agreement = jnp.sum(weights * dweights, axis=-1, keepdims=True)
        dscores = (weights * (dweights - agreement)).astype(jnp.bfloat16)
        dqkv_ref[:, lo:hi] = (factor * dot(dscores, keys)).astype(jnp.bfloat16)
        dqkv_ref[:, width + lo : width + hi] = (
            factor * dot(dscores, queries, ((0,), (0,)))
        ).astype(jnp.bfloat16)
        dqkv_ref[:, 2 * width + lo : 2 * width + hi] = dot(
            probs, dcontext, ((0,), (0,))
        ).astype(jnp.bfloat16)
        skewed = pltpu.roll(dot(flip, dscores), 0, 1, stride=1, stride_axis=0)
        diagonal_ref[h : h + 1, :] = jnp.sum(skewed, axis=0, keepdims=True)


def attend_forward(qkv, wrapped, seq_count, heads):
    width = heads * HEAD_DIM
    return pl.pallas_call(
        forward_kernel,
        grid=(seq_count,),
        out_shape=(
            jax.ShapeDtypeStruct((seq_count * SEQ_LEN, width), jnp.bfloat16),
            jax.ShapeDtypeStruct((seq_count, heads, SEQ_LEN, SEQ_LEN), jnp.bfloat16),
        ),
        in_specs=[
            pl.BlockSpec((SEQ_LEN, 3 * width), lambda s: (s, 0)),
            pl.BlockSpec((heads, SEQ_LEN), lambda s: (0, 0)),
        ],
        out_specs=(
            pl.BlockSpec((SEQ_LEN, width), lambda s: (s, 0)),
            pl.BlockSpec((None, heads, SEQ_LEN, SEQ_LEN), lambda s: (s, 0, 0, 0)),
        ),
        name="attend_forward",
    )(qkv, wrapped)


def attend_backward(qkv, probs, dcontext, seq_count, heads):
    width = heads * HEAD_DIM
    return pl.pallas_call(
        backward_kernel,
        grid=(seq_count,),
        out_shape=(
            jax.ShapeDtypeStruct((seq_count * SEQ_LEN, 3 * width), jnp.bfloat16),
            jax.ShapeDtypeStruct((seq_count, heads, SEQ_LEN), jnp.float32),
        ),
        in_specs=[
            pl.BlockSpec((SEQ_LEN, 3 * width), lambda s: (s, 0)),
            pl.BlockSpec((None, heads, SEQ_LEN, SEQ_LEN), lambda s: (s, 0, 0, 0)),
            pl.BlockSpec((SEQ_LEN, width), lambda s: (s, 0)),
        ],
        out_specs=(
            pl.BlockSpec((SEQ_LEN, 3 * width), lambda s: (s, 0)),
            pl.BlockSpec((None, heads, SEQ_LEN), lambda s: (s, 0, 0)),
        ),
        name="attend_backward",
    )(qkv, probs, dcontext)


def exchange(parcel):
    return lax.all_to_all(parcel, "dp", split_axis=0, concat_axis=0, tiled=True)


def remote(src, dst, send_sem, recv_sem, axis, index):
    return pltpu.make_async_remote_copy(
        src_ref=src,
        dst_ref=dst,
        send_sem=send_sem,
        recv_sem=recv_sem,
        device_id={axis: index},
        device_id_type=pl.DeviceIdType.MESH,
    )


def rows_at(index, count):
    return pl.ds(pl.multiple_of(index * count, count), count)


def gelu_both(u):
    slope = math.sqrt(2.0 / math.pi)
    cubic = 0.044715
    square = u * u
    t = jnp.tanh(slope * u * (1.0 + cubic * square))
    half = 0.5 + 0.5 * t
    value = u * half
    grad = half + 0.5 * u * (1.0 - t * t) * (slope * (1.0 + 3.0 * cubic * square))
    return value, grad


def layer_kernel(
    group_size,
    tensor_size,
    x_hbm,
    q_hbm,
    k_hbm,
    v_hbm,
    o_hbm,
    attn_gain_hbm,
    ffn_gain_hbm,
    router_hbm,
    bias_hbm,
    ids_hbm,
    cot_hbm,
    win_hbm,
    wout_hbm,
    block_hbm_out,
    input_hbm_out,
    qkv_hbm_out,
    wo_hbm_out,
    sums_hbm_out,
    late_hbm_out,
    in_grad_hbm,
    out_grad_hbm,
    wqkv_ref,
    wo_ref,
    gains_ref,
    qkv_ref,
    probs_ref,
    context_ref,
    normed_one_ref,
    normed_ref,
    residual_ref,
    residual_t_ref,
    both_ref,
    signed_ref,
    gated_ref,
    strips_ref,
    rows_ref,
    cots_ref,
    win_ref,
    wout_ref,
    active_ref,
    drows_ref,
    dpre_ref,
    grad_ref,
    send_ref,
    cot_send_ref,
    back_send_ref,
    back_ref,
    out_send_ref,
    out_ref,
    gate_send_ref,
    gate_ref,
    small_buf,
    code_ref,
    gates_ref,
    part_ref,
    near_ref,
    middle_ref,
    total_ref,
    gate_line_ref,
    dres_ref,
    dres_low_ref,
    dkeys_ref,
    dvalues_ref,
    dqkv_ref,
    diagonal_ref,
    terms_send_ref,
    terms_ref,
    oterms_send_ref,
    oterms_ref,
    pair_ref,
    opair_ref,
    mix_send_ref,
    mix_ref,
    sums_send_ref,
    sums_ref,
    late_send_ref,
    late_ref,
    x_ref,
    q_ref,
    k_ref,
    v_ref,
    o_ref,
    attn_gain_ref,
    ffn_gain_ref,
    router_ref,
    bias_ref,
    ids_ref,
    cot_ref,
    block_out,
    input_out,
    qkv_out,
    wo_out,
    sums_out,
    late_out,
    load_sems,
    store_sems,
    row_sems,
    t_sems,
    w_sems,
    a2a_sems,
    line_sems,
    z_sems,
    local_sems,
):
    me = lax.axis_index("dp")
    level = lax.axis_index("tensor")
    token_count, model_width = x_ref.shape
    experts = group_size
    capacity = both_ref.shape[0] // group_size
    half = lax.rem(level, 2)
    strip = 256
    block_rows, head_width = q_ref.shape
    heads = bias_ref.shape[0]
    column_width = model_width // tensor_size
    low = jnp.bfloat16
    f32 = jnp.float32
    near = level + 1 - 2 * lax.rem(level, 2)
    across = tensor_size - 1 - level
    is_end = jnp.logical_or(level == 0, level == tensor_size - 1)
    is_middle = jnp.logical_not(is_end)
    chip = me // 2
    core = lax.rem(me, 2)
    chips = group_size // 2
    chunk = LANES
    chunks = token_count // chunk
    factor = HEAD_DIM ** (-0.5)

    def peer_of(j):
        other_chip = lax.rem(chip - j // 2 + chips, chips)
        return 2 * other_chip + lax.rem(core + j, 2)

    def each_peer(body):
        def step(j, carry):
            body(peer_of(j))
            return carry

        lax.fori_loop(1, group_size, step, 0)

    def load_in():
        return pltpu.make_async_copy(win_hbm, win_ref, local_sems.at[0])

    def load_out():
        return pltpu.make_async_copy(wout_hbm, wout_ref, local_sems.at[1])

    def loads(first, last):
        pairs = [
            (q_hbm, q_ref),
            (k_hbm, k_ref),
            (v_hbm, v_ref),
            (o_hbm, o_ref),
            (attn_gain_hbm, attn_gain_ref),
            (ffn_gain_hbm, ffn_gain_ref),
            (router_hbm, router_ref),
            (ids_hbm, ids_ref),
            (bias_hbm, bias_ref),
            (cot_hbm, cot_ref),
            (x_hbm, x_ref),
        ]
        return [
            pltpu.make_async_copy(src, dst, load_sems.at[place])
            for place, (src, dst) in enumerate(pairs)
            if first <= place < last
        ]

    for copy in loads(0, 11):
        copy.start()
    load_in().start()
    load_out().start()

    def stores():
        pairs = [
            (input_out, input_hbm_out),
            (qkv_out, qkv_hbm_out),
            (wo_out, wo_hbm_out),
            (block_out, block_hbm_out),
            (sums_out, sums_hbm_out),
            (late_out, late_hbm_out),
        ]
        return [
            pltpu.make_async_copy(src, dst, store_sems.at[place])
            for place, (src, dst) in enumerate(pairs)
        ]

    barrier = pltpu.get_barrier_semaphore()
    each_peer(
        lambda peer: pl.semaphore_signal(
            barrier, inc=1, device_id={"dp": peer}, device_id_type=pl.DeviceIdType.MESH
        )
    )

    def greet(step, carry):
        other = lax.rem(level + step, tensor_size)
        pl.semaphore_signal(
            barrier, inc=1, device_id={"tensor": other}, device_id_type=pl.DeviceIdType.MESH
        )
        return carry

    lax.fori_loop(1, tensor_size, greet, 0)
    mine = rows_at(me, block_rows)
    for copy in loads(0, 7):
        copy.wait()
    wqkv_ref[mine, :] = jnp.concatenate([q_ref[...], k_ref[...], v_ref[...]], axis=1)
    wo_ref[mine, :] = o_ref[...]
    slab = jnp.concatenate(
        [
            attn_gain_ref[...].astype(f32),
            ffn_gain_ref[...].astype(f32),
            jnp.zeros((6, block_rows), f32),
            router_ref[...].astype(f32),
        ],
        axis=0,
    )
    slab = jnp.concatenate([slab, jnp.zeros((slab.shape[0], LANES - block_rows), f32)], axis=1)
    small_buf[me] = slab.astype(low)

    pl.semaphore_wait(barrier, group_size + tensor_size - 2)

    sibling = 2 * chip + 1 - core

    def weight_copies(peer, source, slot):
        block = rows_at(source, block_rows)
        return [
            remote(wqkv_ref.at[block], wqkv_ref.at[block], w_sems.at[0, slot], w_sems.at[1, source], "dp", peer),
            remote(wo_ref.at[block], wo_ref.at[block], w_sems.at[2, slot], w_sems.at[3, source], "dp", peer),
            remote(small_buf.at[source], small_buf.at[source], w_sems.at[4, slot], w_sems.at[5, source], "dp", peer),
        ]

    def each_chip(body):
        def step(j, carry):
            body(lax.rem(chip + j, chips))
            return carry

        lax.fori_loop(1, chips, step, 0)

    def start_all(copies):
        for copy in copies:
            copy.start()

    def recv_all(copies):
        for copy in copies:
            copy.wait_recv()

    def sent_all(copies):
        for copy in copies:
            copy.wait_send()

    def send_weights(other):
        peer = 2 * other + core
        start_all(weight_copies(peer, me, peer))

    each_chip(send_weights)
    start_all(weight_copies(sibling, me, sibling))

    def block_copy(kind, src, dst, peer, source, count):
        return remote(
            src.at[rows_at(peer, count)],
            dst.at[rows_at(source, count)],
            a2a_sems.at[2 * kind, peer],
            a2a_sems.at[2 * kind + 1, source],
            "dp",
            peer,
        )

    def cot_copy(peer, source):
        return block_copy(0, cot_send_ref, cots_ref, peer, source, capacity)

    def row_copy(peer, source, strip_index, place):
        return remote(
            send_ref.at[strip_index, rows_at(peer, capacity)],
            rows_ref.at[strip_index, rows_at(source, capacity)],
            row_sems.at[2 * place, peer],
            row_sems.at[2 * place + 1, source],
            "dp",
            peer,
        )

    def hand_over(source, strip_index):
        block = rows_ref.at[strip_index, rows_at(source, capacity)]
        return remote(block, block, row_sems.at[4, source], row_sems.at[5, source], "tensor", near)

    def each_source(body):
        def step(j, carry):
            other_chip = lax.rem(chip + j // 2, chips)
            body(2 * other_chip + lax.rem(core + j, 2))
            return carry

        lax.fori_loop(1, group_size, step, 0)

    def back_copy(peer, source):
        return block_copy(2, back_send_ref, back_ref, peer, source, capacity)

    def out_copy(peer, source):
        return block_copy(3, out_send_ref, out_ref, peer, source, capacity)

    def pair_copies(place):
        block = rows_at(2 * place + 1 - core, block_rows)
        return [
            remote(terms_send_ref.at[block], pair_ref.at[place], t_sems.at[0, place], t_sems.at[1, place], "dp", sibling),
            remote(oterms_send_ref.at[block], opair_ref.at[place], t_sems.at[2, place], t_sems.at[3, place], "dp", sibling),
        ]

    def term_copies(target, source):
        peer = 2 * target + core
        block = rows_at(peer, block_rows)
        landing = rows_at(source, block_rows)
        return [
            remote(terms_send_ref.at[block], terms_ref.at[landing], t_sems.at[4, target], t_sems.at[5, source], "dp", peer),
            remote(oterms_send_ref.at[block], oterms_ref.at[landing], t_sems.at[6, target], t_sems.at[7, source], "dp", peer),
        ]

    def gate_copy(peer, source):
        return remote(
            gate_send_ref.at[peer], gate_ref.at[source], a2a_sems.at[12, peer], a2a_sems.at[13, source], "dp", peer
        )

    def late_copy(peer, source):
        return remote(
            late_send_ref, late_ref.at[source], a2a_sems.at[16, peer], a2a_sems.at[17, source], "dp", peer
        )

    def sums_copy(peer, source):
        return remote(
            sums_send_ref, sums_ref.at[source], a2a_sems.at[14, peer], a2a_sems.at[15, source], "dp", peer
        )

    for copy in loads(7, 11):
        copy.wait()
    ids_first = ids_ref[0:1, :]
    ids_second = ids_ref[1:2, :]
    labels = lax.broadcasted_iota(jnp.int32, (experts, token_count), 0)
    member = jnp.logical_or(labels == ids_first, labels == ids_second)
    tokens_r = lax.broadcasted_iota(jnp.int32, (token_count, token_count), 0)
    tokens_c = lax.broadcasted_iota(jnp.int32, (token_count, token_count), 1)
    upper = jnp.where(tokens_r < tokens_c, 1.0, 0.0).astype(low)
    counted = dot(jnp.where(member, 1.0, 0.0).astype(low), upper)
    code_ref[...] = jnp.where(member, counted, -1.0)
    slots = lax.broadcasted_iota(jnp.int32, (capacity, token_count), 0).astype(f32)
    id_total = jnp.broadcast_to((ids_first + ids_second).astype(f32), (LANES, token_count)).astype(low)

    def make_maps(expert, carry):
        block = rows_at(expert, capacity)
        hit = slots == code_ref[pl.ds(expert, 1), :]
        sign = jnp.where(ids_first == expert, 1.0, -1.0)
        both = jnp.where(hit, 1.0, 0.0).astype(low)
        both_ref[block, :] = both
        signed_ref[block, :] = jnp.where(hit, sign, 0.0).astype(low)
        cot_send_ref[block, :model_width] = dot(both, cot_ref[...]).astype(low)
        cot_send_ref[block, model_width:] = dot(both, id_total, ((1,), (1,))).astype(low)
        return carry

    lax.fori_loop(0, experts, make_maps, 0)

    inputs_f = x_ref[...].astype(f32)
    scaled = inputs_f * rms_scale(inputs_f)

    lane = lax.broadcasted_iota(jnp.int32, (heads, token_count), 1)
    wrap_bucket = bucket_vector_at(jnp.where(lane == 0, 0, token_count - lane), NB)
    wrapped = jnp.zeros((heads, token_count), f32)
    for b in range(NB):
        wrapped = jnp.where(wrap_bucket == b, bias_ref[:, b : b + 1], wrapped)

    def pass_on(other):
        source = 2 * other + core
        recv_all(weight_copies(sibling, source, source))
        start_all(weight_copies(sibling, source, 2 * other + 1 - core))

    def take_passed(other):
        source = 2 * other + 1 - core
        recv_all(weight_copies(sibling, source, source))

    each_chip(pass_on)
    recv_all(weight_copies(sibling, sibling, sibling))
    each_chip(take_passed)
    each_peer(lambda peer: cot_copy(peer, me).start())

    gains = jnp.zeros(gains_ref.shape, f32)
    for source in range(group_size):
        slab = jnp.concatenate(
            [small_buf[source].astype(f32), jnp.zeros((gains.shape[0], model_width - LANES), f32)], axis=1
        )
        gains = gains + (pltpu.roll(slab, source * block_rows, 1) if source else slab)
    gains_ref[...] = gains
    gain_one = gains_ref[0:1, :]
    gain_two = gains_ref[1:2, :]
    normed_one_ref[...] = (scaled * gain_one).astype(low)
    qkv_ref[...] = dot(normed_one_ref[...], wqkv_ref[...]).astype(low)

    def at_chunk(c):
        return slice(c * chunk, (c + 1) * chunk)

    per_chunk = chunk // PIECE
    pieces_all = chunks * per_chunk

    def at_piece(i):
        return slice(i * PIECE, (i + 1) * PIECE)

    def pieces_of(c):
        return [None] if c is None else range(c * per_chunk, (c + 1) * per_chunk)

    def line_copy(r, i, hop):
        at = pieces_all if i is None else i
        if hop == 0:
            peer = near
            src, dst = (
                (gate_line_ref.at[0], gate_line_ref.at[1])
                if i is None
                else (part_ref.at[at_piece(i)], near_ref.at[at_piece(i)])
            )
        elif hop == 1:
            peer = across
            src, dst = (
                (gate_line_ref.at[0], gate_line_ref.at[2])
                if i is None
                else (part_ref.at[at_piece(i)], middle_ref.at[r % 2, at_piece(i)])
            )
        else:
            peer = near
            src = dst = gate_line_ref.at[3] if i is None else total_ref.at[r, at_piece(i)]
        return remote(src, dst, line_sems.at[r, 2 * hop, at], line_sems.at[r, 2 * hop + 1, at], "tensor", peer)

    def line_start(r, c):
        @pl.when(is_end)
        def _():
            for i in pieces_of(c):
                line_copy(r, i, 0).start()

    def line_first(r, i):
        line_copy(r, i, 0).wait_recv()
        if i is None:
            gate_line_ref[0] = (gate_line_ref[0].astype(f32) + gate_line_ref[1].astype(f32)).astype(low)
        else:
            block = at_piece(i)
            part_ref[block, :] = (part_ref[block, :].astype(f32) + near_ref[block, :].astype(f32)).astype(low)
        line_copy(r, i, 1).start()

    def line_second(r, i):
        line_copy(r, i, 1).wait_recv()
        if i is None:
            gate_line_ref[3] = (gate_line_ref[0].astype(f32) + gate_line_ref[2].astype(f32)).astype(low)
        else:
            block = at_piece(i)
            total_ref[r, block, :] = (
                part_ref[block, :].astype(f32) + middle_ref[r % 2, block, :].astype(f32)
            ).astype(low)
        line_copy(r, i, 2).start()

    pending = {0: [], 1: [], 2: []}

    def line_serve(r, c):
        @pl.when(is_middle)
        def _():
            for i in pieces_of(c):
                line_first(r, i)
                pending[r].append(i)
                if len(pending[r]) > LAG:
                    line_second(r, pending[r].pop(0))

    def line_flush(r):
        @pl.when(is_middle)
        def _():
            while pending[r]:
                line_second(r, pending[r].pop(0))

    def line_take(r, c):
        @pl.when(is_end)
        def _():
            for i in pieces_of(c):
                line_copy(r, i, 2).wait_recv()

    def line_drain(r, c):
        @pl.when(is_end)
        def _():
            for i in pieces_of(c):
                line_copy(r, i, 0).wait_send()

        @pl.when(is_middle)
        def _():
            for i in pieces_of(c):
                line_copy(r, i, 1).wait_send()
                line_copy(r, i, 2).wait_send()

    for c in range(chunks):
        lo, hi = c * chunk, (c + 1) * chunk
        causal = lax.broadcasted_iota(jnp.int32, (chunk, hi), 0) + lo >= (
            lax.broadcasted_iota(jnp.int32, (chunk, hi), 1)
        )
        pieces = []
        for h in range(heads):
            at = h * HEAD_DIM
            queries = qkv_ref[lo:hi, at : at + HEAD_DIM]
            keys = qkv_ref[0:hi, head_width + at : head_width + at + HEAD_DIM]
            values = qkv_ref[0:hi, 2 * head_width + at : 2 * head_width + at + HEAD_DIM]
            bias = jnp.broadcast_to(wrapped[h : h + 1, :], (chunk, token_count))
            bias = pltpu.roll(bias, lo, 1, stride=1, stride_axis=0)[:, :hi]
            scores = jnp.where(causal, dot(queries, keys, ((1,), (1,))) * factor + bias, MASKED)
            row_max = jnp.max(scores, axis=-1, keepdims=True)
            grown = jnp.exp(scores - row_max)
            total = jnp.sum(grown, axis=-1, keepdims=True)
            probs = (grown * (1.0 / total)).astype(low)
            probs_ref[h, lo:hi, 0:hi] = probs
            pieces.append(dot(probs, values).astype(low))
        context = jnp.concatenate(pieces, axis=1)
        context_ref[lo:hi, :] = context
        part_ref[lo:hi, :] = dot(context, wo_ref[...], ((1,), (1,))).astype(low)
        line_start(0, c)
        if c >= 1:
            line_serve(0, c - 1)
    line_serve(0, chunks - 1)
    line_flush(0)

    for c in range(chunks):
        block = at_chunk(c)
        line_take(0, c)
        residual = x_ref[block, :].astype(f32) + total_ref[0, block, :].astype(f32)
        residual_ref[block, :] = residual
        normed = (residual * rms_scale(residual) * gain_two).astype(low)
        normed_ref[block, :] = normed
        for k in range(model_width // strip):
            strips_ref[k, block, :] = normed[:, k * strip : (k + 1) * strip]

    def send_strip(strip_index, place):
        def body(peer):
            block = rows_at(peer, capacity)
            send_ref[strip_index, block, :] = dot(both_ref[block, :], strips_ref[strip_index]).astype(low)
            row_copy(peer, me, strip_index, place).start()

        each_peer(body)

    shared = 1 + half
    send_strip(shared, 0)
    send_strip(0, 1)

    def forward(source):
        row_copy(source, source, shared, 0).wait_recv()
        hand_over(source, shared).start()

    each_source(forward)
    own = rows_at(me, capacity)
    for k in range(model_width // strip):
        rows_ref[k, own, :] = dot(both_ref[own, :], strips_ref[k]).astype(low)
    cots_ref[own, :] = cot_send_ref[own, :]

    gains_low = gains_ref[...].astype(low)
    logits = dot(gains_low, normed_ref[...], ((1,), (1,)))
    label_rows = lax.broadcasted_iota(jnp.int32, logits.shape, 0) - 8
    chosen_first = jnp.sum(jnp.where(label_rows == ids_first, logits, 0.0), axis=0, keepdims=True)
    chosen_second = jnp.sum(jnp.where(label_rows == ids_second, logits, 0.0), axis=0, keepdims=True)
    gate_first = jax.nn.sigmoid(chosen_first - chosen_second)
    gate_second = 1.0 - gate_first
    gates_ref[0:1, :] = gate_first
    gates_ref[1:2, :] = gate_second

    def make_gated(expert, carry):
        block = rows_at(expert, capacity)
        sign = signed_ref[block, :].astype(f32)
        gated_ref[block, :] = jnp.where(sign > 0, gate_first, jnp.where(sign < 0, gate_second, 0.0)).astype(low)
        return carry

    lax.fori_loop(0, experts, make_gated, 0)
    for z in range(tensor_size):

        @pl.when(level == z)
        def _():
            residual_t_ref[...] = jnp.transpose(residual_ref[:, z * column_width : (z + 1) * column_width])

    load_in().wait()
    load_out().wait()

    pair = 2 * capacity
    ones = jnp.ones((16, model_width), low)

    def expert_step(step, carry):
        other = lax.rem(chip + step, chips)
        block = rows_at(other, pair)
        for c in range(2):
            source = 2 * other + c

            @pl.when(source != me)
            def _():
                cot_copy(source, source).wait_recv()
                row_copy(source, source, 0, 1).wait_recv()
                hand_over(source, 2 - half).wait_recv()

        rows = jnp.concatenate([rows_ref[k, block, :] for k in range(model_width // strip)], axis=1)
        value, slope = gelu_both(dot(rows, win_ref[...]))
        active = value.astype(low)
        active_ref[block, :] = active
        owner_logits = dot(rows, gains_low, ((1,), (1,)))
        columns = lax.broadcasted_iota(jnp.int32, owner_logits.shape, 1) - 8
        other_ids = cots_ref[block, model_width : model_width + 1].astype(f32).astype(jnp.int32) - me
        own_logit = jnp.sum(jnp.where(columns == me, owner_logits, 0.0), axis=1, keepdims=True)
        other_logit = jnp.sum(jnp.where(columns == other_ids, owner_logits, 0.0), axis=1, keepdims=True)
        row_gate = jax.nn.sigmoid(own_logit - other_logit)
        cot = cots_ref[block, :model_width].astype(f32)
        drows = (row_gate * cot).astype(low)
        drows_ref[block, :] = drows
        dpre = (dot(drows, wout_ref[...], ((1,), (1,))) * slope).astype(low)
        dpre_ref[block, :] = dpre
        back_send_ref[block, :] = dot(dpre, win_ref[...], ((1,), (1,))).astype(low)
        for c in range(2):
            source = 2 * other + c

            @pl.when(source != me)
            def _():
                back_copy(source, me).start()

        owner_out = dot(active, wout_ref[...])
        out_send_ref[block, :] = owner_out.astype(low)
        agree = (cot * owner_out).astype(low)
        for c in range(2):
            source = 2 * other + c
            gate_send_ref[source] = dot(ones, agree[c * capacity : (c + 1) * capacity, :], ((1,), (1,))).astype(low)

            @pl.when(source != me)
            def _():
                gate_copy(source, me).start()

        return carry

    lax.fori_loop(0, chips, expert_step, 0)
    back_ref[own, :] = back_send_ref[own, :]
    out_ref[own, :] = out_send_ref[own, :]
    gate_ref[me] = gate_send_ref[me]

    def grad_out(which, part):
        target = (out_grad_hbm, in_grad_hbm)[which]
        block = slice(part * 256, (part + 1) * 256)
        return pltpu.make_async_copy(grad_ref.at[which, block], target.at[block], local_sems.at[2 + which * 8 + part])

    parts = win_ref.shape[0] // 256
    for part in range(parts):
        block = slice(part * 256, (part + 1) * 256)
        grad_ref[0, block, :] = dot(active_ref[:, block], drows_ref[...], ((0,), (0,)))
        grad_out(0, part).start()
        grad_ref[1, block, :] = dot(rows_ref[part], dpre_ref[...], ((0,), (0,)))
        grad_out(1, part).start()

    each_peer(lambda source: gate_copy(source, source).wait_recv())
    each_peer(lambda source: back_copy(source, source).wait_recv())
    each_peer(lambda peer: out_copy(peer, me).start())
    gate_line = dot(gate_ref[0], signed_ref[0:capacity, :])
    for e in range(1, experts):
        gate_line = gate_line + dot(gate_ref[e], signed_ref[e * capacity : (e + 1) * capacity, :])
    gate_line_ref[0] = gate_line.astype(low)
    line_start(1, None)
    order = list(range(chunks))[::-1]
    queue = [None] + order
    for place, c in enumerate(queue):
        if c is not None:
            block = at_chunk(c)
            line_drain(0, c)
            part_ref[block, :] = dot(both_ref[:, block], back_ref[...], ((0,), (0,))).astype(low)
            line_start(1, c)
        if place >= 1:
            line_serve(1, queue[place - 1])
    line_serve(1, queue[-1])
    line_flush(1)

    line_take(1, None)
    gate_diff = gate_line_ref[3, 0:1, :].astype(f32)
    dlogit = gate_diff * gates_ref[0:1, :] * gates_ref[1:2, :]
    dlogits = jnp.where(
        label_rows == ids_first, dlogit, jnp.where(label_rows == ids_second, -dlogit, 0.0)
    ).astype(low)
    sums_send_ref[...] = dot(dlogits, normed_ref[...])

    def backward_chunk(c, ffn_term):
        lo, hi = c * chunk, (c + 1) * chunk
        block = at_chunk(c)
        line_take(1, c)
        dnormed = total_ref[1, block, :].astype(f32) + dot(dlogits[:, block], gains_low, ((0,), (0,)))
        residual = residual_ref[block, :]
        scale_two = rms_scale(residual)
        ffn_term = ffn_term + jnp.sum(dnormed * residual * scale_two, axis=0, keepdims=True)
        dres = cot_ref[block, :].astype(f32) + norm_back(dnormed, residual, scale_two, gain_two)
        dres_ref[block, :] = dres
        dres_low = dres.astype(low)
        dres_low_ref[block, :] = dres_low
        dcontext = dot(dres_low, wo_ref[...]).astype(low)
        flip = (
            lax.broadcasted_iota(jnp.int32, (chunk, chunk), 0)
            + lax.broadcasted_iota(jnp.int32, (chunk, chunk), 1)
            == chunk - 1
        )
        flip = jnp.where(flip, 1.0, 0.0).astype(low)
        first, second, third = [], [], []
        for h in range(heads):
            at = h * HEAD_DIM
            queries = qkv_ref[lo:hi, at : at + HEAD_DIM]
            keys = qkv_ref[0:hi, head_width + at : head_width + at + HEAD_DIM]
            values = qkv_ref[0:hi, 2 * head_width + at : 2 * head_width + at + HEAD_DIM]
            dctx = dcontext[:, at : at + HEAD_DIM]
            probs = probs_ref[h, lo:hi, 0:hi]
            weights = probs.astype(f32)
            dweights = dot(dctx, values, ((1,), (1,)))
            agreement = jnp.sum(weights * dweights, axis=-1, keepdims=True)
            dscores = (weights * (dweights - agreement)).astype(low)
            first.append((factor * dot(dscores, keys)).astype(low))
            dkeys = dot(dscores, queries, ((0,), (0,)))
            dvalues = dot(probs, dctx, ((0,), (0,)))
            if c < chunks - 1:
                dkeys = dkeys + dkeys_ref[h, 0:hi, :]
                dvalues = dvalues + dvalues_ref[h, 0:hi, :]
            if lo:
                dkeys_ref[h, 0:lo, :] = dkeys[0:lo]
                dvalues_ref[h, 0:lo, :] = dvalues[0:lo]
            second.append((factor * dkeys[lo:hi]).astype(low))
            third.append(dvalues[lo:hi].astype(low))
            flipped = dot(flip, dscores)
            if hi < token_count:
                flipped = jnp.concatenate([flipped, jnp.zeros((chunk, token_count - hi), f32)], axis=1)
            skewed = pltpu.roll(flipped, token_count - (hi - 1), 1, stride=1, stride_axis=0)
            line = jnp.sum(skewed, axis=0, keepdims=True)
            if c < chunks - 1:
                line = line + diagonal_ref[h : h + 1, :]
            diagonal_ref[h : h + 1, :] = line
        dqkv = jnp.concatenate(first + second + third, axis=1)
        dqkv_ref[block, :] = dqkv
        line_drain(1, c)
        part_ref[block, :] = dot(dqkv, wqkv_ref[...], ((1,), (1,))).astype(low)
        line_start(2, c)
        return ffn_term

    ffn_term = jnp.zeros((1, model_width), f32)
    for place, c in enumerate(order):
        ffn_term = backward_chunk(c, ffn_term)
        if place >= 1:
            line_serve(2, order[place - 1])

    for part in range(model_width // 256):
        block = slice(part * 256, (part + 1) * 256)
        terms_send_ref[block, :] = dot(normed_one_ref[:, block], dqkv_ref[...], ((0,), (0,))).astype(low)
        oterms_send_ref[block, :] = dot(dres_low_ref[:, block], context_ref[...], ((0,), (0,))).astype(low)
        if part == 0:
            line_serve(2, order[-1])
        if part == 1:
            line_flush(2)
    for place in range(chips):
        start_all(pair_copies(place))

    def pass_terms():
        for place in range(chips):
            recv_all(pair_copies(place))
            block = rows_at(2 * place + core, block_rows)
            terms_send_ref[block, :] = (
                terms_send_ref[block, :].astype(f32) + pair_ref[place].astype(f32)
            ).astype(low)
            oterms_send_ref[block, :] = (
                oterms_send_ref[block, :].astype(f32) + opair_ref[place].astype(f32)
            ).astype(low)
        each_chip(lambda other: start_all(term_copies(other, chip)))
        terms_ref[rows_at(chip, block_rows), :] = terms_send_ref[mine, :]
        oterms_ref[rows_at(chip, block_rows), :] = oterms_send_ref[mine, :]

    each_peer(lambda source: out_copy(source, source).wait_recv())
    for part in range(model_width // 256):
        block = slice(part * 256, (part + 1) * 256)
        mix_send_ref[block, :] = dot(out_ref[:, block], gated_ref[...], ((0,), (0,))).astype(low)
        if part == 0:
            pass_terms()
    side = level // 2
    end_level = side * (tensor_size - 1)
    middle_level = 1 + side
    away = [2 * (1 - side), 2 * (1 - side) + 1]

    def mix_at(target):
        return rows_at(target, column_width)

    def mix_copy(place, target, peer):
        return remote(
            mix_send_ref.at[mix_at(target)],
            mix_ref.at[place],
            z_sems.at[0, place],
            z_sems.at[1, place],
            "tensor",
            peer,
        )

    def mix_add(target, place):
        mix_send_ref[mix_at(target), :] = (
            mix_send_ref[mix_at(target), :].astype(f32) + mix_ref[place].astype(f32)
        ).astype(low)

    up_order = [away[0], away[1], middle_level]

    @pl.when(is_end)
    def _():
        for place, target in enumerate(up_order):
            mix_copy(place, target, near).start()

    sums_send_ref[0:1, :] = ffn_term
    diagonal = diagonal_ref[0:heads, :]
    lanes = lax.broadcasted_iota(jnp.int32, (heads, model_width), 1)
    bias_rows = jnp.zeros((heads, model_width), f32)
    for b in range(NB):
        bucket_total = jnp.sum(jnp.where(wrap_bucket == b, diagonal, 0.0), axis=1, keepdims=True)
        bias_rows = jnp.where(lanes == b, bucket_total, bias_rows)
    sums_send_ref[2 : 2 + heads, :] = bias_rows
    each_peer(lambda peer: sums_copy(peer, me).start())
    sums_ref[me] = sums_send_ref[...]

    @pl.when(is_middle)
    def _():
        for place in range(2):
            mix_copy(place, up_order[place], near).wait_recv()
            mix_add(up_order[place], place)
            mix_copy(3 + place, up_order[place], across).start()

    attn_term = jnp.zeros((1, model_width), f32)
    for c in order:
        block = at_chunk(c)
        line_take(2, c)
        dnormed = total_ref[2, block, :].astype(f32)
        values = x_ref[block, :].astype(f32)
        scale_one = rms_scale(values)
        attn_term = attn_term + jnp.sum(dnormed * values * scale_one, axis=0, keepdims=True)
        dres_ref[block, :] = dres_ref[block, :] + norm_back(dnormed, values, scale_one, gain_one)

    late_send_ref[...] = jnp.broadcast_to(attn_term, late_send_ref.shape)
    each_peer(lambda peer: late_copy(peer, me).start())
    late_ref[me] = late_send_ref[...]

    for z in range(tensor_size):

        @pl.when(level == z)
        def _():
            input_out[...] = jnp.transpose(dres_ref[:, z * column_width : (z + 1) * column_width])

    @pl.when(is_middle)
    def _():
        own_side = [2 * side, 2 * side + 1]
        for place in range(2):
            mix_copy(3 + place, own_side[place], across).wait_recv()
            mix_add(own_side[place], 3 + place)
        mix_copy(5, end_level, near).start()
        mix_copy(2, middle_level, near).wait_recv()
        mix_add(middle_level, 2)

    stores()[0].start()
    each_chip(lambda source: recv_all(term_copies(source, source)))
    reduced = terms_ref[0:block_rows, :].astype(f32)
    oreduced = oterms_ref[0:block_rows, :].astype(f32)
    for source in range(1, chips):
        block = slice(source * block_rows, (source + 1) * block_rows)
        reduced = reduced + terms_ref[block, :].astype(f32)
        oreduced = oreduced + oterms_ref[block, :].astype(f32)
    for k in range(3):
        qkv_out[k] = reduced[:, k * head_width : (k + 1) * head_width]
    wo_out[...] = oreduced
    stores()[1].start()
    stores()[2].start()

    @pl.when(is_end)
    def _():
        mix_copy(5, level, near).wait_recv()
        mix_add(level, 5)

    mixture = mix_send_ref[mix_at(level), :].astype(f32)
    block_out[...] = (residual_t_ref[...] + mixture).astype(low)
    stores()[3].start()

    each_peer(lambda source: sums_copy(source, source).wait_recv())
    sums = sums_ref[0]
    for source in range(1, group_size):
        sums = sums + sums_ref[source]
    sums_out[...] = sums
    stores()[4].start()
    each_peer(lambda source: late_copy(source, source).wait_recv())
    late = late_ref[0]
    for source in range(1, group_size):
        late = late + late_ref[source]
    late_out[...] = late
    stores()[5].start()

    def drain(peer):
        late_copy(peer, me).wait_send()
        sent_all(weight_copies(peer, me, peer))
        cot_copy(peer, me).wait_send()
        row_copy(peer, me, shared, 0).wait_send()
        row_copy(peer, me, 0, 1).wait_send()
        hand_over(peer, shared).wait_send()
        back_copy(peer, me).wait_send()
        gate_copy(peer, me).wait_send()
        out_copy(peer, me).wait_send()
        sums_copy(peer, me).wait_send()

    each_peer(drain)
    each_chip(lambda other: sent_all(term_copies(other, chip)))
    for place in range(chips):
        sent_all(pair_copies(place))

    @pl.when(is_end)
    def _():
        for place, target in enumerate(up_order):
            mix_copy(place, target, near).wait_send()

    @pl.when(is_middle)
    def _():
        for place in range(2):
            mix_copy(3 + place, up_order[place], across).wait_send()
        mix_copy(5, end_level, near).wait_send()

    line_drain(1, None)
    for c in order:
        line_drain(2, c)
    for part in range(parts):
        grad_out(0, part).wait()
        grad_out(1, part).wait()
    for copy in stores():
        copy.wait()


def run_layer(group_size, tensor_size, capacity, x, q, k, v, o, attn_gain, ffn_gain, router, bias, ids, cot, w_in, w_out):
    tokens, width = x.shape
    block_rows, head_width = q.shape
    small_rows = 8 + router.shape[0]
    heads = bias.shape[0]
    hidden = w_in.shape[1]
    slots = group_size * capacity
    low = jnp.bfloat16
    f32 = jnp.float32
    full = group_size * block_rows
    chunks = tokens // LANES
    column_width = width // tensor_size

    def shape(dims, dtype=low):
        return jax.ShapeDtypeStruct(dims, dtype)

    def room(*dims, dtype=low):
        return pltpu.VMEM(dims, dtype)

    hbm = pl.BlockSpec(memory_space=pl.ANY)
    dma = pltpu.SemaphoreType.DMA
    return pl.pallas_call(
        functools.partial(layer_kernel, group_size, tensor_size),
        out_shape=(
            shape((column_width, tokens)),
            shape((column_width, tokens), f32),
            shape((3, block_rows, head_width), f32),
            shape((block_rows, head_width), f32),
            shape((small_rows, width), f32),
            shape((8, width), f32),
            shape((width, hidden), f32),
            shape((hidden, width), f32),
        ),
        in_specs=[hbm] * 13,
        out_specs=(hbm,) * 8,
        scratch_shapes=[
            room(full, 3 * head_width),
            room(full, head_width),
            room(small_rows, width, dtype=f32),
            room(tokens, 3 * head_width),
            room(heads, tokens, tokens),
            room(tokens, head_width),
            room(tokens, width),
            room(tokens, width),
            room(tokens, width, dtype=f32),
            room(column_width, tokens, dtype=f32),
            room(slots, tokens),
            room(slots, tokens),
            room(slots, tokens),
            room(width // 256, tokens, 256),
            room(width // 256, slots, 256),
            room(slots, width + LANES),
            room(width, hidden),
            room(hidden, width),
            room(slots, hidden),
            room(slots, width),
            room(slots, hidden),
            room(2, width, width, dtype=f32),
            room(width // 256, slots, 256),
            room(slots, width + LANES),
            room(slots, width),
            room(slots, width),
            room(slots, width),
            room(slots, width),
            room(group_size, 16, capacity),
            room(group_size, 16, capacity),
            room(group_size, small_rows, LANES),
            room(group_size, tokens, dtype=f32),
            room(8, tokens, dtype=f32),
            room(tokens, width),
            room(tokens, width),
            room(2, tokens, width),
            room(3, tokens, width),
            room(4, 16, tokens),
            room(tokens, width, dtype=f32),
            room(tokens, width),
            room(heads, tokens, HEAD_DIM, dtype=f32),
            room(heads, tokens, HEAD_DIM, dtype=f32),
            room(tokens, 3 * head_width),
            room(8, tokens, dtype=f32),
            room(full, 3 * head_width),
            room(full // 2, 3 * head_width),
            room(full, head_width),
            room(full // 2, head_width),
            room(group_size // 2, block_rows, 3 * head_width),
            room(group_size // 2, block_rows, head_width),
            room(width, tokens),
            room(6, column_width, tokens),
            room(small_rows, width, dtype=f32),
            room(group_size, small_rows, width, dtype=f32),
            room(8, width, dtype=f32),
            room(group_size, 8, width, dtype=f32),
            *[room(*a.shape, dtype=a.dtype) for a in (x, q, k, v, o, attn_gain, ffn_gain, router, bias, ids, cot)],
            room(column_width, tokens),
            room(column_width, tokens, dtype=f32),
            room(3, block_rows, head_width, dtype=f32),
            room(block_rows, head_width, dtype=f32),
            room(small_rows, width, dtype=f32),
            room(8, width, dtype=f32),
            dma((11,)),
            dma((6,)),
            dma((6, group_size)),
            dma((8, group_size // 2)),
            dma((6, group_size)),
            dma((18, group_size)),
            dma((3, 6, tokens // PIECE + 1)),
            dma((2, 6)),
            dma((18,)),
        ],
        compiler_params=pltpu.CompilerParams(
            collective_id=0, has_side_effects=True, vmem_limit_bytes=VMEM_BYTES
        ),
        name="layer",
    )(x, q, k, v, o, attn_gain, ffn_gain, router, bias, ids, cot, w_in, w_out)


def finish_kernel(group_size, *refs):
    sources, targets = refs[:8], refs[8:20]
    held, built = refs[20:28], refs[28:36]
    in_sems, out_sems = refs[36:]
    me = lax.axis_index("dp")

    def pieces(src, dst, sems, at):
        count = 4 if at >= 6 else 1
        rows = src.shape[0] // count
        return [
            pltpu.make_async_copy(src.at[pl.ds(p * rows, rows)], dst.at[pl.ds(p * rows, rows)], sems.at[at, p])
            for p in range(count)
        ]

    taken = [pieces(src, dst, in_sems, at) for at, (src, dst) in enumerate(zip(sources, held))]
    for group in taken:
        for copy in group:
            copy.start()
    block, inputs, qkv, wo, sums, late, in_grad, out_grad = held
    q_o, k_o, v_o, attn_o, ffn_o, router_o, bias_o = built[:7]
    (block_out, input_out, q_out, k_out, v_out, wo_out, attn_out, ffn_out, router_out, bias_out, in_out, out_out) = targets
    given = []

    def give(src, dst, at):
        for copy in pieces(src, dst, out_sems, at):
            copy.start()
            given.append(copy)

    for at in range(6):
        for copy in taken[at]:
            copy.wait()
    give(block, block_out, 0)
    give(inputs, input_out, 1)
    for k, (src, dst) in enumerate(((q_o, q_out), (k_o, k_out), (v_o, v_out))):
        src[...] = qkv[k]
        give(src, dst, 2 + k)
    give(wo, wo_out, 5)
    for at, (src, dst) in ((6, (in_grad, in_out)), (7, (out_grad, out_out))):
        for p, copy in enumerate(taken[at]):
            copy.wait()
            out = pieces(src, dst, out_sems, at)[p]
            out.start()
            given.append(out)
    block_rows = wo.shape[0]
    heads, buckets = bias_o.shape
    features = sums.shape[1]
    shift = lax.rem((group_size - me) * block_rows, features)
    total = sums[...]
    bias_o[...] = total[2 : 2 + heads, :buckets]
    total = pltpu.roll(total, shift, 1)
    ffn_o[...] = total[0:1, :block_rows]
    router_o[...] = total[8:, :block_rows]
    attn_o[...] = pltpu.roll(late[...], shift, 1)[0:1, :block_rows]
    for k, (src, dst) in enumerate(((attn_o, attn_out), (ffn_o, ffn_out), (router_o, router_out), (bias_o, bias_out))):
        copy = pltpu.make_async_copy(src, dst, out_sems.at[8 + k, 0])
        copy.start()
        given.append(copy)
    for copy in given:
        copy.wait()


def finish(group_size, heads, buckets, *results):
    f32 = jnp.float32
    block, inputs, qkv, wo, sums, late, in_grad, out_grad = results
    block_rows = wo.shape[0]

    def shape(*dims):
        return jax.ShapeDtypeStruct(dims, f32)

    small = [(1, block_rows), (1, block_rows), (sums.shape[0] - 8, block_rows), (heads, buckets)]
    hbm = pl.BlockSpec(memory_space=pl.ANY)
    return pl.pallas_call(
        functools.partial(finish_kernel, group_size),
        out_shape=(
            jax.ShapeDtypeStruct(block.shape, block.dtype),
            shape(*inputs.shape),
            *[shape(*wo.shape)] * 4,
            *[shape(*dims) for dims in small],
            shape(*in_grad.shape),
            shape(*out_grad.shape),
        ),
        in_specs=[hbm] * 8,
        out_specs=(hbm,) * 12,
        scratch_shapes=[
            *[pltpu.VMEM(a.shape, a.dtype) for a in results],
            *[pltpu.VMEM(wo.shape, f32)] * 3,
            *[pltpu.VMEM(dims, f32) for dims in small],
            pltpu.VMEM((8, LANES), f32),
            pltpu.SemaphoreType.DMA((8, 4)),
            pltpu.SemaphoreType.DMA((12, 4)),
        ],
        compiler_params=pltpu.CompilerParams(vmem_limit_bytes=VMEM_BYTES),
        name="finish",
    )(*results)


def on_device_general(
    block_input,
    attn_gain,
    query_weight,
    key_weight,
    value_weight,
    output_weight,
    bias_table,
    ffn_gain,
    router_weight,
    expert_in,
    expert_out,
    expert_ids,
    out_cotangent,
):
    tensor_size = lax.axis_size("tensor")
    group_size = lax.axis_size("dp")
    tensor_index = lax.axis_index("tensor")
    own_expert = lax.axis_index("dp")
    token_count, model_width = block_input.shape
    column_width = model_width // tensor_size
    column_start = tensor_index * column_width
    expert_count = group_size * expert_in.shape[0]
    capacity = tensor_size * max(1, 3 * token_count // (5 * expert_count))
    slot_rows = expert_count * capacity
    seq_count = token_count // SEQ_LEN
    head_local = bias_table.shape[0]
    head_width = head_local * HEAD_DIM
    block_rows = query_weight.shape[0]
    low = jnp.bfloat16

    def own_columns(matrix):
        return lax.dynamic_slice_in_dim(matrix, column_start, column_width, 1)

    packed = jnp.concatenate(
        [
            query_weight,
            key_weight,
            value_weight,
            output_weight,
            router_weight,
            attn_gain[:, None],
            ffn_gain[:, None],
        ],
        axis=1,
    )
    packed = lax.all_gather(packed, "dp", axis=0, tiled=True)

    labels = jnp.arange(expert_count, dtype=jnp.int32)
    flat_ids = expert_ids.reshape(-1)
    ids_onehot = (flat_ids[:, None] == labels[None, :]).astype(jnp.int32)
    pair_rows = lax.broadcasted_iota(jnp.int32, (2 * token_count, 2 * token_count), 0)
    pair_cols = lax.broadcasted_iota(jnp.int32, (2 * token_count, 2 * token_count), 1)
    before = (pair_cols < pair_rows).astype(low)
    earlier = dot(before, ids_onehot.astype(low)).astype(jnp.int32)
    slot_index = jnp.sum(earlier * ids_onehot, axis=1)
    places = (flat_ids * capacity + slot_index).reshape(token_count, 2)
    place_rows = jnp.arange(slot_rows, dtype=jnp.int32)
    at_first = places[:, 0][None, :] == place_rows[:, None]
    at_second = places[:, 1][None, :] == place_rows[:, None]
    map_first = at_first.astype(low)
    map_second = at_second.astype(low)
    map_both = (at_first | at_second).astype(low)

    ids_low = jnp.broadcast_to(expert_ids.astype(low)[:, :, None], (token_count, 2, LANES))
    cot_source = jnp.concatenate(
        [
            jnp.concatenate([out_cotangent, ids_low[:, 1]], axis=1),
            jnp.concatenate([out_cotangent, ids_low[:, 0]], axis=1),
        ],
        axis=0,
    )
    cot_parcel = dot(jnp.concatenate([map_first, map_second], axis=1), cot_source).astype(low)
    packed, cot_parcel = lax.optimization_barrier((packed, cot_parcel))
    cot_arrived = exchange(
        cot_parcel.reshape(expert_count, capacity, model_width + LANES)
    ).reshape(slot_rows, model_width + LANES)
    cot_rows = cot_arrived[:, :model_width].astype(jnp.float32)
    other_ids = cot_arrived[:, model_width].astype(jnp.int32)

    qkv_full = packed[:, : 3 * head_width]
    output_full = packed[:, 3 * head_width : 4 * head_width]
    at = 4 * head_width
    router_full = packed[:, at : at + expert_count]
    gain_one = packed[:, at + expert_count].astype(jnp.float32)
    gain_two = packed[:, at + expert_count + 1].astype(jnp.float32)
    inputs_f = block_input.astype(jnp.float32)
    scale_one = rms_scale(inputs_f)
    normed_one = (inputs_f * scale_one * gain_one).astype(low)
    qkv = dot(normed_one, qkv_full).astype(low)
    bucket_vec = bucket_vector_at(jnp.arange(SEQ_LEN, dtype=jnp.int32), NB)
    bucket_labels = jnp.arange(NB, dtype=jnp.int32)
    wrap = (SEQ_LEN - jnp.arange(SEQ_LEN, dtype=jnp.int32)) % SEQ_LEN
    wrapped_onehot = bucket_vector_at(wrap, NB)[None, :] == bucket_labels[:, None]
    wrapped = jnp.sum(
        jnp.where(wrapped_onehot[None], bias_table[:, :, None], 0.0), axis=1
    )
    context, probs = attend_forward(qkv, wrapped, seq_count, head_local)
    attn_part = dot(context, output_full, ((1,), (1,))).astype(low)
    attn_out = lax.psum(attn_part, "tensor").astype(jnp.float32)
    residual = inputs_f + attn_out
    scale_two = rms_scale(residual)
    normed_two = (residual * scale_two * gain_two).astype(low)

    logits = dot(normed_two, router_full)
    picked = (expert_ids[:, :, None] == labels[None, None, :]).astype(jnp.float32)
    chosen = jnp.sum(picked * logits[:, None, :], axis=2)
    first_gate = jax.nn.sigmoid(chosen[:, 0] - chosen[:, 1])
    second_gate = 1.0 - first_gate

    weight_in = expert_in[0]
    weight_out = expert_out[0]
    parcel = dot(map_both, normed_two).astype(low)
    expert_rows = exchange(parcel.reshape(expert_count, capacity, model_width)).reshape(
        slot_rows, model_width
    )
    pre_act = dot(expert_rows, weight_in)
    active, pullback = jax.vjp(jax.nn.gelu, pre_act)
    active = active.astype(low)
    owner_out = dot(active, weight_out)
    owner_logits = dot(expert_rows, router_full)
    own_logit = jnp.sum(
        jnp.where(labels[None, :] == own_expert, owner_logits, 0.0), axis=1
    )
    other_logit = jnp.sum(
        jnp.where(labels[None, :] == other_ids[:, None], owner_logits, 0.0), axis=1
    )
    row_gate = jax.nn.sigmoid(own_logit - other_logit)
    expert_drows = (row_gate[:, None] * cot_rows).astype(low)
    dpre = pullback(dot(expert_drows, weight_out, ((1,), (1,))))[0].astype(low)
    owner_back = dot(dpre, weight_in, ((1,), (1,))).astype(low)
    gate_part = jnp.sum(cot_rows * owner_out, axis=1, keepdims=True).astype(low)
    back_parcel = jnp.concatenate(
        [owner_back, jnp.broadcast_to(gate_part, (slot_rows, LANES))], axis=1
    )
    back_rows = exchange(
        back_parcel.reshape(group_size, capacity, model_width + LANES)
    ).reshape(slot_rows, model_width + LANES)
    out_rows = exchange(
        owner_out.astype(low).reshape(group_size, capacity, model_width)
    ).reshape(slot_rows, model_width)
    out_grad = dot(active, expert_drows, ((0,), (0,)))
    in_grad = dot(expert_rows, dpre, ((0,), (0,)))

    dnormed_part = dot(map_both, back_rows[:, :model_width], ((0,), (0,)))
    gate_diff_part = dot(map_first - map_second, back_rows[:, model_width:], ((0,), (0,)))
    gate_rows = -(-token_count // model_width)
    gate_line = jnp.pad(gate_diff_part[:, 0], (0, gate_rows * model_width - token_count))
    summed = lax.psum(
        jnp.concatenate(
            [dnormed_part, gate_line.reshape(gate_rows, model_width)], axis=0
        ).astype(low),
        "tensor",
    ).astype(jnp.float32)
    gate_diff = summed[token_count:].reshape(-1)[:token_count]
    mixture_part = first_gate[:, None] * dot(map_first, out_rows, ((0,), (0,)))
    mixture_part = mixture_part + second_gate[:, None] * dot(
        map_second, out_rows, ((0,), (0,))
    )
    mixture_parts = mixture_part.astype(low).reshape(token_count, tensor_size, column_width)
    mixture_parts = jnp.swapaxes(mixture_parts, 0, 1)

    dlogit = gate_diff * first_gate * second_gate
    signed = jnp.stack([dlogit, -dlogit], axis=1)
    dlogits = jnp.sum(picked * signed[:, :, None], axis=1).astype(low)
    router_term = dot(normed_two, dlogits, ((0,), (0,)))
    dnormed_two = summed[:token_count] + dot(dlogits, router_full, ((1,), (1,)))
    ffn_term = jnp.sum(dnormed_two * residual * scale_two, axis=0)
    cot_f = out_cotangent.astype(jnp.float32)
    dresidual = cot_f + norm_back(dnormed_two, residual, scale_two, gain_two)
    dres_low = dresidual.astype(low)
    mixture_parts, dres_low = lax.optimization_barrier((mixture_parts, dres_low))
    mixture_parts = lax.all_to_all(
        mixture_parts, "tensor", split_axis=0, concat_axis=0, tiled=True
    )

    output_term = dot(dres_low, context, ((0,), (0,)))
    dcontext = dot(dres_low, output_full).astype(low)
    dqkv, diagonal = attend_backward(qkv, probs, dcontext, seq_count, head_local)
    reverse_onehot = (bucket_vec[::-1][:, None] == bucket_labels[None, :]).astype(jnp.float32)
    bias_term = jnp.dot(
        jnp.sum(diagonal, axis=0),
        reverse_onehot,
        precision=lax.Precision.HIGHEST,
        preferred_element_type=jnp.float32,
    )
    dnormed_part = dot(dqkv, qkv_full, ((1,), (1,))).astype(low)
    dnormed_part, mixture_parts = lax.optimization_barrier((dnormed_part, mixture_parts))
    dnormed_one = lax.psum(dnormed_part, "tensor").astype(jnp.float32)
    qkv_term = dot(normed_one, dqkv, ((0,), (0,)))
    bias_count = bias_term.size
    bias_cols = -(-bias_count // block_rows)
    bias_block = jnp.pad(bias_term.reshape(-1), (0, bias_cols * block_rows - bias_count))
    bias_block = jnp.tile(bias_block.reshape(block_rows, bias_cols), (group_size, 1))
    terms = jnp.concatenate(
        [qkv_term, output_term, router_term, ffn_term[:, None], bias_block],
        axis=1,
    ).astype(low)
    term_width = terms.shape[1]
    arrived = exchange(terms.reshape(group_size, block_rows, term_width))
    arrived, dnormed_one = lax.optimization_barrier((arrived, dnormed_one))
    mixture = jnp.sum(mixture_parts.astype(jnp.float32), axis=0)
    block_output = (own_columns(residual) + mixture).astype(low)
    reduced = jnp.sum(arrived.astype(jnp.float32), axis=0)
    at = 4 * head_width
    grads = [reduced[:, k * head_width : (k + 1) * head_width] for k in range(4)]
    router_grad = reduced[:, at : at + expert_count]
    at = at + expert_count
    bias_grad = reduced[:, at + 1 :].reshape(-1)[:bias_count].reshape(bias_term.shape)
    attn_term = jnp.sum(dnormed_one * inputs_f * scale_one, axis=0)
    attn_gain_grad = jnp.sum(exchange(attn_term.reshape(group_size, block_rows)), axis=0)
    first_back = norm_back(dnormed_one, inputs_f, scale_one, gain_one)
    input_grad = own_columns(dresidual + first_back)
    return (
        block_output,
        input_grad,
        attn_gain_grad,
        grads[0],
        grads[1],
        grads[2],
        grads[3],
        bias_grad,
        reduced[:, at],
        router_grad,
        in_grad[None],
        out_grad[None],
    )


def on_device(
    block_input,
    attn_gain,
    query_weight,
    key_weight,
    value_weight,
    output_weight,
    bias_table,
    ffn_gain,
    router_weight,
    expert_in,
    expert_out,
    expert_ids,
    out_cotangent,
):
    tensor_size = lax.axis_size("tensor")
    group_size = lax.axis_size("dp")
    token_count = block_input.shape[0]
    block_rows = query_weight.shape[0]
    head_local = bias_table.shape[0]
    low = jnp.bfloat16
    capacity = tensor_size * max(1, 3 * token_count // (5 * group_size))
    capacity = -(-capacity // 16) * 16
    results = run_layer(
        group_size,
        tensor_size,
        capacity,
        block_input,
        query_weight,
        key_weight,
        value_weight,
        output_weight,
        attn_gain[None, :],
        ffn_gain[None, :],
        router_weight.T,
        bias_table,
        expert_ids.T,
        out_cotangent,
        expert_in[0],
        expert_out[0],
    )
    block, inputs, query, key, value, output, attn, ffn, router, bias, in_grad, out_grad = finish(
        group_size, head_local, NB, *results
    )
    return (
        block.T,
        inputs.T,
        attn[0],
        query,
        key,
        value,
        output,
        bias,
        ffn[0],
        router.T,
        in_grad[None],
        out_grad[None],
    )


def choose(mesh):
    def run(*arrays):
        tokens, width = arrays[0].shape
        block_rows = arrays[2].shape[0]
        hidden = arrays[9].shape[2]
        group_size = mesh.shape["dp"]
        fits = (
            block_rows % 16 == 0
            and block_rows <= LANES
            and arrays[9].shape[0] == 1
            and mesh.shape["tensor"] == 4
            and group_size == 8
            and arrays[6].shape[0] <= 6
            and tokens == SEQ_LEN
            and hidden == width
            and width % 256 == 0
            and width == 3 * 256
        )
        return (on_device if fits else on_device_general)(*arrays)

    return run


def solution(mesh):
    placed = (
        P("dp", None),
        P("dp"),
        P("dp", "tensor"),
        P("dp", "tensor"),
        P("dp", "tensor"),
        P("dp", "tensor"),
        P("tensor", None),
        P("dp"),
        P("dp", None),
        P("dp", None, "tensor"),
        P("dp", "tensor", None),
        P("dp", None),
        P("dp", None),
    )
    return jax.shard_map(
        choose(mesh),
        mesh=mesh,
        in_specs=placed,
        out_specs=(
            P("dp", "tensor"),
            P("dp", "tensor"),
            P("dp"),
            P("dp", "tensor"),
            P("dp", "tensor"),
            P("dp", "tensor"),
            P("dp", "tensor"),
            P("tensor", None),
            P("dp"),
            P("dp", None),
            P("dp", None, "tensor"),
            P("dp", "tensor", None),
        ),
        check_vma=False,
    )
```
